32 devices in a mesh: expert: 16 (over z, y, x), tensor: 2 (over core).
Axes of the slice: x: 2, y: 2, z: 4, core: 2. Of those that a mesh axis runs over, the one named last changes fastest.
Arguments:
- tokens: bfloat16 [8192, 2048], P('expert'), may hold values from -6 to 6
- lengths: int32 [16], P('expert'), may hold values from 256 to 512, as said below
- routes: int32 [8192, 8], P('expert'), may hold values from 0 to 15, all different within a row; in each aligned block of 512 rows (0 to 511, 512 to 1023, ...) at most 288 rows name the same one
- attn_gain: float32 [2048], P('expert'), may hold values from 0.5 to 1.5
- w_query: float32 [2048, 2048], P('expert', 'tensor'), may hold values from -0.125 to 0.125
- w_key: float32 [2048, 2048], P('expert', 'tensor'), may hold values from -0.125 to 0.125
- w_value: float32 [2048, 2048], P('expert', 'tensor'), may hold values from -0.125 to 0.125
- query_gain: float32 [128], P('expert'), may hold values from 0.5 to 1.5
- key_gain: float32 [128], P('expert'), may hold values from 0.5 to 1.5
- w_out: float32 [2048, 2048], P('expert', 'tensor'), may hold values from -0.5 to 0.5
- ffn_gain: float32 [2048], P('expert'), may hold values from 0.5 to 1.5
- w_router: float32 [2048, 16], P('expert'), may hold values from -0.0625 to 0.0625
- w_gate: float32 [16, 2048, 1024], P('expert', None, 'tensor'), may hold values from -0.125 to 0.125
- w_up: float32 [16, 2048, 1024], P('expert', None, 'tensor'), may hold values from -0.125 to 0.125
- w_down: float32 [16, 1024, 2048], P('expert', 'tensor'), may hold values from -1 to 1
- cotangent: bfloat16 [8192, 2048], P('expert'), may hold values from -6 to 6
Outputs:
- output: bfloat16 [8192, 2048], P('expert')
- input_grad: bfloat16 [8192, 2048], P('expert')
- grad_attn_gain: float32 [2048], P('expert')
- grad_query: float32 [2048, 2048], P('expert', 'tensor')
- grad_key: float32 [2048, 2048], P('expert', 'tensor')
- grad_value: float32 [2048, 2048], P('expert', 'tensor')
- grad_query_gain: float32 [128], P('expert')
- grad_key_gain: float32 [128], P('expert')
- grad_out: float32 [2048, 2048], P('expert', 'tensor')
- grad_ffn_gain: float32 [2048], P('expert')
- grad_router: float32 [2048, 16], P('expert')
- grad_gate: float32 [16, 2048, 1024], P('expert', None, 'tensor')
- grad_up: float32 [16, 2048, 1024], P('expert', None, 'tensor')
- grad_down: float32 [16, 1024, 2048], P('expert', 'tensor')
The draws below stay inside these ranges and needn't reach their ends.
Inputs may be any that keep to these rules, and one draw needn't show every extreme that they name: `lengths`: each index of expert holds one sequence; at least one sequence fills all 512 slots. `routes`: within the rows of one sequence no expert is named by more than 288 rows, a bound that some block reaches.
All inputs are finite; a program needn't handle non-finite values.
Results may differ from the reference program's by a relative error of at most 0.02.
Values may be sent and summed in bfloat16 or wider, within the bound.
A program may use at most 384 MiB of HBM per device.

```python
import math
import jax
import jax.numpy as jnp
import numpy as np
from jax import lax

D = 2048
HEADS = 16
HD = 128
FF = 1024
TOP = 8
SEQ = 512
SEQS = 16
TOKENS = 8192
EXPERTS = 16
CAP = 288
N_TENSOR = 2


def draw_lengths(key, part):
    pick_key, full_key = jax.random.split(key)
    drawn_len = jax.random.randint(pick_key, (SEQS,), SEQ // 2, SEQ + 1)
    longest = jax.random.randint(full_key, (), 0, SEQS)
    return jnp.where(jnp.arange(SEQS) == longest, SEQ, drawn_len).astype(jnp.int32)


def levels(own_key, extent, cuts, low, largest):
    gain, own = 1.0, jax.random.fold_in(own_key, 6)
    for axis_at, blocks in cuts:
        heights = jnp.exp(jax.random.uniform(jax.random.fold_in(own, axis_at), (blocks,), jnp.float32, low / len(cuts), largest / len(cuts)))
        gain = gain * jnp.repeat(heights, extent[axis_at] // blocks).reshape([-1 if axis == axis_at else 1 for axis in range(len(extent))])
    return gain


def routed_block(own_key, own, number, rows, amount, top, bound, lean):
    sequence = jax.random.permutation(own_key, amount)
    crowded, usual = load_shares(amount, rows * top, bound, lean, True), load_shares(amount, rows * top, bound, lean, False)
    places = jnp.arange(amount)

    def named(sizes, turn):
        used = int((sizes > 0).sum())
        fixed = max(1, used // 4)
        passed = fixed + (places - fixed + turn * (used - fixed)) % max(1, amount - fixed)
        return jnp.zeros((amount,), jnp.int32).at[sequence[jnp.where(places < fixed, places, passed)]].set(jnp.asarray(sizes, jnp.int32))

    sizes = jnp.where(number % 4 == 0, named(crowded, number // 4), named(usual, number - number // 4 - 1))
    mixed = jax.random.permutation(jax.random.fold_in(own, 3), amount)
    source_of, sink = mixed[0:amount // 2 * 2:2], mixed[1:amount // 2 * 2:2]
    margin = jnp.minimum(sizes[source_of] - 1, bound - sizes[sink]) // 2
    margin = jnp.where((source_of == sequence[0]) | (sink == sequence[0]) | (sizes[sink] == 0), 0, jnp.maximum(margin, 0))
    passed = jax.random.randint(jax.random.fold_in(own, 4), (amount // 2,), 0, 1 << 20) % (margin + 1)
    sizes = sizes.at[source_of].add(-passed).at[sink].add(passed)
    items = jnp.searchsorted(jnp.cumsum(sizes), jnp.arange(rows * top), side="right").astype(jnp.int32)
    listing = items.reshape(top, rows).T
    listing = listing[jax.random.permutation(jax.random.fold_in(own, 1), rows)]
    turn = jax.random.randint(jax.random.fold_in(own, 2), (rows, 1), 0, top)
    return jnp.take_along_axis(listing, (jnp.arange(top)[None, :] + turn) % top, axis=1)


def load_shares(number_of, total, reach, slope, full):
    loads = [(1 << 20) // math.isqrt(rank ** slope) + 1 for rank in range(1, number_of + 1)]
    largest = reach if full else min(reach, max(-(-total // number_of), total * loads[0] // sum(loads)))
    least = 1 if total - largest >= number_of - 1 else 0
    given, spare = [largest] + [least] * (number_of - 1), total - largest - least * (number_of - 1)
    while spare > 0:
        movable = [i for i in range(1, number_of) if given[i] < largest] or [i for i in range(1, number_of) if given[i] < reach]
        whole, budget = sum([loads[i] for i in movable]), spare
        for i in movable:
            more = min(reach - given[i], max(1, budget * loads[i] // whole), spare)
            given[i] = given[i] + more
            spare = spare - more
    return np.array(given)


def bell_draw(rng, extent, width, reach, cuts=(), held_as=jnp.bfloat16):
    values = width * jax.random.normal(rng, extent, jnp.float32)
    if cuts:
        values = values * levels(rng, extent, cuts, -0.22, 0.18)
    return jnp.clip(values, -reach, reach).astype(held_as)


def setup_inputs(seed: int = 0) -> dict:
    splits = jax.random.split(jax.random.key(seed), 17)
    tokens = bell_draw(splits[0], (TOKENS, D), 1.0, 6.0, ((0, 16),))
    lengths = draw_lengths(jax.random.fold_in(splits[16], 71), 0)
    routes_keys = jax.random.split(jax.random.fold_in(splits[2], 1), TOKENS // SEQ)
    routes_turns = jax.random.permutation(jax.random.fold_in(splits[2], 3), TOKENS // SEQ)
    routes = jax.vmap(lambda own, number: routed_block(jax.random.fold_in(splits[2], 2), own, number, SEQ, EXPERTS, TOP, CAP, 1))(routes_keys, routes_turns).reshape((TOKENS, TOP))
    attn_gain = jnp.clip(1.0 + 0.1 * jax.random.normal(splits[3], (D,), jnp.float32), 0.5, 1.5)
    w_query = bell_draw(splits[4], (D, HEADS * HD), D ** -0.5, 0.125, ((0, 16), (1, 2)), jnp.float32)
    w_key = bell_draw(splits[5], (D, HEADS * HD), D ** -0.5, 0.125, ((0, 16), (1, 2)), jnp.float32)
    w_value = bell_draw(splits[6], (D, HEADS * HD), D ** -0.5, 0.125, ((0, 16), (1, 2)), jnp.float32)
    query_gain = jnp.clip(1.0 + 0.1 * jax.random.normal(splits[7], (HD,), jnp.float32), 0.5, 1.5)
    key_gain = jnp.clip(1.0 + 0.1 * jax.random.normal(splits[8], (HD,), jnp.float32), 0.5, 1.5)
    w_out = bell_draw(splits[9], (D, HEADS * HD), (HEADS * HD // 16) ** -0.5, 0.5, ((0, 16), (1, 2)), jnp.float32)
    ffn_gain = jnp.clip(1.0 + 0.1 * jax.random.normal(splits[10], (D,), jnp.float32), 0.5, 1.5)
    w_router = bell_draw(splits[11], (D, EXPERTS), (4 * D) ** -0.5, 0.0625, ((0, 16),), jnp.float32)
    w_gate = bell_draw(splits[12], (EXPERTS, D, FF), D ** -0.5, 0.125, ((0, 16), (2, 2)), jnp.float32)
    w_up = bell_draw(splits[13], (EXPERTS, D, FF), D ** -0.5, 0.125, ((0, 16), (2, 2)), jnp.float32)
    w_down = bell_draw(splits[14], (EXPERTS, FF, D), (FF // 32) ** -0.5, 1.0, ((0, 16), (1, 2)), jnp.float32)
    cotangent = bell_draw(splits[15], (TOKENS, D), 1.0, 6.0, ((0, 16),))
    return dict(tokens=tokens, lengths=lengths, routes=routes, attn_gain=attn_gain, w_query=w_query, w_key=w_key, w_value=w_value, query_gain=query_gain, key_gain=key_gain, w_out=w_out, ffn_gain=ffn_gain, w_router=w_router, w_gate=w_gate, w_up=w_up, w_down=w_down, cotangent=cotangent)


EPSILON = 1e-06
ROPE_BASE = 10000.0
NEG_BIG = -1e+30
HIGHEST = lax.Precision.HIGHEST

@jax.custom_vjp
def low(v):
    return lax.optimization_barrier(v.astype(jnp.bfloat16)).astype(jnp.float32)

@jax.custom_vjp
def low_back(v):
    return v

def low_keep(v):
    return (low(v), None)

def low_pass(kept, grad):
    return (grad,)

def back_keep(v):
    return (v, None)

def back_low(kept, grad):
    return (low(grad),)
low.defvjp(low_keep, low_pass)
low_back.defvjp(back_keep, back_low)

def matmul(left_mat, right_mat):
    return jnp.dot(left_mat, right_mat, precision=HIGHEST, preferred_element_type=jnp.float32)

def rms_scale(values, gain_vec):
    return values * lax.rsqrt(lax.optimization_barrier(jnp.mean(values * values, axis=-1, keepdims=True)) + EPSILON) * gain_vec

def rope_tables():
    half_dim = HD // 2
    inverse = ROPE_BASE ** (-(jnp.arange(half_dim).astype(jnp.float32) * 2.0 / HD))
    angles = jnp.arange(SEQ).astype(jnp.float32)[:, None] * inverse[None, :]
    return (jnp.cos(angles), jnp.sin(angles))

def rotate(values, cosine, sine_tab):
    half_dim = HD // 2
    lower_half = values[..., :half_dim]
    upper_half = values[..., half_dim:]
    cos_b = cosine[:, None, :]
    sin_b = sine_tab[:, None, :]
    return jnp.concatenate([lower_half * cos_b - upper_half * sin_b, upper_half * cos_b + lower_half * sin_b], axis=-1)

def slot_tables(block_routes):
    expert_ids = jnp.arange(EXPERTS).astype(jnp.int32)
    match_hot = block_routes[:, :, None] == expert_ids[None, None, :]
    hit_count = lax.optimization_barrier(jnp.sum(match_hot.astype(jnp.int32), axis=1))
    before = jnp.cumsum(hit_count, axis=0) - hit_count
    slot_index = lax.optimization_barrier(jnp.sum(jnp.where(match_hot, before[:, None, :], 0), axis=2)).astype(jnp.int32)
    flat_slot = (block_routes * CAP + slot_index).astype(jnp.int32)
    route_ids = jnp.arange(SEQ * TOP).astype(jnp.int32)
    slot_owner = jnp.full((EXPERTS * CAP,), SEQ * TOP, jnp.int32).at[flat_slot.reshape(-1)].set(route_ids)
    return (flat_slot, slot_owner)

def layer(tokens, attn_gain, w_query, w_key, w_value, query_gain, key_gain, w_out, ffn_gain, w_router, w_gate, w_up, w_down, lengths, routes):
    cosine, sine_tab = rope_tables()
    scale = 1.0 / math.sqrt(HD)
    attn_in = low(rms_scale(tokens, low(attn_gain)))
    wq_low = low(w_query)
    wk_low = low(w_key)
    wv_low = low(w_value)
    qg_low = low(query_gain)
    kg_low = low(key_gain)
    per_step = max([count for count in range(1, SEQS + 1) if SEQS % count == 0 and count * SEQ <= 4096] + [1])
    blocks = SEQS // per_step

    def attend(pieces):
        block_in, block_len = pieces
        flat_in = block_in.reshape(per_step * SEQ, D)
        query_lin = low_back(matmul(flat_in, wq_low)).reshape(per_step, SEQ, HEADS, HD)
        key_lin = low_back(matmul(flat_in, wk_low)).reshape(per_step, SEQ, HEADS, HD)
        values_v = low(low_back(matmul(flat_in, wv_low))).reshape(per_step, SEQ, HEADS, HD)
        queries = low(rotate(rms_scale(query_lin, qg_low), cosine, sine_tab))
        keys_rot = low(rotate(rms_scale(key_lin, kg_low), cosine, sine_tab))
        scores = low_back(jnp.einsum('bqhd,bkhd->bhqk', queries, keys_rot, precision=HIGHEST) * scale)
        allowed = jnp.arange(SEQ)[None, None, None, :] < block_len[:, None, None, None]
        attn_weights = low(jax.nn.softmax(jnp.where(allowed, scores, NEG_BIG), axis=-1))
        mixed = jnp.einsum('bhqk,bkhd->bqhd', attn_weights, values_v, precision=HIGHEST)
        return low(low_back(mixed)).reshape(per_step, SEQ, HEADS * HD)
    mixed_all = lax.map(jax.checkpoint(attend), (attn_in.reshape(blocks, per_step, SEQ, D), lengths.reshape(blocks, per_step)))
    mixed_all = mixed_all.reshape(TOKENS, HEADS * HD)
    attn_total = low_back(matmul(mixed_all, low(w_out).T))
    resid_one = tokens + attn_total
    ffn_in = low(rms_scale(resid_one, low(ffn_gain)))
    logits = low_back(matmul(ffn_in, low(w_router)))
    expert_ids = jnp.arange(EXPERTS).astype(jnp.int32)
    chosen = lax.optimization_barrier(jnp.sum(jnp.where(routes[:, :, None] == expert_ids[None, None, :], logits[:, None, :], 0.0), axis=2))
    gates = jax.nn.softmax(chosen, axis=1)
    flat_slot, slot_owner = jax.vmap(slot_tables)(routes.reshape(SEQS, SEQ, TOP))
    seq_base = (jnp.arange(SEQS).astype(jnp.int32) * SEQ)[:, None]
    owner_tok = jnp.where(slot_owner < SEQ * TOP, seq_base + slot_owner // TOP, TOKENS).astype(jnp.int32)
    owner_tok = owner_tok.reshape(SEQS, EXPERTS, CAP).transpose(1, 0, 2).reshape(EXPERTS, SEQS * CAP)
    padded_in = jnp.concatenate([ffn_in, jnp.zeros((1, D), jnp.float32)], axis=0)
    hidden_part = FF // N_TENSOR

    def expert_fn(pieces):
        row_ids, gate_w, up_w, down_w = pieces
        rows_in = padded_in[row_ids]
        total = jnp.zeros((SEQS * CAP, D), jnp.float32)
        for part_index in range(N_TENSOR):
            start = part_index * hidden_part
            rows_half = low_back(rows_in)
            gate_lin = low_back(matmul(rows_half, low(gate_w[:, start:start + hidden_part])))
            up_lin = low_back(matmul(rows_half, low(up_w[:, start:start + hidden_part])))
            hidden = low(jax.nn.silu(gate_lin) * up_lin)
            total = total + low(matmul(hidden, low(down_w[start:start + hidden_part, :])))
        return low_back(low(total))
    expert_out = lax.map(jax.checkpoint(expert_fn), (owner_tok, w_gate, w_up, w_down))
    expert_flat = expert_out.reshape(EXPERTS * SEQS * CAP, D)
    seq_of = jnp.repeat(jnp.arange(SEQS).astype(jnp.int32), SEQ)[:, None]
    slot_only = flat_slot.reshape(TOKENS, TOP) - routes * CAP
    position = routes * (SEQS * CAP) + seq_of * CAP + slot_only
    moe_out = jnp.zeros((TOKENS, D), jnp.float32)
    for route_index in range(TOP):
        moe_out = moe_out + gates[:, route_index:route_index + 1] * expert_flat[position[:, route_index]]
    return resid_one + moe_out

def reference(tokens, lengths, routes, attn_gain, w_query, w_key, w_value, query_gain, key_gain, w_out, ffn_gain, w_router, w_gate, w_up, w_down, cotangent):
    params = (tokens.astype(jnp.float32), attn_gain, w_query, w_key, w_value, query_gain, key_gain, w_out, ffn_gain, w_router, w_gate, w_up, w_down)

    def forward(*inputs):
        return layer(*inputs, lengths, routes)
    result, pullback = jax.vjp(forward, *params)
    live = (jnp.arange(SEQ)[None, :] < lengths[:, None]).reshape(TOKENS, 1)
    grads = pullback(jnp.where(live, cotangent.astype(jnp.float32), 0.0))
    return (result.astype(jnp.bfloat16), grads[0].astype(jnp.bfloat16), grads[1], grads[2], grads[3], grads[4], grads[5], grads[6], grads[7], grads[8], grads[9], grads[10], grads[11], grads[12])
```

```python
import math

import jax
import jax.numpy as jnp
from jax import lax
from jax.experimental import pallas as pl
from jax.experimental.pallas import tpu as pltpu
from jax.sharding import PartitionSpec as P

D = 2048
HD = 128
TOP = 8
SEQ = 512


EPSILON = 1e-06
ROPE_BASE = 10000.0
NEG_BIG = -1e30


def rope_tables(seq_len, head_dim):
    half_dim = head_dim // 2
    inverse = ROPE_BASE ** (-(jnp.arange(half_dim).astype(jnp.float32) * 2.0 / head_dim))
    angles = jnp.arange(seq_len).astype(jnp.float32)[:, None] * inverse[None, :]
    return (jnp.cos(angles), jnp.sin(angles))


def rotate(values, cosine, sine_tab):
    half_dim = values.shape[-1] // 2
    lower_half = values[..., :half_dim]
    upper_half = values[..., half_dim:]
    cos_b = cosine[:, None, :]
    sin_b = sine_tab[:, None, :]
    return jnp.concatenate(
        [lower_half * cos_b - upper_half * sin_b, upper_half * cos_b + lower_half * sin_b], axis=-1
    )


def rotate_back(grads_in, cosine, sine_tab):
    half_dim = grads_in.shape[-1] // 2
    lower_half = grads_in[..., :half_dim]
    upper_half = grads_in[..., half_dim:]
    cos_b = cosine[:, None, :]
    sin_b = sine_tab[:, None, :]
    return jnp.concatenate(
        [lower_half * cos_b + upper_half * sin_b, upper_half * cos_b - lower_half * sin_b], axis=-1
    )


def norm_stats(values):
    inverse = lax.rsqrt(jnp.mean(values * values, axis=-1, keepdims=True) + EPSILON)
    return (values * inverse, inverse)


def norm_back(grad_normed, normed, inverse):
    return inverse * (grad_normed - normed * jnp.mean(grad_normed * normed, axis=-1, keepdims=True))


def contract_rows(left_mat, right_mat):
    return lax.dot_general(
        left_mat, right_mat, (((0,), (0,)), ((), ())), preferred_element_type=jnp.float32
    )


def contract_cols(left_mat, right_mat):
    return lax.dot_general(
        left_mat, right_mat, (((1,), (1,)), ((), ())), preferred_element_type=jnp.float32
    )


PLANES = 4
CORES = 2


class Grid:
    def __init__(self, count):
        self.count = count
        self.plane = count // PLANES
        self.side = math.isqrt(self.plane)
        self.near = range(1, self.side)

    def first(self, step):
        return (step, step * self.side)

    def second(self, step):
        return (step * self.side, step)

    def planes_of(self, turn):
        return ((0, 3)[turn] * self.plane, (1, 2)[turn] * self.plane)

    def send(self, value, masks):
        pairs = [
            (device * CORES + core, (device ^ masks[core]) * CORES + core)
            for device in range(self.count)
            for core in range(CORES)
        ]
        return lax.ppermute(value, ("expert", "tensor"), pairs)


def swap(value):
    return lax.ppermute(value, "tensor", [(0, 1), (1, 0)])


def spread(grid, base):
    row = [base] + [grid.send(base, grid.first(step)) for step in grid.near]
    blocks = list(row)
    for step in grid.near:
        blocks += [grid.send(block, grid.second(step)) for block in row]
    return blocks


def gather_tokens(grid, block):
    return [spread(grid, grid.send(block, grid.planes_of(turn))) for turn in range(2)]


def collect(grid, blocks):
    side = grid.side
    sums = [block.astype(jnp.float32) for block in blocks[:side]]
    for far in grid.near:
        for step in range(side):
            sums[step] = sums[step] + grid.send(
                blocks[far * side + step], grid.second(far)
            ).astype(jnp.float32)
    total = sums[0]
    for step in grid.near:
        total = total + grid.send(sums[step].astype(jnp.bfloat16), grid.first(step)).astype(
            jnp.float32
        )
    return total


def scatter_tokens(grid, turns):
    total = None
    for turn in (1, 0):
        part = grid.send(collect(grid, turns[turn]).astype(jnp.bfloat16), grid.planes_of(turn))
        part = part.astype(jnp.float32)
        total = part if total is None else total + part
    total = total.astype(jnp.bfloat16)
    return total.astype(jnp.float32) + swap(total).astype(jnp.float32)


def scatter_rows(grid, value, axes, wire):
    me = lax.axis_index("expert")
    units = (grid.plane, grid.side, 1)
    sizes = (PLANES, grid.side, grid.side)
    gone = []
    for axis in axes:
        unit, size = units[axis], sizes[axis]
        place = (me // unit) % size
        at = axis - sum(1 for other in gone if other < axis)
        total = lax.dynamic_index_in_dim(value, place, at, keepdims=False).astype(jnp.float32)
        for step in range(1, size):
            part = lax.dynamic_index_in_dim(value, place ^ step, at, keepdims=False).astype(wire)
            total = total + grid.send(part, (unit * step,) * CORES).astype(jnp.float32)
        value = total
        gone.append(axis)
    return value


def assemble(grid, blocks, rows, extra):
    count, width = grid.count, blocks[0].shape[1]
    me = lax.axis_index("expert")
    core = lax.axis_index("tensor")
    place = jnp.arange(count)
    top, mid, low = place // grid.plane, (place // grid.side) % grid.side, place % grid.side
    turned = top * grid.plane + low * grid.side + mid
    owner = me ^ jnp.where(core == 0, place, turned)

    def body(owner_ref, *refs):
        ins, outs, small, sem = refs[:count], refs[count : count + 4], refs[count + 4], refs[-1]
        copies = []
        for index in range(count):
            at = owner_ref[index]
            for which in range(4):
                copies.append(
                    pltpu.make_async_copy(
                        ins[index].at[pl.ds(which * rows, rows)],
                        outs[which].at[pl.ds(pl.multiple_of(at * rows, rows), rows)],
                        sem.at[index, which],
                    )
                )
            copies.append(
                pltpu.make_async_copy(
                    ins[index].at[pl.ds(4 * rows, extra)], small.at[at], sem.at[index, 4]
                )
            )
        for copy in copies:
            copy.start()
        for copy in copies:
            copy.wait()

    full = jax.ShapeDtypeStruct((count * rows, width), jnp.bfloat16)
    small = jax.ShapeDtypeStruct((count, extra, width), jnp.bfloat16)
    return pl.pallas_call(
        body,
        grid_spec=pltpu.PrefetchScalarGridSpec(
            num_scalar_prefetch=1,
            grid=(),
            in_specs=[pl.BlockSpec(memory_space=pl.ANY)] * count,
            out_specs=[pl.BlockSpec(memory_space=pltpu.VMEM)] * 5,
            scratch_shapes=[pltpu.SemaphoreType.DMA((count, 5))],
        ),
        out_shape=[full] * 4 + [small],
        name="assemble",
    )(owner, *blocks)


def split_three(value):
    high = value.astype(jnp.bfloat16)
    rest = value - high.astype(jnp.float32)
    middle = rest.astype(jnp.bfloat16)
    low = (rest - middle.astype(jnp.float32)).astype(jnp.bfloat16)
    return jnp.concatenate([high, middle, low], axis=-1)


def join_three(parts, length):
    parts = parts.astype(jnp.float32)
    return (
        parts[..., :length] + parts[..., length : 2 * length] + parts[..., 2 * length : 3 * length]
    )


def expert_turn(blocks, grads, weights, capacity):
    wg, wu, wd = weights
    me = lax.axis_index("expert")
    experts = blocks[0].shape[0] - SEQ
    gate = jnp.concatenate(
        [
            join_three(lax.dynamic_slice(block, (SEQ + me, 0), (1, 3 * SEQ)), SEQ)
            for block in blocks
        ],
        axis=0,
    )
    used = gate > 0.0
    ordered = (jnp.arange(SEQ)[:, None] < jnp.arange(SEQ)[None, :]).astype(jnp.bfloat16)
    slot = jnp.dot(used.astype(jnp.bfloat16), ordered, preferred_element_type=jnp.float32)
    slot = slot.astype(jnp.int32)
    hot = (jnp.arange(capacity)[None, :, None] == slot[:, None, :]) & used[:, None, :]
    pick = hot.astype(jnp.bfloat16)
    slot_gate = jnp.sum(jnp.where(hot, gate[:, None, :], 0.0), axis=2).reshape(-1, 1)
    rows = jnp.concatenate(
        [
            jnp.dot(pick[i], block[:SEQ], preferred_element_type=jnp.float32).astype(jnp.bfloat16)
            for i, block in enumerate(blocks)
        ],
        axis=0,
    )
    grad_rows = jnp.concatenate(
        [
            jnp.dot(pick[i], block, preferred_element_type=jnp.float32).astype(jnp.bfloat16)
            for i, block in enumerate(grads)
        ],
        axis=0,
    )
    gate_lin = jnp.dot(rows, wg, preferred_element_type=jnp.float32)
    up_lin = jnp.dot(rows, wu, preferred_element_type=jnp.float32)
    grad_full = contract_cols(grad_rows, wd)
    sigmoid_gate = jax.nn.sigmoid(gate_lin)
    activated = gate_lin * sigmoid_gate
    hidden = activated * up_lin
    hidden_low = (hidden * slot_gate).astype(jnp.bfloat16)
    slot_grad = jnp.sum(hidden * grad_full, axis=1).reshape(len(blocks), capacity, 1)
    grad_hidden = grad_full * slot_gate
    silu_slope = sigmoid_gate * (1.0 + gate_lin * (1.0 - sigmoid_gate))
    grad_gate = (grad_hidden * up_lin * silu_slope).astype(jnp.bfloat16)
    grad_up = (grad_hidden * activated).astype(jnp.bfloat16)
    value = jnp.dot(hidden_low, wd, preferred_element_type=jnp.float32).astype(jnp.bfloat16)
    grad_in = (contract_cols(grad_gate, wg) + contract_cols(grad_up, wu)).astype(jnp.bfloat16)
    token_grad = split_three(jnp.sum(jnp.where(hot, slot_grad, 0.0), axis=1))
    outs, backs = [], []
    for i in range(len(blocks)):
        span = slice(i * capacity, (i + 1) * capacity)
        outs.append(contract_rows(pick[i], value[span]).astype(jnp.bfloat16))
        back = contract_rows(pick[i], grad_in[span]).astype(jnp.bfloat16)
        extra = jnp.where(
            (jnp.arange(experts) == me)[:, None],
            jnp.pad(token_grad[i : i + 1], ((0, 0), (0, D - 3 * SEQ))),
            0,
        )
        backs.append(jnp.concatenate([back, extra], axis=0))
    return outs, backs, (rows, grad_rows, hidden_low, grad_gate, grad_up)


def local(
    tokens,
    lengths,
    routes,
    attn_gain,
    w_query,
    w_key,
    w_value,
    query_gain,
    key_gain,
    w_out,
    ffn_gain,
    w_router,
    w_gate,
    w_up,
    w_down,
    cotangent,
):
    grid = Grid(lax.axis_size("expert"))
    count = grid.count
    experts = w_router.shape[1]
    capacity = SEQ * TOP * 9 // (8 * experts)
    scale = 1.0 / math.sqrt(HD)
    low = jnp.bfloat16
    own_rows, width = w_query.shape
    heads_here = width // HD
    core = lax.axis_index("tensor")

    small = jnp.concatenate(
        [
            w_router.astype(low).T,
            jnp.pad(
                jnp.stack(
                    [
                        attn_gain.astype(low),
                        ffn_gain.astype(low),
                        jnp.pad(query_gain.astype(low), (0, own_rows - HD // count)),
                        jnp.pad(key_gain.astype(low), (0, own_rows - HD // count)),
                    ]
                ),
                ((0, experts - 4), (0, 0)),
            ),
        ],
        axis=1,
    )
    small = jnp.pad(small, ((0, 0), (0, width - 2 * own_rows)))
    mine = jnp.concatenate(
        [w_query.astype(low), w_key.astype(low), w_value.astype(low), w_out.astype(low), small],
        axis=0,
    )
    arrived = []
    for top in range(PLANES):
        base = mine if top == 0 else grid.send(mine, (top * grid.plane,) * CORES)
        arrived += spread(grid, base)
    wq_full, wk_full, wv_full, wo_full, smalls = assemble(grid, arrived, own_rows, experts)
    router_t = smalls[:, :, :own_rows].transpose(1, 0, 2).reshape(experts, D)
    gain_one = smalls[:, 0, own_rows : 2 * own_rows].reshape(D).astype(jnp.float32)
    gain_two = smalls[:, 1, own_rows : 2 * own_rows].reshape(D).astype(jnp.float32)
    head_cols = slice(own_rows, own_rows + HD // count)
    gain_query = smalls[:, 2, head_cols].reshape(HD).astype(jnp.float32)
    gain_key = smalls[:, 3, head_cols].reshape(HD).astype(jnp.float32)

    wg_own, wu_own, wd_own = (w_gate[0].astype(low), w_up[0].astype(low), w_down[0].astype(low))
    wg = jnp.concatenate([wg_own, swap(wg_own)], axis=1)
    wu = jnp.concatenate([wu_own, swap(wu_own)], axis=1)
    wd = jnp.concatenate([wd_own, swap(wd_own)], axis=0)

    allowed = jnp.arange(SEQ) < lengths[0]
    grad_two_low = jnp.where(allowed[:, None], cotangent, 0)
    grad_two_sent, wq_full, wk_full, wv_full, wo_full = lax.optimization_barrier(
        (grad_two_low, wq_full, wk_full, wv_full, wo_full)
    )
    grad_turns = gather_tokens(grid, grad_two_sent)
    grad_two = grad_two_low.astype(jnp.float32)

    cosine, sine_tab = rope_tables(SEQ, HD)
    resid_zero = tokens.astype(jnp.float32)
    normed_one, inverse_one = norm_stats(resid_zero)
    attn_in = (normed_one * gain_one).astype(low)
    query_lin = jnp.dot(attn_in, wq_full, preferred_element_type=jnp.float32).reshape(
        SEQ, heads_here, HD
    )
    key_lin = jnp.dot(attn_in, wk_full, preferred_element_type=jnp.float32).reshape(
        SEQ, heads_here, HD
    )
    values_b = (
        jnp.dot(attn_in, wv_full, preferred_element_type=jnp.float32)
        .astype(low)
        .reshape(SEQ, heads_here, HD)
    )
    query_hat, query_inv = norm_stats(query_lin)
    key_hat, key_inv = norm_stats(key_lin)
    queries = rotate(query_hat * gain_query, cosine, sine_tab).astype(low)
    keys_rot = rotate(key_hat * gain_key, cosine, sine_tab).astype(low)

    def masked_scores():
        scores = (
            jnp.einsum("qhd,khd->hqk", queries, keys_rot, preferred_element_type=jnp.float32)
            * scale
        )
        return jnp.where(allowed[None, None, :], scores, NEG_BIG)

    masked = masked_scores()
    top_score = jnp.max(masked, axis=-1, keepdims=True)
    expo_vals = jnp.exp(masked - top_score)
    totals = jnp.sum(expo_vals, axis=-1, keepdims=True)
    probs_low = (expo_vals / totals).astype(low)
    log_total = top_score + jnp.log(totals)
    mixed = (
        jnp.einsum("hqk,khd->qhd", probs_low, values_b, preferred_element_type=jnp.float32)
        .reshape(SEQ, heads_here * HD)
        .astype(low)
    )
    attn_part = contract_cols(mixed, wo_full)
    resid_one = resid_zero + (attn_part + swap(attn_part))
    normed_two, inverse_two = norm_stats(resid_one)
    ffn_in = (normed_two * gain_two).astype(low)
    logits = contract_cols(ffn_in, router_t)
    route_hot = routes[:, :, None] == jnp.arange(experts)[None, None, :]
    chosen = jnp.sum(jnp.where(route_hot, logits[:, None, :], 0.0), axis=2)
    gates = jax.nn.softmax(chosen, axis=1)
    gates_wide = jnp.sum(jnp.where(route_hot, gates[:, :, None], 0.0), axis=1)

    gate_rows = jnp.pad(split_three(gates_wide.T), ((0, 0), (0, D - 3 * SEQ)))
    token_turns = gather_tokens(grid, jnp.concatenate([ffn_in, gate_rows], axis=0))
    out_turns, back_turns, saved = [], [], []
    for turn in range(2):
        outs, backs, kept = expert_turn(
            token_turns[turn], grad_turns[turn], (wg, wu, wd), capacity
        )
        out_turns.append(outs)
        back_turns.append(backs)
        saved.append(kept)
    back_sum = scatter_tokens(grid, back_turns)
    out_sum = scatter_tokens(grid, out_turns)
    output = (resid_one + out_sum).astype(low)

    def over_turns(left, right):
        return sum(contract_rows(kept[left], kept[right]) for kept in saved)

    half = w_gate.shape[2]
    gate_w = over_turns(0, 3)
    up_w = over_turns(0, 4)
    down_w = over_turns(2, 1)
    grad_gate_w = (gate_w[:, :half] + swap(gate_w[:, half:]))[None]
    grad_up_w = (up_w[:, :half] + swap(up_w[:, half:]))[None]
    grad_down_w = (down_w[:half] + swap(down_w[half:]))[None]

    grad_gates_wide = join_three(back_sum[SEQ:], SEQ).T
    grad_gate_sel = jnp.sum(jnp.where(route_hot, grad_gates_wide[:, None, :], 0.0), axis=2)
    grad_chosen = gates * (grad_gate_sel - jnp.sum(gates * grad_gate_sel, axis=1, keepdims=True))
    grad_logits = jnp.sum(jnp.where(route_hot, grad_chosen[:, :, None], 0.0), axis=1).astype(low)
    grad_router_t = contract_rows(grad_logits, ffn_in)
    grad_ffn_in = back_sum[:SEQ] + jnp.dot(
        grad_logits, router_t, preferred_element_type=jnp.float32
    )
    grad_gain_two = jnp.sum(grad_ffn_in * normed_two, axis=0)
    grad_one = grad_two + norm_back(grad_ffn_in * gain_two, normed_two, inverse_two)
    grad_attn = grad_one.astype(low)

    def reduce_weight(left, right, axes):
        whole = contract_rows(left, right)
        return scatter_rows(
            grid, whole.reshape(PLANES, grid.side, grid.side, own_rows, width), axes, low
        )

    grad_wo = reduce_weight(grad_attn, mixed, (1, 2, 0))
    grad_mixed = (
        jnp.dot(grad_attn, wo_full, preferred_element_type=jnp.float32)
        .astype(low)
        .reshape(SEQ, heads_here, HD)
    )
    masked = masked_scores()
    attn_probs = jnp.exp(masked - log_total)
    probs_again = attn_probs.astype(low)
    grad_probs = jnp.einsum(
        "qhd,khd->hqk", grad_mixed, values_b, preferred_element_type=jnp.float32
    )
    grad_values = jnp.einsum(
        "hqk,qhd->khd", probs_again, grad_mixed, preferred_element_type=jnp.float32
    )
    grad_value_lin = grad_values.astype(low).reshape(SEQ, heads_here * HD)
    grad_wv = reduce_weight(attn_in, grad_value_lin, (2, 1, 0))
    grad_scores = (
        attn_probs * (grad_probs - jnp.sum(attn_probs * grad_probs, axis=-1, keepdims=True))
    ).astype(low)
    grad_queries = (
        jnp.einsum("hqk,khd->qhd", grad_scores, keys_rot, preferred_element_type=jnp.float32)
        * scale
    )
    grad_keys = (
        jnp.einsum("hqk,qhd->khd", grad_scores, queries, preferred_element_type=jnp.float32) * scale
    )
    grad_query_scaled = rotate_back(grad_queries, cosine, sine_tab)
    grad_key_scaled = rotate_back(grad_keys, cosine, sine_tab)
    grad_gain_query = jnp.sum(grad_query_scaled * query_hat, axis=(0, 1))
    grad_gain_key = jnp.sum(grad_key_scaled * key_hat, axis=(0, 1))
    grad_query_lin = (
        norm_back(grad_query_scaled * gain_query, query_hat, query_inv)
        .astype(low)
        .reshape(SEQ, heads_here * HD)
    )
    grad_key_lin = (
        norm_back(grad_key_scaled * gain_key, key_hat, key_inv)
        .astype(low)
        .reshape(SEQ, heads_here * HD)
    )
    grad_wq = reduce_weight(attn_in, grad_query_lin, (1, 2, 0))
    grad_wk = reduce_weight(attn_in, grad_key_lin, (2, 1, 0))
    grad_attn_part = (
        contract_cols(grad_query_lin, wq_full)
        + contract_cols(grad_key_lin, wk_full)
        + contract_cols(grad_value_lin, wv_full)
    ).astype(low)
    grad_attn_in = grad_attn_part.astype(jnp.float32) + swap(grad_attn_part).astype(jnp.float32)
    grad_gain_one = jnp.sum(grad_attn_in * normed_one, axis=0)
    grad_input = grad_one + norm_back(grad_attn_in * gain_one, normed_one, inverse_one)

    head_part = HD // count
    heads_row = jnp.stack([grad_gain_query, grad_gain_key]).reshape(2, count, head_part)
    heads_row = jnp.pad(heads_row, ((0, 0), (0, 0), (0, own_rows - head_part)))
    parts = jnp.concatenate(
        [
            jnp.concatenate([grad_router_t, grad_gain_one[None], grad_gain_two[None]]).reshape(
                experts + 2, count, own_rows
            ),
            heads_row,
        ],
        axis=0,
    ).transpose(1, 0, 2)
    sums = scatter_rows(
        grid,
        parts.reshape(PLANES, grid.side, grid.side, experts + 4, own_rows),
        (1, 2, 0),
        jnp.float32,
    )
    sums = sums + swap(sums)
    return (
        output,
        grad_input.astype(low),
        0.5 * sums[experts],
        grad_wq,
        grad_wk,
        grad_wv,
        sums[experts + 2, :head_part],
        sums[experts + 3, :head_part],
        grad_wo,
        0.5 * sums[experts + 1],
        0.5 * sums[:experts].T,
        grad_gate_w,
        grad_up_w,
        grad_down_w,
    )


def solution(mesh):
    return jax.shard_map(
        local,
        mesh=mesh,
        in_specs=(
            P("expert", None),
            P("expert"),
            P("expert", None),
            P("expert"),
            P("expert", "tensor"),
            P("expert", "tensor"),
            P("expert", "tensor"),
            P("expert"),
            P("expert"),
            P("expert", "tensor"),
            P("expert"),
            P("expert", None),
            P("expert", None, "tensor"),
            P("expert", None, "tensor"),
            P("expert", "tensor", None),
            P("expert", None),
        ),
        out_specs=(
            P("expert", None),
            P("expert", None),
            P("expert"),
            P("expert", "tensor"),
            P("expert", "tensor"),
            P("expert", "tensor"),
            P("expert"),
            P("expert"),
            P("expert", "tensor"),
            P("expert"),
            P("expert", None),
            P("expert", None, "tensor"),
            P("expert", None, "tensor"),
            P("expert", "tensor", None),
        ),
        check_vma=False,
    )
```

```python
import functools
import math

import jax
import jax.numpy as jnp
from jax import lax
from jax.experimental import pallas as pl
from jax.experimental.pallas import tpu as pltpu
from jax.sharding import PartitionSpec as P

D = 2048
HD = 128
TOP = 8
SEQ = 512


EPSILON = 1e-06
ROPE_BASE = 10000.0
NEG_BIG = -1e30


def rope_tables(seq_len, head_dim):
    half_dim = head_dim // 2
    inverse = ROPE_BASE ** (-(jnp.arange(half_dim).astype(jnp.float32) * 2.0 / head_dim))
    angles = jnp.arange(seq_len).astype(jnp.float32)[:, None] * inverse[None, :]
    return (jnp.cos(angles), jnp.sin(angles))


def rotate(values, cosine, sine_tab):
    half_dim = values.shape[-1] // 2
    lower_half = values[..., :half_dim]
    upper_half = values[..., half_dim:]
    cos_b = cosine[:, None, :]
    sin_b = sine_tab[:, None, :]
    return jnp.concatenate(
        [lower_half * cos_b - upper_half * sin_b, upper_half * cos_b + lower_half * sin_b], axis=-1
    )


def rotate_back(grads_in, cosine, sine_tab):
    half_dim = grads_in.shape[-1] // 2
    lower_half = grads_in[..., :half_dim]
    upper_half = grads_in[..., half_dim:]
    cos_b = cosine[:, None, :]
    sin_b = sine_tab[:, None, :]
    return jnp.concatenate(
        [lower_half * cos_b + upper_half * sin_b, upper_half * cos_b - lower_half * sin_b], axis=-1
    )


def norm_stats(values):
    inverse = lax.rsqrt(jnp.mean(values * values, axis=-1, keepdims=True) + EPSILON)
    return (values * inverse, inverse)


def norm_back(grad_normed, normed, inverse):
    return inverse * (grad_normed - normed * jnp.mean(grad_normed * normed, axis=-1, keepdims=True))


def contract_rows(left_mat, right_mat):
    return lax.dot_general(
        left_mat, right_mat, (((0,), (0,)), ((), ())), preferred_element_type=jnp.float32
    )


def contract_cols(left_mat, right_mat):
    return lax.dot_general(
        left_mat, right_mat, (((1,), (1,)), ((), ())), preferred_element_type=jnp.float32
    )


PLANES = 4
CORES = 2


class Grid:
    def __init__(self, count):
        self.count = count
        self.plane = count // PLANES
        self.side = math.isqrt(self.plane)
        self.near = range(1, self.side)

    def first(self, step):
        return (step, step * self.side)

    def second(self, step):
        return (step * self.side, step)

    def planes_of(self, turn):
        return ((0, 3)[turn] * self.plane, (1, 2)[turn] * self.plane)

    def send(self, value, masks):
        pairs = [
            (device * CORES + core, (device ^ masks[core]) * CORES + core)
            for device in range(self.count)
            for core in range(CORES)
        ]
        return lax.ppermute(value, ("expert", "tensor"), pairs)


def swap(value):
    return lax.ppermute(value, "tensor", [(0, 1), (1, 0)])


def both_cores(part):
    return part.astype(jnp.float32) + swap(part).astype(jnp.float32)


def spread(grid, base):
    row = [base] + [grid.send(base, grid.first(step)) for step in grid.near]
    blocks = list(row)
    for step in grid.near:
        blocks += [grid.send(block, grid.second(step)) for block in row]
    return blocks


def gather_tokens(grid, block):
    return [spread(grid, grid.send(block, grid.planes_of(turn))) for turn in range(2)]


def collect(grid, blocks):
    side = grid.side
    sums = [block.astype(jnp.float32) for block in blocks[:side]]
    for far in grid.near:
        for step in range(side):
            sums[step] = sums[step] + grid.send(
                blocks[far * side + step], grid.second(far)
            ).astype(jnp.float32)
    total = sums[0]
    for step in grid.near:
        total = total + grid.send(sums[step].astype(jnp.bfloat16), grid.first(step)).astype(
            jnp.float32
        )
    return total


def scatter_tokens(grid, turns):
    total = None
    for turn in (1, 0):
        part = grid.send(collect(grid, turns[turn]).astype(jnp.bfloat16), grid.planes_of(turn))
        part = part.astype(jnp.float32)
        total = part if total is None else total + part
    return both_cores(total.astype(jnp.bfloat16))


def scatter_rows(grid, value, axes, wire):
    me = lax.axis_index("expert")
    units = (grid.plane, grid.side, 1)
    sizes = (PLANES, grid.side, grid.side)
    gone = []
    for axis in axes:
        unit, size = units[axis], sizes[axis]
        place = (me // unit) % size
        at = axis - sum(1 for other in gone if other < axis)
        total = lax.dynamic_index_in_dim(value, place, at, keepdims=False).astype(jnp.float32)
        for step in range(1, size):
            part = lax.dynamic_index_in_dim(value, place ^ step, at, keepdims=False).astype(wire)
            total = total + grid.send(part, (unit * step,) * CORES).astype(jnp.float32)
        value = total
        gone.append(axis)
    return value


def assemble(grid, blocks, rows, extra):
    count, width = grid.count, blocks[0].shape[1]
    me = lax.axis_index("expert")
    core = lax.axis_index("tensor")
    place = jnp.arange(count)
    top, mid, low = place // grid.plane, (place // grid.side) % grid.side, place % grid.side
    turned = top * grid.plane + low * grid.side + mid
    owner = me ^ jnp.where(core == 0, place, turned)

    def body(owner_ref, *refs):
        ins, outs, small, sem = refs[:count], refs[count : count + 4], refs[count + 4], refs[-1]
        copies = []
        for index in range(count):
            at = owner_ref[index]
            for which in range(4):
                copies.append(
                    pltpu.make_async_copy(
                        ins[index].at[pl.ds(which * rows, rows)],
                        outs[which].at[pl.ds(pl.multiple_of(at * rows, rows), rows)],
                        sem.at[index, which],
                    )
                )
            copies.append(
                pltpu.make_async_copy(
                    ins[index].at[pl.ds(4 * rows, extra)], small.at[at], sem.at[index, 4]
                )
            )
        for copy in copies:
            copy.start()
        for copy in copies:
            copy.wait()

    full = jax.ShapeDtypeStruct((count * rows, width), jnp.bfloat16)
    small = jax.ShapeDtypeStruct((count, extra, width), jnp.bfloat16)
    return pl.pallas_call(
        body,
        grid_spec=pltpu.PrefetchScalarGridSpec(
            num_scalar_prefetch=1,
            grid=(),
            in_specs=[pl.BlockSpec(memory_space=pl.ANY)] * count,
            out_specs=[pl.BlockSpec(memory_space=pltpu.VMEM)] * 5,
            scratch_shapes=[pltpu.SemaphoreType.DMA((count, 5))],
        ),
        out_shape=[full] * 4 + [small],
        name="assemble",
    )(owner, *blocks)


def split_three(value):
    high = value.astype(jnp.bfloat16)
    rest = value - high.astype(jnp.float32)
    middle = rest.astype(jnp.bfloat16)
    low = (rest - middle.astype(jnp.float32)).astype(jnp.bfloat16)
    return jnp.concatenate([high, middle, low], axis=-1)


def join_three(parts, length):
    parts = parts.astype(jnp.float32)
    return (
        parts[..., :length] + parts[..., length : 2 * length] + parts[..., 2 * length : 3 * length]
    )


def expert_turn(blocks, grads, weights, capacity):
    wg, wu, wd = weights
    me = lax.axis_index("expert")
    experts = blocks[0].shape[0] - SEQ
    gate = jnp.concatenate(
        [
            join_three(lax.dynamic_slice(block, (SEQ + me, 0), (1, 3 * SEQ)), SEQ)
            for block in blocks
        ],
        axis=0,
    )
    used = gate > 0.0
    ordered = (jnp.arange(SEQ)[:, None] < jnp.arange(SEQ)[None, :]).astype(jnp.bfloat16)
    slot = jnp.dot(used.astype(jnp.bfloat16), ordered, preferred_element_type=jnp.float32)
    slot = slot.astype(jnp.int32)
    hot = (jnp.arange(capacity)[None, :, None] == slot[:, None, :]) & used[:, None, :]
    pick = hot.astype(jnp.bfloat16)
    slot_gate = jnp.sum(jnp.where(hot, gate[:, None, :], 0.0), axis=2).reshape(-1, 1)
    rows = jnp.concatenate(
        [
            jnp.dot(pick[i], block[:SEQ], preferred_element_type=jnp.float32).astype(jnp.bfloat16)
            for i, block in enumerate(blocks)
        ],
        axis=0,
    )
    grad_rows = jnp.concatenate(
        [
            jnp.dot(pick[i], block, preferred_element_type=jnp.float32).astype(jnp.bfloat16)
            for i, block in enumerate(grads)
        ],
        axis=0,
    )
    gate_lin = jnp.dot(rows, wg, preferred_element_type=jnp.float32)
    up_lin = jnp.dot(rows, wu, preferred_element_type=jnp.float32)
    grad_full = contract_cols(grad_rows, wd)
    sigmoid_gate = jax.nn.sigmoid(gate_lin)
    activated = gate_lin * sigmoid_gate
    hidden = activated * up_lin
    hidden_low = (hidden * slot_gate).astype(jnp.bfloat16)
    slot_grad = jnp.sum(hidden * grad_full, axis=1).reshape(len(blocks), capacity, 1)
    grad_hidden = grad_full * slot_gate
    silu_slope = sigmoid_gate * (1.0 + gate_lin * (1.0 - sigmoid_gate))
    grad_gate = (grad_hidden * up_lin * silu_slope).astype(jnp.bfloat16)
    grad_up = (grad_hidden * activated).astype(jnp.bfloat16)
    value = jnp.dot(hidden_low, wd, preferred_element_type=jnp.float32).astype(jnp.bfloat16)
    grad_in = (contract_cols(grad_gate, wg) + contract_cols(grad_up, wu)).astype(jnp.bfloat16)
    token_grad = split_three(jnp.sum(jnp.where(hot, slot_grad, 0.0), axis=1))
    outs, backs = [], []
    for i in range(len(blocks)):
        span = slice(i * capacity, (i + 1) * capacity)
        outs.append(contract_rows(pick[i], value[span]).astype(jnp.bfloat16))
        back = contract_rows(pick[i], grad_in[span]).astype(jnp.bfloat16)
        extra = jnp.where(
            (jnp.arange(experts) == me)[:, None],
            jnp.pad(token_grad[i : i + 1], ((0, 0), (0, D - 3 * SEQ))),
            0,
        )
        backs.append(jnp.concatenate([back, extra], axis=0))
    return outs, backs, (rows, grad_rows, hidden_low, grad_gate, grad_up)


def moe_kernel(
    capacity,
    experts,
    own,
    wg,
    wu,
    wd,
    *refs,
):
    grads, refs = refs[:8], refs[8:]
    parts, refs = refs[:8], refs[8:]
    (
    blocks,
    far_sums,
    near_sums,
    plane_sums,
    rows_out,
    grows_out,
    hidden_out,
    gate_out,
    up_out,
    result,
    wg_v,
    wu_v,
    wd_v,
    block_v,
    grad_v,
    rows_v,
    grows_v,
    hidden_v,
    gate_v,
    up_v,
    pick_v,
    pick_t,
    ordered,
    stage,
    part_v,
    taken,
    weight_sem,
    load_sem,
    save_sem,
    send_sem,
    recv_sem,
    back_send,
    back_recv,
    ) = refs
    me = lax.axis_index("expert")
    core = lax.axis_index("tensor")
    top, mid, low = me // 4, (me // 2) % 2, me % 2
    flip_low = me + 1 - 2 * low
    flip_mid = me + 2 - 4 * mid
    first = flip_low + core * (flip_mid - flip_low)
    second = flip_mid + core * (flip_low - flip_mid)
    plane_one = me + 4 - 8 * (top % 2)
    plane_two = me + 8 - 16 * (top // 2)
    plane_three = me + 12 - 8 * top
    far_plane = plane_three + core * (plane_two - plane_three)
    mesh = pl.DeviceIdType.MESH

    barrier = pltpu.get_barrier_semaphore()
    for device in (first, second, plane_one, plane_two, plane_three):
        pl.semaphore_signal(barrier, inc=1, device_id=(device, core), device_id_type=mesh)
    pl.semaphore_wait(barrier, 5)

    def pass_on(source, slot, device):
        return pltpu.make_async_remote_copy(
            src_ref=source,
            dst_ref=blocks.at[slot],
            send_sem=send_sem.at[slot],
            recv_sem=recv_sem.at[slot],
            device_id=(device, core),
            device_id_type=mesh,
        )

    def give(source, target, index, device):
        return pltpu.make_async_remote_copy(
            src_ref=source,
            dst_ref=target,
            send_sem=back_send.at[index],
            recv_sem=back_recv.at[index],
            device_id=(device, core),
            device_id_type=mesh,
        )

    loads = [
        pltpu.make_async_copy(source, target, weight_sem.at[index])
        for index, (source, target) in enumerate(((wg, wg_v), (wu, wu_v), (wd, wd_v)))
    ]

    @pl.when(core == 0)
    def _():
        pass_on(own, 1, first).start()
        pass_on(own, 2, second).start()

    @pl.when(core == 1)
    def _():
        pass_on(own, 0, plane_one).start()

    pass_on(own, 4, far_plane).start()
    for copy in loads:
        copy.start()

    length = SEQ
    ordered[...] = jnp.where(
        lax.broadcasted_iota(jnp.int32, (length, length), 0)
        < lax.broadcasted_iota(jnp.int32, (length, length), 1),
        1.0,
        0.0,
    ).astype(jnp.bfloat16)
    width = block_v.shape[1]
    hidden = hidden_v.shape[1]
    both = (((1,), (1,)), ((), ()))

    def dot(left, right):
        return jnp.dot(left, right, preferred_element_type=jnp.float32)

    def dot_t(left, right):
        return lax.dot_general(left, right, both, preferred_element_type=jnp.float32)

    def add_block(slot, sources):
        for index, source in enumerate(sources):
            pltpu.make_async_copy(source, taken.at[index], load_sem.at[2 + index]).start()
        for index, source in enumerate(sources):
            pltpu.make_async_copy(source, taken.at[index], load_sem.at[2 + index]).wait()

        def rows_of(step, carry):
            span = pl.ds(pl.multiple_of(step * 16, 16), 16)
            total = stage[slot, span, :].astype(jnp.float32)
            for index in range(len(sources)):
                total = total + taken[index, span, :].astype(jnp.float32)
            stage[slot, span, :] = total.astype(jnp.bfloat16)
            return carry

        lax.fori_loop(0, (length + experts) // 16, rows_of, 0)

    def first_sum(turn):
        give(far_sums.at[2 * turn + 1], far_sums.at[2 * turn + 1], 2 * turn + 1, second).wait_recv()
        add_block(4 * turn + 1, [far_sums.at[2 * turn + 1]])
        give(stage.at[4 * turn + 1], near_sums.at[turn], 4 + turn, first).start()

    def plane_sum(turn):
        give(far_sums.at[2 * turn], far_sums.at[2 * turn], 2 * turn, second).wait_recv()
        give(near_sums.at[turn], near_sums.at[turn], 4 + turn, first).wait_recv()
        add_block(4 * turn, [far_sums.at[2 * turn], near_sums.at[turn]])

    def block_step(k, carry):
        turn_at = k % 4
        relayed = jnp.logical_or(k != 0, core != 0)

        @pl.when(relayed)
        def _():
            pass_on(blocks.at[k], k, first).wait_recv()
            pltpu.make_async_copy(blocks.at[k], block_v, load_sem.at[0]).start()

        @pl.when(jnp.logical_not(relayed))
        def _():
            pltpu.make_async_copy(own, block_v, load_sem.at[0]).start()

        @pl.when(jnp.logical_and(relayed, turn_at == 0))
        def _():
            pass_on(blocks.at[k], k + 1, first).start()

        @pl.when(jnp.logical_and(relayed, turn_at < 2))
        def _():
            pass_on(blocks.at[k], k + 2, second).start()

        for index in range(8):

            @pl.when(k == index)
            def _():
                pltpu.make_async_copy(grads[index], grad_v, load_sem.at[1]).start()


        @pl.when(k == 0)
        def _():
            for copy in loads:
                copy.wait()

        pltpu.make_async_copy(blocks.at[k], block_v, load_sem.at[0]).wait()

        here = lax.broadcasted_iota(jnp.int32, (experts, 3 * length), 0) == me
        row = jnp.sum(
            jnp.where(here, block_v[length:, : 3 * length].astype(jnp.float32), 0.0),
            axis=0,
            keepdims=True,
        )
        gate = row[:, :length] + row[:, length : 2 * length] + row[:, 2 * length :]
        used = jnp.where(gate > 0.0, 1.0, 0.0)
        slot = dot(jnp.broadcast_to(used, (16, length)).astype(jnp.bfloat16), ordered[...])[:1]
        slot = jnp.where(gate > 0.0, slot, -1.0)
        number = lax.broadcasted_iota(jnp.int32, (capacity, length), 0).astype(jnp.float32)
        pick = jnp.where(number == slot, 1.0, 0.0)
        slot_gate = jnp.sum(pick * gate, axis=1, keepdims=True)
        pick_v[...] = pick.astype(jnp.bfloat16)
        pick_t[...] = pick.T.astype(jnp.bfloat16)
        for at in range(0, width, 512):
            span = slice(at, at + 512)
            rows_v[:, span] = dot(pick_v[...], block_v[:length, span]).astype(jnp.bfloat16)
        pltpu.make_async_copy(grads[0], grad_v, load_sem.at[1]).wait()
        for at in range(0, width, 512):
            span = slice(at, at + 512)
            grows_v[:, span] = dot(pick_v[...], grad_v[:, span]).astype(jnp.bfloat16)
        slot_grad = jnp.zeros((capacity, 1), jnp.float32)
        for at in range(0, hidden, 256):
            span = slice(at, at + 256)
            gate_lin = dot(rows_v[...], wg_v[:, span])
            up_lin = dot(rows_v[...], wu_v[:, span])
            grad_full = dot_t(grows_v[...], wd_v[span, :])
            sigmoid_gate = 1.0 / (1.0 + jnp.exp(-gate_lin))
            activated = gate_lin * sigmoid_gate
            value = activated * up_lin
            hidden_v[:, span] = (value * slot_gate).astype(jnp.bfloat16)
            slot_grad = slot_grad + jnp.sum(value * grad_full, axis=1, keepdims=True)
            grad_hidden = grad_full * slot_gate
            slope = sigmoid_gate * (1.0 + gate_lin * (1.0 - sigmoid_gate))
            gate_v[:, span] = (grad_hidden * up_lin * slope).astype(jnp.bfloat16)
            up_v[:, span] = (grad_hidden * activated).astype(jnp.bfloat16)
        at = pl.multiple_of(k * capacity, capacity)
        saves = [
            pltpu.make_async_copy(source, target.at[pl.ds(at, capacity)], save_sem.at[index])
            for index, (source, target) in enumerate(
                (
                    (rows_v, rows_out),
                    (grows_v, grows_out),
                    (hidden_v, hidden_out),
                    (gate_v, gate_out),
                    (up_v, up_out),
                )
            )
        ]
        for copy in saves:
            copy.start()

        @pl.when(k > 0)
        def _():
            pltpu.make_async_copy(part_v, parts[0], save_sem.at[5]).wait()

        for at in range(0, width, 512):
            span = slice(at, at + 512)
            value = dot(hidden_v[...], wd_v[:, span]).astype(jnp.bfloat16)
            part_v[:, span] = dot(pick_t[...], value).astype(jnp.bfloat16)
            back = dot_t(gate_v[...], wg_v[span, :]) + dot_t(up_v[...], wu_v[span, :])
            stage[k, :length, span] = dot(pick_t[...], back.astype(jnp.bfloat16)).astype(
                jnp.bfloat16
            )
        total = jnp.sum(pick_v[...].astype(jnp.float32) * slot_grad, axis=0, keepdims=True)
        here = lax.broadcasted_iota(jnp.int32, (experts, length), 0) == me
        for index in range(3):
            high = total.astype(jnp.bfloat16).astype(jnp.float32)
            stage[k, length:, index * length : (index + 1) * length] = jnp.where(
                here, high, 0.0
            ).astype(jnp.bfloat16)
            total = total - high
        stage[k, length:, 3 * length :] = jnp.zeros((experts, width - 3 * length), jnp.bfloat16)
        for index in range(8):

            @pl.when(k == index)
            def _():
                pltpu.make_async_copy(part_v, parts[index], save_sem.at[5]).start()

        @pl.when(turn_at >= 2)
        def _():
            index = 2 * (k // 4) + turn_at - 2
            give(stage.at[k], far_sums.at[index], index, second).start()

        @pl.when(k == 5)
        def _():
            first_sum(0)

        @pl.when(k == 6)
        def _():
            plane_sum(0)

            @pl.when(core == 1)
            def _():
                give(stage.at[0], plane_sums.at[0], 6, plane_one).start()

        for copy in saves:
            copy.wait()
        return carry

    lax.fori_loop(0, 8, block_step, 0)
    first_sum(1)
    plane_sum(1)
    give(stage.at[4], plane_sums.at[1], 7, far_plane).start()
    give(stage.at[4], plane_sums.at[1], 7, far_plane).wait_recv()

    @pl.when(core == 1)
    def _():
        give(stage.at[0], plane_sums.at[0], 6, plane_one).wait()
        pltpu.make_async_copy(plane_sums.at[0], stage.at[0], load_sem.at[0]).start()
        pltpu.make_async_copy(plane_sums.at[0], stage.at[0], load_sem.at[0]).wait()

    add_block(0, [plane_sums.at[1]])
    final = pltpu.make_async_copy(stage.at[0], result, load_sem.at[0])
    final.start()
    pltpu.make_async_copy(part_v, parts[7], save_sem.at[5]).wait()
    for k in range(8):
        if k > 0:
            pass_on(blocks.at[k], k, first).wait_send()
    @pl.when(core == 1)
    def _():
        pass_on(blocks.at[0], 0, first).wait_send()

    for index in range(8):
        if index != 6:
            give(result, result, index, first).wait_send()
    final.wait()


def moe_layer(own, grads, wg, wu, wd, capacity):
    rows, width = own.shape
    hidden = wg.shape[1]
    experts = rows - SEQ
    low = jnp.bfloat16
    hbm = pl.BlockSpec(memory_space=pl.ANY)

    def shape(*dims):
        return jax.ShapeDtypeStruct(dims, low)

    return pl.pallas_call(
        functools.partial(moe_kernel, capacity, experts),
        in_specs=[hbm] * 12,
        out_specs=[hbm] * 18,
        out_shape=[shape(SEQ, width)] * 8
        + [
            shape(8, rows, width),
            shape(4, rows, width),
            shape(2, rows, width),
            shape(2, rows, width),
            shape(8 * capacity, width),
            shape(8 * capacity, width),
            shape(8 * capacity, hidden),
            shape(8 * capacity, hidden),
            shape(8 * capacity, hidden),
            shape(rows, width),
        ],
        scratch_shapes=[
            pltpu.VMEM((width, hidden), low),
            pltpu.VMEM((width, hidden), low),
            pltpu.VMEM((hidden, width), low),
            pltpu.VMEM((rows, width), low),
            pltpu.VMEM((SEQ, width), low),
            pltpu.VMEM((capacity, width), low),
            pltpu.VMEM((capacity, width), low),
            pltpu.VMEM((capacity, hidden), low),
            pltpu.VMEM((capacity, hidden), low),
            pltpu.VMEM((capacity, hidden), low),
            pltpu.VMEM((capacity, SEQ), low),
            pltpu.VMEM((SEQ, capacity), low),
            pltpu.VMEM((SEQ, SEQ), low),
            pltpu.VMEM((8, rows, width), low),
            pltpu.VMEM((SEQ, width), low),
            pltpu.VMEM((2, rows, width), low),
            pltpu.SemaphoreType.DMA((3,)),
            pltpu.SemaphoreType.DMA((4,)),
            pltpu.SemaphoreType.DMA((6,)),
            pltpu.SemaphoreType.DMA((8,)),
            pltpu.SemaphoreType.DMA((8,)),
            pltpu.SemaphoreType.DMA((8,)),
            pltpu.SemaphoreType.DMA((8,)),
        ],
        compiler_params=pltpu.CompilerParams(
            collective_id=0, has_side_effects=True, vmem_limit_bytes=67043328
        ),
        name="moe_layer",
    )(own, wg, wu, wd, *grads)


def local(
    tokens,
    lengths,
    routes,
    attn_gain,
    w_query,
    w_key,
    w_value,
    query_gain,
    key_gain,
    w_out,
    ffn_gain,
    w_router,
    w_gate,
    w_up,
    w_down,
    cotangent,
):
    grid = Grid(lax.axis_size("expert"))
    count = grid.count
    experts = w_router.shape[1]
    capacity = SEQ * TOP * 9 // (8 * experts)
    scale = 1.0 / math.sqrt(HD)
    low = jnp.bfloat16
    own_rows, width = w_query.shape
    heads_here = width // HD
    core = lax.axis_index("tensor")

    small = jnp.concatenate(
        [
            w_router.astype(low).T,
            jnp.pad(
                jnp.stack(
                    [
                        attn_gain.astype(low),
                        ffn_gain.astype(low),
                        jnp.pad(query_gain.astype(low), (0, own_rows - HD // count)),
                        jnp.pad(key_gain.astype(low), (0, own_rows - HD // count)),
                    ]
                ),
                ((0, experts - 4), (0, 0)),
            ),
        ],
        axis=1,
    )
    small = jnp.pad(small, ((0, 0), (0, width - 2 * own_rows)))
    mine = jnp.concatenate(
        [w_query.astype(low), w_key.astype(low), w_value.astype(low), w_out.astype(low), small],
        axis=0,
    )
    arrived = []
    for top in range(PLANES):
        base = mine if top == 0 else grid.send(mine, (top * grid.plane,) * CORES)
        arrived += spread(grid, base)
    wq_full, wk_full, wv_full, wo_full, smalls = assemble(grid, arrived, own_rows, experts)
    router_t = smalls[:, :, :own_rows].transpose(1, 0, 2).reshape(experts, D)
    gain_one = smalls[:, 0, own_rows : 2 * own_rows].reshape(D).astype(jnp.float32)
    gain_two = smalls[:, 1, own_rows : 2 * own_rows].reshape(D).astype(jnp.float32)
    head_cols = slice(own_rows, own_rows + HD // count)
    gain_query = smalls[:, 2, head_cols].reshape(HD).astype(jnp.float32)
    gain_key = smalls[:, 3, head_cols].reshape(HD).astype(jnp.float32)

    wg_own, wu_own, wd_own = (w_gate[0].astype(low), w_up[0].astype(low), w_down[0].astype(low))
    wg = jnp.concatenate([wg_own, swap(wg_own)], axis=1)
    wu = jnp.concatenate([wu_own, swap(wu_own)], axis=1)
    wd = jnp.concatenate([wd_own, swap(wd_own)], axis=0)

    allowed = jnp.arange(SEQ) < lengths[0]
    grad_two_low = jnp.where(allowed[:, None], cotangent, 0)
    grad_two_sent, wq_full, wk_full, wv_full, wo_full = lax.optimization_barrier(
        (grad_two_low, wq_full, wk_full, wv_full, wo_full)
    )
    grad_turns = gather_tokens(grid, grad_two_sent)
    grad_two = grad_two_low.astype(jnp.float32)

    cosine, sine_tab = rope_tables(SEQ, HD)
    resid_zero = tokens.astype(jnp.float32)
    normed_one, inverse_one = norm_stats(resid_zero)
    attn_in = (normed_one * gain_one).astype(low)
    query_lin = jnp.dot(attn_in, wq_full, preferred_element_type=jnp.float32).reshape(
        SEQ, heads_here, HD
    )
    key_lin = jnp.dot(attn_in, wk_full, preferred_element_type=jnp.float32).reshape(
        SEQ, heads_here, HD
    )
    values_b = (
        jnp.dot(attn_in, wv_full, preferred_element_type=jnp.float32)
        .astype(low)
        .reshape(SEQ, heads_here, HD)
    )
    query_hat, query_inv = norm_stats(query_lin)
    key_hat, key_inv = norm_stats(key_lin)
    queries = rotate(query_hat * gain_query, cosine, sine_tab).astype(low)
    keys_rot = rotate(key_hat * gain_key, cosine, sine_tab).astype(low)

    def masked_scores():
        scores = (
            jnp.einsum("qhd,khd->hqk", queries, keys_rot, preferred_element_type=jnp.float32)
            * scale
        )
        return jnp.where(allowed[None, None, :], scores, NEG_BIG)

    masked = masked_scores()
    top_score = jnp.max(masked, axis=-1, keepdims=True)
    expo_vals = jnp.exp(masked - top_score)
    totals = jnp.sum(expo_vals, axis=-1, keepdims=True)
    probs_low = (expo_vals / totals).astype(low)
    log_total = top_score + jnp.log(totals)
    mixed = (
        jnp.einsum("hqk,khd->qhd", probs_low, values_b, preferred_element_type=jnp.float32)
        .reshape(SEQ, heads_here * HD)
        .astype(low)
    )
    attn_part = contract_cols(mixed, wo_full)
    resid_one = resid_zero + (attn_part + swap(attn_part))
    normed_two, inverse_two = norm_stats(resid_one)
    ffn_in = (normed_two * gain_two).astype(low)
    logits = contract_cols(ffn_in, router_t)
    route_hot = routes[:, :, None] == jnp.arange(experts)[None, None, :]
    chosen = jnp.sum(jnp.where(route_hot, logits[:, None, :], 0.0), axis=2)
    gates = jax.nn.softmax(chosen, axis=1)
    gates_wide = jnp.sum(jnp.where(route_hot, gates[:, :, None], 0.0), axis=1)

    gate_rows = jnp.pad(split_three(gates_wide.T), ((0, 0), (0, D - 3 * SEQ)))
    token_block = jnp.concatenate([ffn_in, gate_rows], axis=0)
    if grid.side == 2:
        done = moe_layer(token_block, grad_turns[0] + grad_turns[1], wg, wu, wd, capacity)
        saved = [tuple(done[12:17])]
        out_turns = [done[:4], done[4:8]]
        back_sum = both_cores(done[17])
    else:
        token_turns = gather_tokens(grid, token_block)
        out_turns, back_turns, saved = [], [], []
        for turn in range(2):
            outs, backs, kept = expert_turn(
                token_turns[turn], grad_turns[turn], (wg, wu, wd), capacity
            )
            out_turns.append(outs)
            back_turns.append(backs)
            saved.append(kept)
        back_sum = scatter_tokens(grid, back_turns)
    out_sum = scatter_tokens(grid, out_turns)
    output = (resid_one + out_sum).astype(low)

    def over_turns(left, right):
        return sum(contract_rows(kept[left], kept[right]) for kept in saved)

    half = w_gate.shape[2]
    gate_w = over_turns(0, 3)
    up_w = over_turns(0, 4)
    down_w = over_turns(2, 1)
    grad_gate_w = (gate_w[:, :half] + swap(gate_w[:, half:]))[None]
    grad_up_w = (up_w[:, :half] + swap(up_w[:, half:]))[None]
    grad_down_w = (down_w[:half] + swap(down_w[half:]))[None]

    grad_gates_wide = join_three(back_sum[SEQ:], SEQ).T
    grad_gate_sel = jnp.sum(jnp.where(route_hot, grad_gates_wide[:, None, :], 0.0), axis=2)
    grad_chosen = gates * (grad_gate_sel - jnp.sum(gates * grad_gate_sel, axis=1, keepdims=True))
    grad_logits = jnp.sum(jnp.where(route_hot, grad_chosen[:, :, None], 0.0), axis=1).astype(low)
    grad_router_t = contract_rows(grad_logits, ffn_in)
    grad_ffn_in = back_sum[:SEQ] + jnp.dot(
        grad_logits, router_t, preferred_element_type=jnp.float32
    )
    grad_gain_two = jnp.sum(grad_ffn_in * normed_two, axis=0)
    grad_one = grad_two + norm_back(grad_ffn_in * gain_two, normed_two, inverse_two)
    grad_attn = grad_one.astype(low)

    def reduce_weight(left, right, axes):
        whole = contract_rows(left, right)
        return scatter_rows(
            grid, whole.reshape(PLANES, grid.side, grid.side, own_rows, width), axes, low
        )

    grad_wo = reduce_weight(grad_attn, mixed, (1, 2, 0))
    grad_mixed = (
        jnp.dot(grad_attn, wo_full, preferred_element_type=jnp.float32)
        .astype(low)
        .reshape(SEQ, heads_here, HD)
    )
    masked = masked_scores()
    attn_probs = jnp.exp(masked - log_total)
    probs_again = attn_probs.astype(low)
    grad_probs = jnp.einsum(
        "qhd,khd->hqk", grad_mixed, values_b, preferred_element_type=jnp.float32
    )
    grad_values = jnp.einsum(
        "hqk,qhd->khd", probs_again, grad_mixed, preferred_element_type=jnp.float32
    )
    grad_value_lin = grad_values.astype(low).reshape(SEQ, heads_here * HD)
    grad_wv = reduce_weight(attn_in, grad_value_lin, (2, 1, 0))
    grad_scores = (
        attn_probs * (grad_probs - jnp.sum(attn_probs * grad_probs, axis=-1, keepdims=True))
    ).astype(low)
    grad_queries = (
        jnp.einsum("hqk,khd->qhd", grad_scores, keys_rot, preferred_element_type=jnp.float32)
        * scale
    )
    grad_keys = (
        jnp.einsum("hqk,qhd->khd", grad_scores, queries, preferred_element_type=jnp.float32) * scale
    )
    grad_query_scaled = rotate_back(grad_queries, cosine, sine_tab)
    grad_key_scaled = rotate_back(grad_keys, cosine, sine_tab)
    grad_gain_query = jnp.sum(grad_query_scaled * query_hat, axis=(0, 1))
    grad_gain_key = jnp.sum(grad_key_scaled * key_hat, axis=(0, 1))
    grad_query_lin = (
        norm_back(grad_query_scaled * gain_query, query_hat, query_inv)
        .astype(low)
        .reshape(SEQ, heads_here * HD)
    )
    grad_key_lin = (
        norm_back(grad_key_scaled * gain_key, key_hat, key_inv)
        .astype(low)
        .reshape(SEQ, heads_here * HD)
    )
    grad_wq = reduce_weight(attn_in, grad_query_lin, (1, 2, 0))
    grad_wk = reduce_weight(attn_in, grad_key_lin, (2, 1, 0))
    grad_attn_part = (
        contract_cols(grad_query_lin, wq_full)
        + contract_cols(grad_key_lin, wk_full)
        + contract_cols(grad_value_lin, wv_full)
    ).astype(low)
    grad_attn_in = grad_attn_part.astype(jnp.float32) + swap(grad_attn_part).astype(jnp.float32)
    grad_gain_one = jnp.sum(grad_attn_in * normed_one, axis=0)
    grad_input = grad_one + norm_back(grad_attn_in * gain_one, normed_one, inverse_one)

    head_part = HD // count
    heads_row = jnp.stack([grad_gain_query, grad_gain_key]).reshape(2, count, head_part)
    heads_row = jnp.pad(heads_row, ((0, 0), (0, 0), (0, own_rows - head_part)))
    parts = jnp.concatenate(
        [
            jnp.concatenate([grad_router_t, grad_gain_one[None], grad_gain_two[None]]).reshape(
                experts + 2, count, own_rows
            ),
            heads_row,
        ],
        axis=0,
    ).transpose(1, 0, 2)
    sums = scatter_rows(
        grid,
        parts.reshape(PLANES, grid.side, grid.side, experts + 4, own_rows),
        (1, 2, 0),
        jnp.float32,
    )
    sums = sums + swap(sums)
    return (
        output,
        grad_input.astype(low),
        0.5 * sums[experts],
        grad_wq,
        grad_wk,
        grad_wv,
        sums[experts + 2, :head_part],
        sums[experts + 3, :head_part],
        grad_wo,
        0.5 * sums[experts + 1],
        0.5 * sums[:experts].T,
        grad_gate_w,
        grad_up_w,
        grad_down_w,
    )


def solution(mesh):
    return jax.shard_map(
        local,
        mesh=mesh,
        in_specs=(
            P("expert", None),
            P("expert"),
            P("expert", None),
            P("expert"),
            P("expert", "tensor"),
            P("expert", "tensor"),
            P("expert", "tensor"),
            P("expert"),
            P("expert"),
            P("expert", "tensor"),
            P("expert"),
            P("expert", None),
            P("expert", None, "tensor"),
            P("expert", None, "tensor"),
            P("expert", "tensor", None),
            P("expert", None),
        ),
        out_specs=(
            P("expert", None),
            P("expert", None),
            P("expert"),
            P("expert", "tensor"),
            P("expert", "tensor"),
            P("expert", "tensor"),
            P("expert"),
            P("expert"),
            P("expert", "tensor"),
            P("expert"),
            P("expert", None),
            P("expert", None, "tensor"),
            P("expert", None, "tensor"),
            P("expert", "tensor", None),
        ),
        check_vma=False,
    )
```

```python
import functools
import math

import jax
import jax.numpy as jnp
from jax import lax
from jax.experimental import pallas as pl
from jax.experimental.pallas import tpu as pltpu
from jax.sharding import PartitionSpec as P

D = 2048
HD = 128
TOP = 8
SEQ = 512


EPSILON = 1e-06
ROPE_BASE = 10000.0
NEG_BIG = -1e30


def rope_tables(seq_len, head_dim):
    half_dim = head_dim // 2
    inverse = ROPE_BASE ** (-(jnp.arange(half_dim).astype(jnp.float32) * 2.0 / head_dim))
    angles = jnp.arange(seq_len).astype(jnp.float32)[:, None] * inverse[None, :]
    return (jnp.cos(angles), jnp.sin(angles))


def rotate(values, cosine, sine_tab):
    half_dim = values.shape[-1] // 2
    lower_half = values[..., :half_dim]
    upper_half = values[..., half_dim:]
    cos_b = cosine[:, None, :]
    sin_b = sine_tab[:, None, :]
    return jnp.concatenate(
        [lower_half * cos_b - upper_half * sin_b, upper_half * cos_b + lower_half * sin_b], axis=-1
    )


def rotate_back(grads_in, cosine, sine_tab):
    half_dim = grads_in.shape[-1] // 2
    lower_half = grads_in[..., :half_dim]
    upper_half = grads_in[..., half_dim:]
    cos_b = cosine[:, None, :]
    sin_b = sine_tab[:, None, :]
    return jnp.concatenate(
        [lower_half * cos_b + upper_half * sin_b, upper_half * cos_b - lower_half * sin_b], axis=-1
    )


def norm_stats(values):
    inverse = lax.rsqrt(jnp.mean(values * values, axis=-1, keepdims=True) + EPSILON)
    return (values * inverse, inverse)


def norm_back(grad_normed, normed, inverse):
    return inverse * (grad_normed - normed * jnp.mean(grad_normed * normed, axis=-1, keepdims=True))


def contract_rows(left_mat, right_mat):
    return lax.dot_general(
        left_mat, right_mat, (((0,), (0,)), ((), ())), preferred_element_type=jnp.float32
    )


def contract_cols(left_mat, right_mat):
    return lax.dot_general(
        left_mat, right_mat, (((1,), (1,)), ((), ())), preferred_element_type=jnp.float32
    )


PLANES = 4
CORES = 2


class Grid:
    def __init__(self, count):
        self.count = count
        self.plane = count // PLANES
        self.side = math.isqrt(self.plane)
        self.near = range(1, self.side)

    def first(self, step):
        return (step, step * self.side)

    def second(self, step):
        return (step * self.side, step)

    def planes_of(self, turn):
        return ((0, 3)[turn] * self.plane, (1, 2)[turn] * self.plane)

    def send(self, value, masks):
        pairs = [
            (device * CORES + core, (device ^ masks[core]) * CORES + core)
            for device in range(self.count)
            for core in range(CORES)
        ]
        return lax.ppermute(value, ("expert", "tensor"), pairs)


def swap(value):
    return lax.ppermute(value, "tensor", [(0, 1), (1, 0)])


def both_cores(part):
    return part.astype(jnp.float32) + swap(part).astype(jnp.float32)


def spread(grid, base):
    row = [base] + [grid.send(base, grid.first(step)) for step in grid.near]
    blocks = list(row)
    for step in grid.near:
        blocks += [grid.send(block, grid.second(step)) for block in row]
    return blocks


def gather_tokens(grid, block):
    return [spread(grid, grid.send(block, grid.planes_of(turn))) for turn in range(2)]


def collect(grid, blocks):
    side = grid.side
    sums = [block.astype(jnp.float32) for block in blocks[:side]]
    for far in grid.near:
        for step in range(side):
            sums[step] = sums[step] + grid.send(
                blocks[far * side + step], grid.second(far)
            ).astype(jnp.float32)
    total = sums[0]
    for step in grid.near:
        total = total + grid.send(sums[step].astype(jnp.bfloat16), grid.first(step)).astype(
            jnp.float32
        )
    return total


def scatter_tokens(grid, turns):
    total = None
    for turn in (1, 0):
        part = grid.send(collect(grid, turns[turn]).astype(jnp.bfloat16), grid.planes_of(turn))
        part = part.astype(jnp.float32)
        total = part if total is None else total + part
    return both_cores(total.astype(jnp.bfloat16))


def scatter_rows(grid, value, axes, wire):
    me = lax.axis_index("expert")
    units = (grid.plane, grid.side, 1)
    sizes = (PLANES, grid.side, grid.side)
    gone = []
    for axis in axes:
        unit, size = units[axis], sizes[axis]
        place = (me // unit) % size
        at = axis - sum(1 for other in gone if other < axis)
        total = lax.dynamic_index_in_dim(value, place, at, keepdims=False).astype(jnp.float32)
        for step in range(1, size):
            part = lax.dynamic_index_in_dim(value, place ^ step, at, keepdims=False).astype(wire)
            total = total + grid.send(part, (unit * step,) * CORES).astype(jnp.float32)
        value = total
        gone.append(axis)
    return value


def assemble(grid, blocks, rows, extra):
    count, width = grid.count, blocks[0].shape[1]
    me = lax.axis_index("expert")
    core = lax.axis_index("tensor")
    place = jnp.arange(count)
    top, mid, low = place // grid.plane, (place // grid.side) % grid.side, place % grid.side
    turned = top * grid.plane + low * grid.side + mid
    owner = me ^ jnp.where(core == 0, place, turned)

    def body(owner_ref, *refs):
        ins, outs, small, sem = refs[:count], refs[count : count + 4], refs[count + 4], refs[-1]
        copies = []
        for index in range(count):
            at = owner_ref[index]
            for which in range(4):
                copies.append(
                    pltpu.make_async_copy(
                        ins[index].at[pl.ds(which * rows, rows)],
                        outs[which].at[pl.ds(pl.multiple_of(at * rows, rows), rows)],
                        sem.at[index, which],
                    )
                )
            copies.append(
                pltpu.make_async_copy(
                    ins[index].at[pl.ds(4 * rows, extra)], small.at[at], sem.at[index, 4]
                )
            )
        for copy in copies:
            copy.start()
        for copy in copies:
            copy.wait()

    full = jax.ShapeDtypeStruct((count * rows, width), jnp.bfloat16)
    small = jax.ShapeDtypeStruct((count, extra, width), jnp.bfloat16)
    return pl.pallas_call(
        body,
        grid_spec=pltpu.PrefetchScalarGridSpec(
            num_scalar_prefetch=1,
            grid=(),
            in_specs=[pl.BlockSpec(memory_space=pl.ANY)] * count,
            out_specs=[pl.BlockSpec(memory_space=pltpu.VMEM)] * 5,
            scratch_shapes=[pltpu.SemaphoreType.DMA((count, 5))],
        ),
        out_shape=[full] * 4 + [small],
        name="assemble",
    )(owner, *blocks)


class Place:
    def __init__(self):
        self.me = me = lax.axis_index("expert")
        self.core = core = lax.axis_index("tensor")
        top, mid, low = me // 4, (me // 2) % 2, me % 2
        flip_low = me + 1 - 2 * low
        flip_mid = me + 2 - 4 * mid
        self.first = flip_low + core * (flip_mid - flip_low)
        self.second = flip_mid + core * (flip_low - flip_mid)
        self.planes = (
            me,
            me + 4 - 8 * (top % 2),
            me + 8 - 16 * (top // 2),
            me + 12 - 8 * top,
        )

    def owner(self, plane, far, near):
        return self.planes[plane] + far * (self.second - self.me) + near * (self.first - self.me)

    def greet(self, sibling):
        barrier = pltpu.get_barrier_semaphore()
        partners = [(device, self.core) for device in (self.first, self.second) + self.planes[1:]]
        if sibling:
            partners.append((self.me, 1 - self.core))
        for partner in partners:
            pl.semaphore_signal(
                barrier, inc=1, device_id=partner, device_id_type=pl.DeviceIdType.MESH
            )
        pl.semaphore_wait(barrier, len(partners))


def remote(source, target, send, recv, device):
    return pltpu.make_async_remote_copy(
        src_ref=source,
        dst_ref=target,
        send_sem=send,
        recv_sem=recv,
        device_id=device,
        device_id_type=pl.DeviceIdType.MESH,
    )


def gather_kernel(rows, *refs):
    mine, grad, halves, refs = refs[:5], refs[5], refs[6:9], refs[9:]
    full, grads, others, refs = refs[:5], refs[5], refs[6:9], refs[9:]
    send_sem, recv_sem, grad_send, grad_recv, half_send, half_recv, own_sem = refs
    place = Place()
    core = place.core
    place.greet(True)

    def part(which, plane, far, near):
        owner = place.owner(plane, far, near)
        if which == 4:
            return full[4].at[owner]
        return full[which].at[pl.ds(pl.multiple_of(owner * rows, rows), rows)]

    def pass_weights(source, plane, slot, device):
        out = []
        for which in range(5):
            here = part(which, *source)
            out.append(
                remote(
                    mine[which] if source == (0, 0, 0) else here,
                    here,
                    send_sem.at[4 * plane + slot, which],
                    recv_sem.at[4 * plane + slot, which],
                    (device, core),
                )
            )
        return out

    def start(copies):
        for copy in copies:
            copy.start()

    def arrived(plane, slot):
        for copy in pass_weights((plane, slot // 2, slot % 2), plane, slot, place.first):
            copy.wait_recv()

    def pass_grad(source, slot, device):
        return remote(
            source, grads.at[slot], grad_send.at[slot], grad_recv.at[slot], (device, core)
        )

    for plane in (1, 2, 3):
        start(pass_weights((0, 0, 0), plane, 0, place.planes[plane]))
    start(pass_weights((0, 0, 0), 0, 1, place.first))
    start(pass_weights((0, 0, 0), 0, 2, place.second))
    far_plane = place.planes[3] + core * (place.planes[2] - place.planes[3])

    @pl.when(core == 1)
    def _():
        pass_grad(grad, 0, place.planes[1]).start()

    pass_grad(grad, 4, far_plane).start()
    swaps = [
        remote(halves[i], others[i], half_send.at[i], half_recv.at[i], (place.me, 1 - core))
        for i in range(3)
    ]
    start(swaps)
    keeps = [
        pltpu.make_async_copy(mine[which], part(which, 0, 0, 0), own_sem.at[which])
        for which in range(5)
    ]
    start(keeps)

    @pl.when(core == 0)
    def _():
        pltpu.make_async_copy(grad, grads.at[0], own_sem.at[5]).start()

    for plane in range(4):
        if plane > 0:
            arrived(plane, 0)
            start(pass_weights((plane, 0, 0), plane, 1, place.first))
            start(pass_weights((plane, 0, 0), plane, 2, place.second))
        arrived(plane, 1)
        start(pass_weights((plane, 0, 1), plane, 3, place.second))

    @pl.when(core == 0)
    def _():
        pass_grad(grad, 1, place.first).start()
        pass_grad(grad, 2, place.second).start()

    @pl.when(core == 1)
    def _():
        pass_grad(grads.at[0], 0, place.first).wait_recv()
        pass_grad(grads.at[0], 1, place.first).start()
        pass_grad(grads.at[0], 2, place.second).start()

    pass_grad(grads.at[1], 1, place.first).wait_recv()
    pass_grad(grads.at[1], 3, place.second).start()
    pass_grad(grads.at[4], 4, place.first).wait_recv()
    pass_grad(grads.at[4], 5, place.first).start()
    pass_grad(grads.at[4], 6, place.second).start()
    pass_grad(grads.at[5], 5, place.first).wait_recv()
    pass_grad(grads.at[5], 7, place.second).start()

    for plane in range(4):
        arrived(plane, 2)
        arrived(plane, 3)
    for slot in (2, 3, 6, 7):
        pass_grad(grads.at[slot], slot, place.first).wait_recv()
    for slot in range(1, 16):
        for copy in pass_weights((slot // 4, 0, 0), slot // 4, slot % 4, place.first):
            copy.wait_send()
    for slot in range(1, 8):
        pass_grad(grads.at[slot], slot, place.first).wait_send()

    @pl.when(core == 1)
    def _():
        pass_grad(grads.at[0], 0, place.first).wait_send()

    @pl.when(core == 0)
    def _():
        pltpu.make_async_copy(grad, grads.at[0], own_sem.at[5]).wait()

    for copy in swaps + keeps:
        copy.wait()


def gather_all(mine, grad, halves, count):
    rows, width = mine[0].shape
    extra = mine[4].shape[0]
    low = jnp.bfloat16
    hbm = pl.BlockSpec(memory_space=pl.ANY)
    full = jax.ShapeDtypeStruct((count * rows, width), low)
    return pl.pallas_call(
        functools.partial(gather_kernel, rows),
        in_specs=[hbm] * 9,
        out_specs=[hbm] * 9,
        out_shape=[full] * 4
        + [
            jax.ShapeDtypeStruct((count, extra, width), low),
            jax.ShapeDtypeStruct((8,) + grad.shape, low),
        ]
        + [jax.ShapeDtypeStruct(half.shape, low) for half in halves],
        scratch_shapes=[
            pltpu.SemaphoreType.DMA((16, 5)),
            pltpu.SemaphoreType.DMA((16, 5)),
            pltpu.SemaphoreType.DMA((8,)),
            pltpu.SemaphoreType.DMA((8,)),
            pltpu.SemaphoreType.DMA((3,)),
            pltpu.SemaphoreType.DMA((3,)),
            pltpu.SemaphoreType.DMA((6,)),
        ],
        compiler_params=pltpu.CompilerParams(collective_id=1, has_side_effects=True),
        name="gather_all",
    )(*mine, grad, *halves)


def reduce_kernel(rows, *refs):
    whole, small, halves, refs = refs[:4], refs[4], refs[5:8], refs[8:]
    out, small_out, others, refs = refs[:4], refs[4], refs[5:8], refs[8:]
    (
        own,
        far_in,
        near_in,
        plane_in,
        near_stage,
        plane_stage,
        small_own,
        small_far,
        small_near,
        small_plane,
        small_near_stage,
        small_plane_stage,
        small_last,
        small_other,
        load_sem,
        far_send,
        far_recv,
        near_send,
        near_recv,
        plane_send,
        plane_recv,
        half_send,
        half_recv,
        last_send,
        last_recv,
    ) = refs
    place = Place()
    core = place.core
    sibling = (place.me, 1 - core)
    place.greet(True)
    second, first = (place.second, core), (place.first, core)

    def source(which, plane, far, near):
        owner = place.owner(plane, far, near)
        if which == 4:
            return small.at[owner]
        return whole[which].at[pl.ds(pl.multiple_of(owner * rows, rows), rows)]

    def load(which, plane, near):
        target = small_own.at[2 * plane + near] if which == 4 else own.at[2 * plane + near, which]
        return pltpu.make_async_copy(
            source(which, plane, 0, near), target, load_sem.at[2 * plane + near, which]
        )

    def to_second(which, plane, near):
        target = small_far.at[2 * plane + near]
        if which != 4:
            target = far_in.at[2 * plane + near, which]
        return remote(
            source(which, plane, 1, near),
            target,
            far_send.at[2 * plane + near, which],
            far_recv.at[2 * plane + near, which],
            second,
        )

    def to_first(which, plane):
        here, there = small_near_stage.at[plane], small_near.at[plane]
        if which is not None:
            here, there = near_stage.at[plane, which], near_in.at[plane, which]
        at = 4 if which is None else which
        return remote(here, there, near_send.at[plane, at], near_recv.at[plane, at], first)

    def to_plane(which, plane):
        here, there = small_plane_stage.at[plane - 1], small_plane.at[plane - 1]
        if which is not None:
            here, there = plane_stage.at[plane - 1, which], plane_in.at[plane - 1, which]
        at = 4 if which is None else which
        return remote(
            here,
            there,
            plane_send.at[plane - 1, at],
            plane_recv.at[plane - 1, at],
            (place.planes[plane], core),
        )

    for plane in (3, 2, 1, 0):
        for near in (1, 0):
            for which in range(5):
                to_second(which, plane, near).start()
    for plane in (3, 2, 1, 0):
        for near in (1, 0):
            for which in range(5):
                load(which, plane, near).start()
    middle = others[0].shape[1]
    theirs = [
        halves[0].at[:, pl.ds(middle, middle)],
        halves[1].at[:, pl.ds(middle, middle)],
        halves[2].at[pl.ds(middle, middle)],
    ]
    swaps = [
        remote(theirs[i], others[i], half_send.at[i], half_recv.at[i], sibling) for i in range(3)
    ]
    for copy in swaps:
        copy.start()

    def added(parts, target):
        total = parts[0].astype(jnp.float32)
        for value in parts[1:]:
            total = total + value.astype(jnp.float32)
        return total.astype(target.dtype)

    def over_rows(parts, target):
        def body(step, carry):
            span = pl.ds(pl.multiple_of(step * 16, 16), 16)
            target[span, :] = added([part[span, :] for part in parts], target)
            return carry

        lax.fori_loop(0, rows // 16, body, 0)

    def near_sums(plane):
        for which in range(4):
            load(which, plane, 1).wait()
            to_second(which, plane, 1).wait_recv()
            over_rows(
                [own.at[2 * plane + 1, which], far_in.at[2 * plane + 1, which]],
                near_stage.at[plane, which],
            )
            to_first(which, plane).start()
        load(4, plane, 1).wait()
        to_second(4, plane, 1).wait_recv()
        small_near_stage[plane] = small_own[2 * plane + 1] + small_far[2 * plane + 1]
        to_first(None, plane).start()

    def plane_sums(plane):
        for which in range(4):
            load(which, plane, 0).wait()
            to_second(which, plane, 0).wait_recv()
            to_first(which, plane).wait_recv()
            over_rows(
                [
                    own.at[2 * plane, which],
                    far_in.at[2 * plane, which],
                    near_in.at[plane, which],
                ],
                plane_stage.at[plane - 1, which],
            )
            to_plane(which, plane).start()
        load(4, plane, 0).wait()
        to_second(4, plane, 0).wait_recv()
        to_first(None, plane).wait_recv()
        small_plane_stage[plane - 1] = (
            small_own[2 * plane] + small_far[2 * plane] + small_near[plane]
        )
        to_plane(None, plane).start()

    near_sums(3)
    near_sums(2)
    plane_sums(3)
    near_sums(1)
    plane_sums(2)
    near_sums(0)
    plane_sums(1)
    load(4, 0, 0).wait()
    to_second(4, 0, 0).wait_recv()
    to_first(None, 0).wait_recv()
    for plane in (1, 2, 3):
        to_plane(None, plane).wait_recv()
    small_last[...] = (
        small_own[0]
        + small_far[0]
        + small_near[0]
        + small_plane[0]
        + small_plane[1]
        + small_plane[2]
    )
    last = remote(small_last, small_other, last_send.at[0], last_recv.at[0], sibling)
    last.start()
    for which in range(4):
        load(which, 0, 0).wait()
        to_second(which, 0, 0).wait_recv()
        to_first(which, 0).wait_recv()
        for plane in (1, 2, 3):
            to_plane(which, plane).wait_recv()
        over_rows(
            [own.at[0, which], far_in.at[0, which], near_in.at[0, which]]
            + [plane_in.at[plane, which] for plane in range(3)],
            out[which],
        )
    last.wait()
    small_out[...] = small_last[...] + small_other[...]
    for plane in range(4):
        for which in range(5):
            at = None if which == 4 else which
            for near in range(2):
                to_second(which, plane, near).wait_send()
            to_first(at, plane).wait_send()
            if plane > 0:
                to_plane(at, plane).wait_send()
    for copy in swaps:
        copy.wait()


def reduce_all(whole, small, halves, count):
    rows, width = whole[0].shape[0] // count, whole[0].shape[1]
    low = jnp.bfloat16
    hbm = pl.BlockSpec(memory_space=pl.ANY)
    vmem = pl.BlockSpec(memory_space=pltpu.VMEM)
    tiny = small.shape[1:]

    def wide(*dims):
        return pltpu.VMEM(dims + (rows, width), low)

    def little(*dims):
        return pltpu.VMEM(dims + tiny, jnp.float32)

    def sems(*dims):
        return pltpu.SemaphoreType.DMA(dims)

    return pl.pallas_call(
        functools.partial(reduce_kernel, rows),
        in_specs=[hbm] * 8,
        out_specs=[vmem] * 5 + [hbm] * 3,
        out_shape=[jax.ShapeDtypeStruct((rows, width), jnp.float32)] * 4
        + [jax.ShapeDtypeStruct(tiny, jnp.float32)]
        + [
            jax.ShapeDtypeStruct((dims[0] // cut, dims[1] // (3 - cut)), jnp.float32)
            for dims, cut in ((halves[0].shape, 1), (halves[1].shape, 1), (halves[2].shape, 2))
        ],
        scratch_shapes=[wide(8, 4), wide(8, 4), wide(4, 4), wide(3, 4), wide(4, 4), wide(3, 4)]
        + [little(8), little(8), little(4), little(3), little(4), little(3), little(), little()]
        + [sems(8, 5)] * 3
        + [sems(4, 5)] * 2
        + [sems(3, 5)] * 2
        + [sems(3)] * 2
        + [sems(1)] * 2,
        compiler_params=pltpu.CompilerParams(
            collective_id=2, has_side_effects=True, vmem_limit_bytes=60 * 1024 * 1024
        ),
        name="reduce_all",
    )(*whole, small, *halves)


def split_three(value):
    high = value.astype(jnp.bfloat16)
    rest = value - high.astype(jnp.float32)
    middle = rest.astype(jnp.bfloat16)
    low = (rest - middle.astype(jnp.float32)).astype(jnp.bfloat16)
    return jnp.concatenate([high, middle, low], axis=-1)


def join_three(parts, length):
    parts = parts.astype(jnp.float32)
    return (
        parts[..., :length] + parts[..., length : 2 * length] + parts[..., 2 * length : 3 * length]
    )


def expert_turn(blocks, grads, weights, capacity):
    wg, wu, wd = weights
    me = lax.axis_index("expert")
    experts = blocks[0].shape[0] - SEQ
    gate = jnp.concatenate(
        [
            join_three(lax.dynamic_slice(block, (SEQ + me, 0), (1, 3 * SEQ)), SEQ)
            for block in blocks
        ],
        axis=0,
    )
    used = gate > 0.0
    ordered = (jnp.arange(SEQ)[:, None] < jnp.arange(SEQ)[None, :]).astype(jnp.bfloat16)
    slot = jnp.dot(used.astype(jnp.bfloat16), ordered, preferred_element_type=jnp.float32)
    slot = slot.astype(jnp.int32)
    hot = (jnp.arange(capacity)[None, :, None] == slot[:, None, :]) & used[:, None, :]
    pick = hot.astype(jnp.bfloat16)
    slot_gate = jnp.sum(jnp.where(hot, gate[:, None, :], 0.0), axis=2).reshape(-1, 1)
    rows = jnp.concatenate(
        [
            jnp.dot(pick[i], block[:SEQ], preferred_element_type=jnp.float32).astype(jnp.bfloat16)
            for i, block in enumerate(blocks)
        ],
        axis=0,
    )
    grad_rows = jnp.concatenate(
        [
            jnp.dot(pick[i], block, preferred_element_type=jnp.float32).astype(jnp.bfloat16)
            for i, block in enumerate(grads)
        ],
        axis=0,
    )
    gate_lin = jnp.dot(rows, wg, preferred_element_type=jnp.float32)
    up_lin = jnp.dot(rows, wu, preferred_element_type=jnp.float32)
    grad_full = contract_cols(grad_rows, wd)
    sigmoid_gate = jax.nn.sigmoid(gate_lin)
    activated = gate_lin * sigmoid_gate
    hidden = activated * up_lin
    hidden_low = (hidden * slot_gate).astype(jnp.bfloat16)
    slot_grad = jnp.sum(hidden * grad_full, axis=1).reshape(len(blocks), capacity, 1)
    grad_hidden = grad_full * slot_gate
    silu_slope = sigmoid_gate * (1.0 + gate_lin * (1.0 - sigmoid_gate))
    grad_gate = (grad_hidden * up_lin * silu_slope).astype(jnp.bfloat16)
    grad_up = (grad_hidden * activated).astype(jnp.bfloat16)
    value = jnp.dot(hidden_low, wd, preferred_element_type=jnp.float32).astype(jnp.bfloat16)
    grad_in = (contract_cols(grad_gate, wg) + contract_cols(grad_up, wu)).astype(jnp.bfloat16)
    token_grad = split_three(jnp.sum(jnp.where(hot, slot_grad, 0.0), axis=1))
    outs, backs = [], []
    for i in range(len(blocks)):
        span = slice(i * capacity, (i + 1) * capacity)
        outs.append(contract_rows(pick[i], value[span]).astype(jnp.bfloat16))
        back = contract_rows(pick[i], grad_in[span]).astype(jnp.bfloat16)
        extra = jnp.where(
            (jnp.arange(experts) == me)[:, None],
            jnp.pad(token_grad[i : i + 1], ((0, 0), (0, D - 3 * SEQ))),
            0,
        )
        backs.append(jnp.concatenate([back, extra], axis=0))
    return outs, backs, (rows, grad_rows, hidden_low, grad_gate, grad_up)


def moe_kernel(
    capacity,
    experts,
    own,
    *refs,
):
    weights, grads, refs = refs[:6], refs[6], refs[7:]
    parts, refs = refs[:8], refs[8:]
    (
    blocks,
    far_sums,
    near_sums,
    plane_sums,
    rows_out,
    grows_out,
    hidden_out,
    gate_out,
    up_out,
    result,
    wg_v,
    wu_v,
    wd_v,
    block_v,
    grad_v,
    rows_v,
    grows_v,
    hidden_v,
    gate_v,
    up_v,
    pick_v,
    pick_t,
    ordered,
    stage,
    part_v,
    taken,
    weight_sem,
    load_sem,
    save_sem,
    send_sem,
    recv_sem,
    back_send,
    back_recv,
    ) = refs
    me = lax.axis_index("expert")
    core = lax.axis_index("tensor")
    top, mid, low = me // 4, (me // 2) % 2, me % 2
    flip_low = me + 1 - 2 * low
    flip_mid = me + 2 - 4 * mid
    first = flip_low + core * (flip_mid - flip_low)
    second = flip_mid + core * (flip_low - flip_mid)
    plane_one = me + 4 - 8 * (top % 2)
    plane_two = me + 8 - 16 * (top // 2)
    plane_three = me + 12 - 8 * top
    far_plane = plane_three + core * (plane_two - plane_three)
    mesh = pl.DeviceIdType.MESH

    barrier = pltpu.get_barrier_semaphore()
    for device in (first, second, plane_one, plane_two, plane_three):
        pl.semaphore_signal(barrier, inc=1, device_id=(device, core), device_id_type=mesh)
    pl.semaphore_wait(barrier, 5)

    def pass_on(source, slot, device):
        return pltpu.make_async_remote_copy(
            src_ref=source,
            dst_ref=blocks.at[slot],
            send_sem=send_sem.at[slot],
            recv_sem=recv_sem.at[slot],
            device_id=(device, core),
            device_id_type=mesh,
        )

    def give(source, target, index, device):
        return pltpu.make_async_remote_copy(
            src_ref=source,
            dst_ref=target,
            send_sem=back_send.at[index],
            recv_sem=back_recv.at[index],
            device_id=(device, core),
            device_id_type=mesh,
        )

    half = wg_v.shape[1] // 2
    targets = []
    for span in (slice(0, half), slice(half, 2 * half)):
        targets += [wg_v.at[:, span], wu_v.at[:, span], wd_v.at[span]]
    loads = [
        pltpu.make_async_copy(source, target, weight_sem.at[index])
        for index, (source, target) in enumerate(zip(weights, targets))
    ]

    @pl.when(core == 0)
    def _():
        pass_on(own, 1, first).start()
        pass_on(own, 2, second).start()

    @pl.when(core == 1)
    def _():
        pass_on(own, 0, plane_one).start()

    pass_on(own, 4, far_plane).start()
    for copy in loads:
        copy.start()

    length = SEQ
    ordered[...] = jnp.where(
        lax.broadcasted_iota(jnp.int32, (length, length), 0)
        < lax.broadcasted_iota(jnp.int32, (length, length), 1),
        1.0,
        0.0,
    ).astype(jnp.bfloat16)
    width = block_v.shape[1]
    hidden = hidden_v.shape[1]
    both = (((1,), (1,)), ((), ()))

    def dot(left, right):
        return jnp.dot(left, right, preferred_element_type=jnp.float32)

    def dot_t(left, right):
        return lax.dot_general(left, right, both, preferred_element_type=jnp.float32)

    def add_block(slot, sources):
        for index, source in enumerate(sources):
            pltpu.make_async_copy(source, taken.at[index], load_sem.at[2 + index]).start()
        for index, source in enumerate(sources):
            pltpu.make_async_copy(source, taken.at[index], load_sem.at[2 + index]).wait()

        def rows_of(step, carry):
            span = pl.ds(pl.multiple_of(step * 16, 16), 16)
            total = stage[slot, span, :].astype(jnp.float32)
            for index in range(len(sources)):
                total = total + taken[index, span, :].astype(jnp.float32)
            stage[slot, span, :] = total.astype(jnp.bfloat16)
            return carry

        lax.fori_loop(0, (length + experts) // 16, rows_of, 0)

    def first_sum(turn):
        give(far_sums.at[2 * turn + 1], far_sums.at[2 * turn + 1], 2 * turn + 1, second).wait_recv()
        add_block(4 * turn + 1, [far_sums.at[2 * turn + 1]])
        give(stage.at[4 * turn + 1], near_sums.at[turn], 4 + turn, first).start()

    def plane_sum(turn):
        give(far_sums.at[2 * turn], far_sums.at[2 * turn], 2 * turn, second).wait_recv()
        give(near_sums.at[turn], near_sums.at[turn], 4 + turn, first).wait_recv()
        add_block(4 * turn, [far_sums.at[2 * turn], near_sums.at[turn]])

    def block_step(k, carry):
        turn_at = k % 4
        relayed = jnp.logical_or(k != 0, core != 0)

        @pl.when(relayed)
        def _():
            pass_on(blocks.at[k], k, first).wait_recv()
            pltpu.make_async_copy(blocks.at[k], block_v, load_sem.at[0]).start()

        @pl.when(jnp.logical_not(relayed))
        def _():
            pltpu.make_async_copy(own, block_v, load_sem.at[0]).start()

        @pl.when(jnp.logical_and(relayed, turn_at == 0))
        def _():
            pass_on(blocks.at[k], k + 1, first).start()

        @pl.when(jnp.logical_and(relayed, turn_at < 2))
        def _():
            pass_on(blocks.at[k], k + 2, second).start()

        pltpu.make_async_copy(grads.at[k], grad_v, load_sem.at[1]).start()

        @pl.when(k == 0)
        def _():
            for copy in loads:
                copy.wait()

        pltpu.make_async_copy(blocks.at[k], block_v, load_sem.at[0]).wait()

        here = lax.broadcasted_iota(jnp.int32, (experts, 3 * length), 0) == me
        row = jnp.sum(
            jnp.where(here, block_v[length:, : 3 * length].astype(jnp.float32), 0.0),
            axis=0,
            keepdims=True,
        )
        gate = row[:, :length] + row[:, length : 2 * length] + row[:, 2 * length :]
        used = jnp.where(gate > 0.0, 1.0, 0.0)
        slot = dot(jnp.broadcast_to(used, (16, length)).astype(jnp.bfloat16), ordered[...])[:1]
        slot = jnp.where(gate > 0.0, slot, -1.0)
        number = lax.broadcasted_iota(jnp.int32, (capacity, length), 0).astype(jnp.float32)
        pick = jnp.where(number == slot, 1.0, 0.0)
        slot_gate = jnp.sum(pick * gate, axis=1, keepdims=True)
        pick_v[...] = pick.astype(jnp.bfloat16)
        pick_t[...] = pick.T.astype(jnp.bfloat16)
        for at in range(0, width, 512):
            span = slice(at, at + 512)
            rows_v[:, span] = dot(pick_v[...], block_v[:length, span]).astype(jnp.bfloat16)
        pltpu.make_async_copy(grads.at[k], grad_v, load_sem.at[1]).wait()
        for at in range(0, width, 512):
            span = slice(at, at + 512)
            grows_v[:, span] = dot(pick_v[...], grad_v[:, span]).astype(jnp.bfloat16)
        slot_grad = jnp.zeros((capacity, 1), jnp.float32)
        for at in range(0, hidden, 256):
            span = slice(at, at + 256)
            gate_lin = dot(rows_v[...], wg_v[:, span])
            up_lin = dot(rows_v[...], wu_v[:, span])
            grad_full = dot_t(grows_v[...], wd_v[span, :])
            sigmoid_gate = 1.0 / (1.0 + jnp.exp(-gate_lin))
            activated = gate_lin * sigmoid_gate
            value = activated * up_lin
            hidden_v[:, span] = (value * slot_gate).astype(jnp.bfloat16)
            slot_grad = slot_grad + jnp.sum(value * grad_full, axis=1, keepdims=True)
            grad_hidden = grad_full * slot_gate
            slope = sigmoid_gate * (1.0 + gate_lin * (1.0 - sigmoid_gate))
            gate_v[:, span] = (grad_hidden * up_lin * slope).astype(jnp.bfloat16)
            up_v[:, span] = (grad_hidden * activated).astype(jnp.bfloat16)
        at = pl.multiple_of(k * capacity, capacity)
        saves = [
            pltpu.make_async_copy(source, target.at[pl.ds(at, capacity)], save_sem.at[index])
            for index, (source, target) in enumerate(
                (
                    (rows_v, rows_out),
                    (grows_v, grows_out),
                    (hidden_v, hidden_out),
                    (gate_v, gate_out),
                    (up_v, up_out),
                )
            )
        ]
        for copy in saves:
            copy.start()

        @pl.when(k > 0)
        def _():
            pltpu.make_async_copy(part_v, parts[0], save_sem.at[5]).wait()

        for at in range(0, width, 512):
            span = slice(at, at + 512)
            value = dot(hidden_v[...], wd_v[:, span]).astype(jnp.bfloat16)
            part_v[:, span] = dot(pick_t[...], value).astype(jnp.bfloat16)
            back = dot_t(gate_v[...], wg_v[span, :]) + dot_t(up_v[...], wu_v[span, :])
            stage[k, :length, span] = dot(pick_t[...], back.astype(jnp.bfloat16)).astype(
                jnp.bfloat16
            )
        total = jnp.sum(pick_v[...].astype(jnp.float32) * slot_grad, axis=0, keepdims=True)
        here = lax.broadcasted_iota(jnp.int32, (experts, length), 0) == me
        for index in range(3):
            high = total.astype(jnp.bfloat16).astype(jnp.float32)
            stage[k, length:, index * length : (index + 1) * length] = jnp.where(
                here, high, 0.0
            ).astype(jnp.bfloat16)
            total = total - high
        stage[k, length:, 3 * length :] = jnp.zeros((experts, width - 3 * length), jnp.bfloat16)
        for index in range(8):

            @pl.when(k == index)
            def _():
                pltpu.make_async_copy(part_v, parts[index], save_sem.at[5]).start()

        @pl.when(turn_at >= 2)
        def _():
            index = 2 * (k // 4) + turn_at - 2
            give(stage.at[k], far_sums.at[index], index, second).start()

        @pl.when(k == 5)
        def _():
            first_sum(0)

        @pl.when(k == 6)
        def _():
            plane_sum(0)

            @pl.when(core == 1)
            def _():
                give(stage.at[0], plane_sums.at[0], 6, plane_one).start()

        for copy in saves:
            copy.wait()
        return carry

    lax.fori_loop(0, 8, block_step, 0)
    first_sum(1)
    plane_sum(1)
    give(stage.at[4], plane_sums.at[1], 7, far_plane).start()
    give(stage.at[4], plane_sums.at[1], 7, far_plane).wait_recv()

    @pl.when(core == 1)
    def _():
        give(stage.at[0], plane_sums.at[0], 6, plane_one).wait()
        pltpu.make_async_copy(plane_sums.at[0], stage.at[0], load_sem.at[0]).start()
        pltpu.make_async_copy(plane_sums.at[0], stage.at[0], load_sem.at[0]).wait()

    add_block(0, [plane_sums.at[1]])
    final = pltpu.make_async_copy(stage.at[0], result, load_sem.at[0])
    final.start()
    pltpu.make_async_copy(part_v, parts[7], save_sem.at[5]).wait()
    for k in range(8):
        if k > 0:
            pass_on(blocks.at[k], k, first).wait_send()
    @pl.when(core == 1)
    def _():
        pass_on(blocks.at[0], 0, first).wait_send()

    for index in range(8):
        if index != 6:
            give(result, result, index, first).wait_send()
    final.wait()


def moe_layer(own, grads, weights, capacity):
    rows, width = own.shape
    hidden = 2 * weights[0].shape[1]
    experts = rows - SEQ
    low = jnp.bfloat16
    hbm = pl.BlockSpec(memory_space=pl.ANY)

    def shape(*dims):
        return jax.ShapeDtypeStruct(dims, low)

    return pl.pallas_call(
        functools.partial(moe_kernel, capacity, experts),
        in_specs=[hbm] * 8,
        out_specs=[hbm] * 18,
        out_shape=[shape(SEQ, width)] * 8
        + [
            shape(8, rows, width),
            shape(4, rows, width),
            shape(2, rows, width),
            shape(2, rows, width),
            shape(8 * capacity, width),
            shape(8 * capacity, width),
            shape(8 * capacity, hidden),
            shape(8 * capacity, hidden),
            shape(8 * capacity, hidden),
            shape(rows, width),
        ],
        scratch_shapes=[
            pltpu.VMEM((width, hidden), low),
            pltpu.VMEM((width, hidden), low),
            pltpu.VMEM((hidden, width), low),
            pltpu.VMEM((rows, width), low),
            pltpu.VMEM((SEQ, width), low),
            pltpu.VMEM((capacity, width), low),
            pltpu.VMEM((capacity, width), low),
            pltpu.VMEM((capacity, hidden), low),
            pltpu.VMEM((capacity, hidden), low),
            pltpu.VMEM((capacity, hidden), low),
            pltpu.VMEM((capacity, SEQ), low),
            pltpu.VMEM((SEQ, capacity), low),
            pltpu.VMEM((SEQ, SEQ), low),
            pltpu.VMEM((8, rows, width), low),
            pltpu.VMEM((SEQ, width), low),
            pltpu.VMEM((2, rows, width), low),
            pltpu.SemaphoreType.DMA((6,)),
            pltpu.SemaphoreType.DMA((4,)),
            pltpu.SemaphoreType.DMA((6,)),
            pltpu.SemaphoreType.DMA((8,)),
            pltpu.SemaphoreType.DMA((8,)),
            pltpu.SemaphoreType.DMA((8,)),
            pltpu.SemaphoreType.DMA((8,)),
        ],
        compiler_params=pltpu.CompilerParams(
            collective_id=0, has_side_effects=True, vmem_limit_bytes=67043328
        ),
        name="moe_layer",
    )(own, *weights, grads)


def local(
    tokens,
    lengths,
    routes,
    attn_gain,
    w_query,
    w_key,
    w_value,
    query_gain,
    key_gain,
    w_out,
    ffn_gain,
    w_router,
    w_gate,
    w_up,
    w_down,
    cotangent,
):
    grid = Grid(lax.axis_size("expert"))
    count = grid.count
    experts = w_router.shape[1]
    capacity = SEQ * TOP * 9 // (8 * experts)
    scale = 1.0 / math.sqrt(HD)
    low = jnp.bfloat16
    own_rows, width = w_query.shape
    heads_here = width // HD
    core = lax.axis_index("tensor")

    small = jnp.concatenate(
        [
            w_router.astype(low).T,
            jnp.pad(
                jnp.stack(
                    [
                        attn_gain.astype(low),
                        ffn_gain.astype(low),
                        jnp.pad(query_gain.astype(low), (0, own_rows - HD // count)),
                        jnp.pad(key_gain.astype(low), (0, own_rows - HD // count)),
                    ]
                ),
                ((0, experts - 4), (0, 0)),
            ),
        ],
        axis=1,
    )
    small = jnp.pad(small, ((0, 0), (0, width - 2 * own_rows)))
    mine = [w_query.astype(low), w_key.astype(low), w_value.astype(low), w_out.astype(low), small]
    halves = [w_gate[0].astype(low), w_up[0].astype(low), w_down[0].astype(low)]
    allowed = jnp.arange(SEQ) < lengths[0]
    grad_two_low = jnp.where(allowed[:, None], cotangent, 0)
    if grid.side == 2:
        wq_full, wk_full, wv_full, wo_full, smalls, grad_blocks, *others = gather_all(
            mine, grad_two_low, halves, count
        )
    else:
        whole = jnp.concatenate(mine, axis=0)
        arrived = []
        for top in range(PLANES):
            base = whole if top == 0 else grid.send(whole, (top * grid.plane,) * CORES)
            arrived += spread(grid, base)
        wq_full, wk_full, wv_full, wo_full, smalls = assemble(grid, arrived, own_rows, experts)
    router_t = smalls[:, :, :own_rows].transpose(1, 0, 2).reshape(experts, D)
    gain_one = smalls[:, 0, own_rows : 2 * own_rows].reshape(D).astype(jnp.float32)
    gain_two = smalls[:, 1, own_rows : 2 * own_rows].reshape(D).astype(jnp.float32)
    head_cols = slice(own_rows, own_rows + HD // count)
    gain_query = smalls[:, 2, head_cols].reshape(HD).astype(jnp.float32)
    gain_key = smalls[:, 3, head_cols].reshape(HD).astype(jnp.float32)

    grad_two = grad_two_low.astype(jnp.float32)

    cosine, sine_tab = rope_tables(SEQ, HD)
    resid_zero = tokens.astype(jnp.float32)
    normed_one, inverse_one = norm_stats(resid_zero)
    attn_in = (normed_one * gain_one).astype(low)
    query_lin = jnp.dot(attn_in, wq_full, preferred_element_type=jnp.float32).reshape(
        SEQ, heads_here, HD
    )
    key_lin = jnp.dot(attn_in, wk_full, preferred_element_type=jnp.float32).reshape(
        SEQ, heads_here, HD
    )
    values_b = (
        jnp.dot(attn_in, wv_full, preferred_element_type=jnp.float32)
        .astype(low)
        .reshape(SEQ, heads_here, HD)
    )
    query_hat, query_inv = norm_stats(query_lin)
    key_hat, key_inv = norm_stats(key_lin)
    queries = rotate(query_hat * gain_query, cosine, sine_tab).astype(low)
    keys_rot = rotate(key_hat * gain_key, cosine, sine_tab).astype(low)

    def masked_scores():
        scores = (
            jnp.einsum("qhd,khd->hqk", queries, keys_rot, preferred_element_type=jnp.float32)
            * scale
        )
        return jnp.where(allowed[None, None, :], scores, NEG_BIG)

    masked = masked_scores()
    top_score = jnp.max(masked, axis=-1, keepdims=True)
    expo_vals = jnp.exp(masked - top_score)
    totals = jnp.sum(expo_vals, axis=-1, keepdims=True)
    probs_low = (expo_vals / totals).astype(low)
    log_total = top_score + jnp.log(totals)
    mixed = (
        jnp.einsum("hqk,khd->qhd", probs_low, values_b, preferred_element_type=jnp.float32)
        .reshape(SEQ, heads_here * HD)
        .astype(low)
    )
    attn_part = contract_cols(mixed, wo_full)
    resid_one = resid_zero + (attn_part + swap(attn_part))
    normed_two, inverse_two = norm_stats(resid_one)
    ffn_in = (normed_two * gain_two).astype(low)
    logits = contract_cols(ffn_in, router_t)
    route_hot = routes[:, :, None] == jnp.arange(experts)[None, None, :]
    chosen = jnp.sum(jnp.where(route_hot, logits[:, None, :], 0.0), axis=2)
    gates = jax.nn.softmax(chosen, axis=1)
    gates_wide = jnp.sum(jnp.where(route_hot, gates[:, :, None], 0.0), axis=1)

    gate_rows = jnp.pad(split_three(gates_wide.T), ((0, 0), (0, D - 3 * SEQ)))
    token_block = jnp.concatenate([ffn_in, gate_rows], axis=0)
    if grid.side == 2:
        done = moe_layer(token_block, grad_blocks, halves + others, capacity)
        saved = [tuple(done[12:17])]
        out_turns = [done[:4], done[4:8]]
        back_sum = both_cores(done[17])
    else:
        wg, wu, wd = (
            jnp.concatenate([half, swap(half)], axis=axis) for half, axis in zip(halves, (1, 1, 0))
        )
        grad_turns = gather_tokens(grid, grad_two_low)
        token_turns = gather_tokens(grid, token_block)
        out_turns, back_turns, saved = [], [], []
        for turn in range(2):
            outs, backs, kept = expert_turn(
                token_turns[turn], grad_turns[turn], (wg, wu, wd), capacity
            )
            out_turns.append(outs)
            back_turns.append(backs)
            saved.append(kept)
        back_sum = scatter_tokens(grid, back_turns)
    out_sum = scatter_tokens(grid, out_turns)
    output = (resid_one + out_sum).astype(low)

    def over_turns(left, right):
        return sum(contract_rows(kept[left], kept[right]) for kept in saved)

    half = w_gate.shape[2]
    gate_w = over_turns(0, 3)
    up_w = over_turns(0, 4)
    down_w = over_turns(2, 1)

    grad_gates_wide = join_three(back_sum[SEQ:], SEQ).T
    grad_gate_sel = jnp.sum(jnp.where(route_hot, grad_gates_wide[:, None, :], 0.0), axis=2)
    grad_chosen = gates * (grad_gate_sel - jnp.sum(gates * grad_gate_sel, axis=1, keepdims=True))
    grad_logits = jnp.sum(jnp.where(route_hot, grad_chosen[:, :, None], 0.0), axis=1).astype(low)
    grad_router_t = contract_rows(grad_logits, ffn_in)
    grad_ffn_in = back_sum[:SEQ] + jnp.dot(
        grad_logits, router_t, preferred_element_type=jnp.float32
    )
    grad_gain_two = jnp.sum(grad_ffn_in * normed_two, axis=0)
    grad_one = grad_two + norm_back(grad_ffn_in * gain_two, normed_two, inverse_two)
    grad_attn = grad_one.astype(low)

    part_wo = contract_rows(grad_attn, mixed)
    grad_mixed = (
        jnp.dot(grad_attn, wo_full, preferred_element_type=jnp.float32)
        .astype(low)
        .reshape(SEQ, heads_here, HD)
    )
    masked = masked_scores()
    attn_probs = jnp.exp(masked - log_total)
    probs_again = attn_probs.astype(low)
    grad_probs = jnp.einsum(
        "qhd,khd->hqk", grad_mixed, values_b, preferred_element_type=jnp.float32
    )
    grad_values = jnp.einsum(
        "hqk,qhd->khd", probs_again, grad_mixed, preferred_element_type=jnp.float32
    )
    grad_value_lin = grad_values.astype(low).reshape(SEQ, heads_here * HD)
    part_wv = contract_rows(attn_in, grad_value_lin)
    grad_scores = (
        attn_probs * (grad_probs - jnp.sum(attn_probs * grad_probs, axis=-1, keepdims=True))
    ).astype(low)
    grad_queries = (
        jnp.einsum("hqk,khd->qhd", grad_scores, keys_rot, preferred_element_type=jnp.float32)
        * scale
    )
    grad_keys = (
        jnp.einsum("hqk,qhd->khd", grad_scores, queries, preferred_element_type=jnp.float32) * scale
    )
    grad_query_scaled = rotate_back(grad_queries, cosine, sine_tab)
    grad_key_scaled = rotate_back(grad_keys, cosine, sine_tab)
    grad_gain_query = jnp.sum(grad_query_scaled * query_hat, axis=(0, 1))
    grad_gain_key = jnp.sum(grad_key_scaled * key_hat, axis=(0, 1))
    grad_query_lin = (
        norm_back(grad_query_scaled * gain_query, query_hat, query_inv)
        .astype(low)
        .reshape(SEQ, heads_here * HD)
    )
    grad_key_lin = (
        norm_back(grad_key_scaled * gain_key, key_hat, key_inv)
        .astype(low)
        .reshape(SEQ, heads_here * HD)
    )
    part_wq = contract_rows(attn_in, grad_query_lin)
    part_wk = contract_rows(attn_in, grad_key_lin)
    grad_attn_part = (
        contract_cols(grad_query_lin, wq_full)
        + contract_cols(grad_key_lin, wk_full)
        + contract_cols(grad_value_lin, wv_full)
    ).astype(low)
    grad_attn_in = grad_attn_part.astype(jnp.float32) + swap(grad_attn_part).astype(jnp.float32)
    grad_gain_one = jnp.sum(grad_attn_in * normed_one, axis=0)
    grad_input = grad_one + norm_back(grad_attn_in * gain_one, normed_one, inverse_one)

    head_part = HD // count
    heads_row = jnp.stack([grad_gain_query, grad_gain_key]).reshape(2, count, head_part)
    heads_row = jnp.pad(heads_row, ((0, 0), (0, 0), (0, own_rows - head_part)))
    parts = jnp.concatenate(
        [
            jnp.concatenate([grad_router_t, grad_gain_one[None], grad_gain_two[None]]).reshape(
                experts + 2, count, own_rows
            ),
            heads_row,
        ],
        axis=0,
    ).transpose(1, 0, 2)
    weight_parts = [part_wq, part_wk, part_wv, part_wo]
    if grid.side == 2:
        weight_parts = [part.astype(low) for part in weight_parts]
        parts = jnp.pad(parts, ((0, 0), (0, 4), (0, 0)))
        grad_wq, grad_wk, grad_wv, grad_wo, sums, *received = reduce_all(
            weight_parts, parts, [gate_w, up_w, down_w], count
        )
    else:
        shape = (PLANES, grid.side, grid.side)
        grad_wq, grad_wk, grad_wv, grad_wo = [
            scatter_rows(grid, part.reshape(shape + (own_rows, width)), axes, low)
            for part, axes in zip(weight_parts, ((1, 2, 0), (2, 1, 0)) * 2)
        ]
        sums = scatter_rows(
            grid, parts.reshape(shape + (experts + 4, own_rows)), (1, 2, 0), jnp.float32
        )
        sums = sums + swap(sums)
        received = [swap(part) for part in (gate_w[:, half:], up_w[:, half:], down_w[half:])]
    grad_gate_w = (gate_w[:, :half] + received[0])[None]
    grad_up_w = (up_w[:, :half] + received[1])[None]
    grad_down_w = (down_w[:half] + received[2])[None]
    return (
        output,
        grad_input.astype(low),
        0.5 * sums[experts],
        grad_wq,
        grad_wk,
        grad_wv,
        sums[experts + 2, :head_part],
        sums[experts + 3, :head_part],
        grad_wo,
        0.5 * sums[experts + 1],
        0.5 * sums[:experts].T,
        grad_gate_w,
        grad_up_w,
        grad_down_w,
    )


def solution(mesh):
    return jax.shard_map(
        local,
        mesh=mesh,
        in_specs=(
            P("expert", None),
            P("expert"),
            P("expert", None),
            P("expert"),
            P("expert", "tensor"),
            P("expert", "tensor"),
            P("expert", "tensor"),
            P("expert"),
            P("expert"),
            P("expert", "tensor"),
            P("expert"),
            P("expert", None),
            P("expert", None, "tensor"),
            P("expert", None, "tensor"),
            P("expert", "tensor", None),
            P("expert", None),
        ),
        out_specs=(
            P("expert", None),
            P("expert", None),
            P("expert"),
            P("expert", "tensor"),
            P("expert", "tensor"),
            P("expert", "tensor"),
            P("expert"),
            P("expert"),
            P("expert", "tensor"),
            P("expert"),
            P("expert", None),
            P("expert", None, "tensor"),
            P("expert", None, "tensor"),
            P("expert", "tensor", None),
        ),
        check_vma=False,
    )
```

```python
import functools
import math

import jax
import jax.numpy as jnp
from jax import lax
from jax.experimental import pallas as pl
from jax.experimental.pallas import tpu as pltpu
from jax.sharding import PartitionSpec as P

D = 2048
HD = 128
TOP = 8
SEQ = 512


EPSILON = 1e-06
ROPE_BASE = 10000.0
NEG_BIG = -1e30


def rope_tables(seq_len, head_dim):
    half_dim = head_dim // 2
    inverse = ROPE_BASE ** (-(jnp.arange(half_dim).astype(jnp.float32) * 2.0 / head_dim))
    angles = jnp.arange(seq_len).astype(jnp.float32)[:, None] * inverse[None, :]
    return (jnp.cos(angles), jnp.sin(angles))


def rotate(values, cosine, sine_tab):
    half_dim = values.shape[-1] // 2
    lower_half = values[..., :half_dim]
    upper_half = values[..., half_dim:]
    cos_b = cosine[:, None, :]
    sin_b = sine_tab[:, None, :]
    return jnp.concatenate(
        [lower_half * cos_b - upper_half * sin_b, upper_half * cos_b + lower_half * sin_b], axis=-1
    )


def rotate_back(grads_in, cosine, sine_tab):
    half_dim = grads_in.shape[-1] // 2
    lower_half = grads_in[..., :half_dim]
    upper_half = grads_in[..., half_dim:]
    cos_b = cosine[:, None, :]
    sin_b = sine_tab[:, None, :]
    return jnp.concatenate(
        [lower_half * cos_b + upper_half * sin_b, upper_half * cos_b - lower_half * sin_b], axis=-1
    )


def norm_stats(values):
    inverse = lax.rsqrt(jnp.mean(values * values, axis=-1, keepdims=True) + EPSILON)
    return (values * inverse, inverse)


def norm_back(grad_normed, normed, inverse):
    return inverse * (grad_normed - normed * jnp.mean(grad_normed * normed, axis=-1, keepdims=True))


def contract_rows(left_mat, right_mat):
    return lax.dot_general(
        left_mat, right_mat, (((0,), (0,)), ((), ())), preferred_element_type=jnp.float32
    )


def contract_cols(left_mat, right_mat):
    return lax.dot_general(
        left_mat, right_mat, (((1,), (1,)), ((), ())), preferred_element_type=jnp.float32
    )


PLANES = 4
CORES = 2


class Grid:
    def __init__(self, count):
        self.count = count
        self.plane = count // PLANES
        self.side = math.isqrt(self.plane)
        self.near = range(1, self.side)

    def first(self, step):
        return (step, step * self.side)

    def second(self, step):
        return (step * self.side, step)

    def planes_of(self, turn):
        return ((0, 3)[turn] * self.plane, (1, 2)[turn] * self.plane)

    def send(self, value, masks):
        pairs = [
            (device * CORES + core, (device ^ masks[core]) * CORES + core)
            for device in range(self.count)
            for core in range(CORES)
        ]
        return lax.ppermute(value, ("expert", "tensor"), pairs)


def swap(value):
    return lax.ppermute(value, "tensor", [(0, 1), (1, 0)])


def both_cores(part):
    return part.astype(jnp.float32) + swap(part).astype(jnp.float32)


def spread(grid, base):
    row = [base] + [grid.send(base, grid.first(step)) for step in grid.near]
    blocks = list(row)
    for step in grid.near:
        blocks += [grid.send(block, grid.second(step)) for block in row]
    return blocks


def gather_tokens(grid, block):
    return [spread(grid, grid.send(block, grid.planes_of(turn))) for turn in range(2)]


def collect(grid, blocks):
    side = grid.side
    sums = [block.astype(jnp.float32) for block in blocks[:side]]
    for far in grid.near:
        for step in range(side):
            sums[step] = sums[step] + grid.send(
                blocks[far * side + step], grid.second(far)
            ).astype(jnp.float32)
    total = sums[0]
    for step in grid.near:
        total = total + grid.send(sums[step].astype(jnp.bfloat16), grid.first(step)).astype(
            jnp.float32
        )
    return total


def scatter_tokens(grid, turns):
    total = None
    for turn in (1, 0):
        part = grid.send(collect(grid, turns[turn]).astype(jnp.bfloat16), grid.planes_of(turn))
        part = part.astype(jnp.float32)
        total = part if total is None else total + part
    return both_cores(total.astype(jnp.bfloat16))


def scatter_rows(grid, value, axes, wire):
    me = lax.axis_index("expert")
    units = (grid.plane, grid.side, 1)
    sizes = (PLANES, grid.side, grid.side)
    gone = []
    for axis in axes:
        unit, size = units[axis], sizes[axis]
        place = (me // unit) % size
        at = axis - sum(1 for other in gone if other < axis)
        total = lax.dynamic_index_in_dim(value, place, at, keepdims=False).astype(jnp.float32)
        for step in range(1, size):
            part = lax.dynamic_index_in_dim(value, place ^ step, at, keepdims=False).astype(wire)
            total = total + grid.send(part, (unit * step,) * CORES).astype(jnp.float32)
        value = total
        gone.append(axis)
    return value


def assemble(grid, blocks, rows, extra):
    count, width = grid.count, blocks[0].shape[1]
    me = lax.axis_index("expert")
    core = lax.axis_index("tensor")
    place = jnp.arange(count)
    top, mid, low = place // grid.plane, (place // grid.side) % grid.side, place % grid.side
    turned = top * grid.plane + low * grid.side + mid
    owner = me ^ jnp.where(core == 0, place, turned)

    def body(owner_ref, *refs):
        ins, outs, small, sem = refs[:count], refs[count : count + 4], refs[count + 4], refs[-1]
        copies = []
        for index in range(count):
            at = owner_ref[index]
            for which in range(4):
                copies.append(
                    pltpu.make_async_copy(
                        ins[index].at[pl.ds(which * rows, rows)],
                        outs[which].at[pl.ds(pl.multiple_of(at * rows, rows), rows)],
                        sem.at[index, which],
                    )
                )
            copies.append(
                pltpu.make_async_copy(
                    ins[index].at[pl.ds(4 * rows, extra)], small.at[at], sem.at[index, 4]
                )
            )
        for copy in copies:
            copy.start()
        for copy in copies:
            copy.wait()

    full = jax.ShapeDtypeStruct((count * rows, width), jnp.bfloat16)
    small = jax.ShapeDtypeStruct((count, extra, width), jnp.bfloat16)
    return pl.pallas_call(
        body,
        grid_spec=pltpu.PrefetchScalarGridSpec(
            num_scalar_prefetch=1,
            grid=(),
            in_specs=[pl.BlockSpec(memory_space=pl.ANY)] * count,
            out_specs=[pl.BlockSpec(memory_space=pltpu.VMEM)] * 5,
            scratch_shapes=[pltpu.SemaphoreType.DMA((count, 5))],
        ),
        out_shape=[full] * 4 + [small],
        name="assemble",
    )(owner, *blocks)


class Place:
    def __init__(self):
        self.me = me = lax.axis_index("expert")
        self.core = core = lax.axis_index("tensor")
        top, mid, low = me // 4, (me // 2) % 2, me % 2
        flip_low = me + 1 - 2 * low
        flip_mid = me + 2 - 4 * mid
        self.first = flip_low + core * (flip_mid - flip_low)
        self.second = flip_mid + core * (flip_low - flip_mid)
        self.planes = (
            me,
            me + 4 - 8 * (top % 2),
            me + 8 - 16 * (top // 2),
            me + 12 - 8 * top,
        )

    def owner(self, plane, far, near):
        return self.planes[plane] + far * (self.second - self.me) + near * (self.first - self.me)

    def greet(self, sibling):
        barrier = pltpu.get_barrier_semaphore()
        partners = [(device, self.core) for device in (self.first, self.second) + self.planes[1:]]
        if sibling:
            partners.append((self.me, 1 - self.core))
        for partner in partners:
            pl.semaphore_signal(
                barrier, inc=1, device_id=partner, device_id_type=pl.DeviceIdType.MESH
            )
        pl.semaphore_wait(barrier, len(partners))


def remote(source, target, send, recv, device):
    return pltpu.make_async_remote_copy(
        src_ref=source,
        dst_ref=target,
        send_sem=send,
        recv_sem=recv,
        device_id=device,
        device_id_type=pl.DeviceIdType.MESH,
    )


def gather_kernel(rows, *refs):
    mine, grad, halves, refs = refs[:5], refs[5], refs[6:9], refs[9:]
    full, grads, others, refs = refs[:5], refs[5], refs[6:9], refs[9:]
    send_sem, recv_sem, grad_send, grad_recv, half_send, half_recv, own_sem = refs
    place = Place()
    core = place.core
    place.greet(True)

    def part(which, plane, far, near):
        owner = place.owner(plane, far, near)
        if which == 4:
            return full[4].at[owner]
        return full[which].at[pl.ds(pl.multiple_of(owner * rows, rows), rows)]

    def pass_weights(source, plane, slot, device):
        out = []
        for which in range(5):
            here = part(which, *source)
            out.append(
                remote(
                    mine[which] if source == (0, 0, 0) else here,
                    here,
                    send_sem.at[4 * plane + slot, which],
                    recv_sem.at[4 * plane + slot, which],
                    (device, core),
                )
            )
        return out

    def start(copies):
        for copy in copies:
            copy.start()

    def arrived(plane, slot):
        for copy in pass_weights((plane, slot // 2, slot % 2), plane, slot, place.first):
            copy.wait_recv()

    def pass_grad(source, slot, device):
        return remote(
            source, grads.at[slot], grad_send.at[slot], grad_recv.at[slot], (device, core)
        )

    for plane in (1, 2, 3):
        start(pass_weights((0, 0, 0), plane, 0, place.planes[plane]))
    start(pass_weights((0, 0, 0), 0, 1, place.first))
    start(pass_weights((0, 0, 0), 0, 2, place.second))
    far_plane = place.planes[3] + core * (place.planes[2] - place.planes[3])

    @pl.when(core == 1)
    def _():
        pass_grad(grad, 0, place.planes[1]).start()

    pass_grad(grad, 4, far_plane).start()
    swaps = [
        remote(halves[i], others[i], half_send.at[i], half_recv.at[i], (place.me, 1 - core))
        for i in range(3)
    ]
    start(swaps)
    keeps = [
        pltpu.make_async_copy(mine[which], part(which, 0, 0, 0), own_sem.at[which])
        for which in range(5)
    ]
    start(keeps)

    @pl.when(core == 0)
    def _():
        pltpu.make_async_copy(grad, grads.at[0], own_sem.at[5]).start()

    for plane in range(4):
        if plane > 0:
            arrived(plane, 0)
            start(pass_weights((plane, 0, 0), plane, 1, place.first))
            start(pass_weights((plane, 0, 0), plane, 2, place.second))
        arrived(plane, 1)
        start(pass_weights((plane, 0, 1), plane, 3, place.second))

    @pl.when(core == 0)
    def _():
        pass_grad(grad, 1, place.first).start()
        pass_grad(grad, 2, place.second).start()

    @pl.when(core == 1)
    def _():
        pass_grad(grads.at[0], 0, place.first).wait_recv()
        pass_grad(grads.at[0], 1, place.first).start()
        pass_grad(grads.at[0], 2, place.second).start()

    pass_grad(grads.at[1], 1, place.first).wait_recv()
    pass_grad(grads.at[1], 3, place.second).start()
    pass_grad(grads.at[4], 4, place.first).wait_recv()
    pass_grad(grads.at[4], 5, place.first).start()
    pass_grad(grads.at[4], 6, place.second).start()
    pass_grad(grads.at[5], 5, place.first).wait_recv()
    pass_grad(grads.at[5], 7, place.second).start()

    for plane in range(4):
        arrived(plane, 2)
        arrived(plane, 3)
    for slot in (2, 3, 6, 7):
        pass_grad(grads.at[slot], slot, place.first).wait_recv()
    for slot in range(1, 16):
        for copy in pass_weights((slot // 4, 0, 0), slot // 4, slot % 4, place.first):
            copy.wait_send()
    for slot in range(1, 8):
        pass_grad(grads.at[slot], slot, place.first).wait_send()

    @pl.when(core == 1)
    def _():
        pass_grad(grads.at[0], 0, place.first).wait_send()

    @pl.when(core == 0)
    def _():
        pltpu.make_async_copy(grad, grads.at[0], own_sem.at[5]).wait()

    for copy in swaps + keeps:
        copy.wait()


def gather_all(mine, grad, halves, count):
    rows, width = mine[0].shape
    extra = mine[4].shape[0]
    low = jnp.bfloat16
    hbm = pl.BlockSpec(memory_space=pl.ANY)
    full = jax.ShapeDtypeStruct((count * rows, width), low)
    return pl.pallas_call(
        functools.partial(gather_kernel, rows),
        in_specs=[hbm] * 9,
        out_specs=[hbm] * 9,
        out_shape=[full] * 4
        + [
            jax.ShapeDtypeStruct((count, extra, width), low),
            jax.ShapeDtypeStruct((8,) + grad.shape, low),
        ]
        + [jax.ShapeDtypeStruct(half.shape, low) for half in halves],
        scratch_shapes=[
            pltpu.SemaphoreType.DMA((16, 5)),
            pltpu.SemaphoreType.DMA((16, 5)),
            pltpu.SemaphoreType.DMA((8,)),
            pltpu.SemaphoreType.DMA((8,)),
            pltpu.SemaphoreType.DMA((3,)),
            pltpu.SemaphoreType.DMA((3,)),
            pltpu.SemaphoreType.DMA((6,)),
        ],
        compiler_params=pltpu.CompilerParams(collective_id=1, has_side_effects=True),
        name="gather_all",
    )(*mine, grad, *halves)


def reduce_kernel(rows, *refs):
    whole, small, halves, refs = refs[:4], refs[4], refs[5:8], refs[8:]
    out, small_out, others, refs = refs[:4], refs[4], refs[5:8], refs[8:]
    (
        own,
        far_in,
        near_in,
        plane_in,
        near_stage,
        plane_stage,
        small_own,
        small_far,
        small_near,
        small_plane,
        small_near_stage,
        small_plane_stage,
        small_last,
        small_other,
        load_sem,
        far_send,
        far_recv,
        near_send,
        near_recv,
        plane_send,
        plane_recv,
        half_send,
        half_recv,
        last_send,
        last_recv,
    ) = refs
    place = Place()
    core = place.core
    sibling = (place.me, 1 - core)
    place.greet(True)
    second, first = (place.second, core), (place.first, core)

    def source(which, plane, far, near):
        owner = place.owner(plane, far, near)
        if which == 4:
            return small.at[owner]
        return whole[which].at[pl.ds(pl.multiple_of(owner * rows, rows), rows)]

    def load(which, plane, near):
        target = small_own.at[2 * plane + near] if which == 4 else own.at[2 * plane + near, which]
        return pltpu.make_async_copy(
            source(which, plane, 0, near), target, load_sem.at[2 * plane + near, which]
        )

    def to_second(which, plane, near):
        target = small_far.at[2 * plane + near]
        if which != 4:
            target = far_in.at[2 * plane + near, which]
        return remote(
            source(which, plane, 1, near),
            target,
            far_send.at[2 * plane + near, which],
            far_recv.at[2 * plane + near, which],
            second,
        )

    def to_first(which, plane):
        here, there = small_near_stage.at[plane], small_near.at[plane]
        if which is not None:
            here, there = near_stage.at[plane, which], near_in.at[plane, which]
        at = 4 if which is None else which
        return remote(here, there, near_send.at[plane, at], near_recv.at[plane, at], first)

    def to_plane(which, plane):
        here, there = small_plane_stage.at[plane - 1], small_plane.at[plane - 1]
        if which is not None:
            here, there = plane_stage.at[plane - 1, which], plane_in.at[plane - 1, which]
        at = 4 if which is None else which
        return remote(
            here,
            there,
            plane_send.at[plane - 1, at],
            plane_recv.at[plane - 1, at],
            (place.planes[plane], core),
        )

    for plane in (3, 2, 1, 0):
        for near in (1, 0):
            for which in range(5):
                to_second(which, plane, near).start()
    for plane in (3, 2, 1, 0):
        for near in (1, 0):
            for which in range(5):
                load(which, plane, near).start()
    middle = others[0].shape[1]
    theirs = [
        halves[0].at[:, pl.ds(middle, middle)],
        halves[1].at[:, pl.ds(middle, middle)],
        halves[2].at[pl.ds(middle, middle)],
    ]
    swaps = [
        remote(theirs[i], others[i], half_send.at[i], half_recv.at[i], sibling) for i in range(3)
    ]
    for copy in swaps:
        copy.start()

    def added(parts, target):
        total = parts[0].astype(jnp.float32)
        for value in parts[1:]:
            total = total + value.astype(jnp.float32)
        return total.astype(target.dtype)

    def over_rows(parts, target):
        def body(step, carry):
            span = pl.ds(pl.multiple_of(step * 16, 16), 16)
            target[span, :] = added([part[span, :] for part in parts], target)
            return carry

        lax.fori_loop(0, rows // 16, body, 0)

    def near_sums(plane):
        for which in range(4):
            load(which, plane, 1).wait()
            to_second(which, plane, 1).wait_recv()
            over_rows(
                [own.at[2 * plane + 1, which], far_in.at[2 * plane + 1, which]],
                near_stage.at[plane, which],
            )
            to_first(which, plane).start()
        load(4, plane, 1).wait()
        to_second(4, plane, 1).wait_recv()
        small_near_stage[plane] = small_own[2 * plane + 1] + small_far[2 * plane + 1]
        to_first(None, plane).start()

    def plane_sums(plane):
        for which in range(4):
            load(which, plane, 0).wait()
            to_second(which, plane, 0).wait_recv()
            to_first(which, plane).wait_recv()
            over_rows(
                [
                    own.at[2 * plane, which],
                    far_in.at[2 * plane, which],
                    near_in.at[plane, which],
                ],
                plane_stage.at[plane - 1, which],
            )
            to_plane(which, plane).start()
        load(4, plane, 0).wait()
        to_second(4, plane, 0).wait_recv()
        to_first(None, plane).wait_recv()
        small_plane_stage[plane - 1] = (
            small_own[2 * plane] + small_far[2 * plane] + small_near[plane]
        )
        to_plane(None, plane).start()

    near_sums(3)
    near_sums(2)
    plane_sums(3)
    near_sums(1)
    plane_sums(2)
    near_sums(0)
    plane_sums(1)
    load(4, 0, 0).wait()
    to_second(4, 0, 0).wait_recv()
    to_first(None, 0).wait_recv()
    for plane in (1, 2, 3):
        to_plane(None, plane).wait_recv()
    small_last[...] = (
        small_own[0]
        + small_far[0]
        + small_near[0]
        + small_plane[0]
        + small_plane[1]
        + small_plane[2]
    )
    last = remote(small_last, small_other, last_send.at[0], last_recv.at[0], sibling)
    last.start()
    for which in range(4):
        load(which, 0, 0).wait()
        to_second(which, 0, 0).wait_recv()
        to_first(which, 0).wait_recv()
        for plane in (1, 2, 3):
            to_plane(which, plane).wait_recv()
        over_rows(
            [own.at[0, which], far_in.at[0, which], near_in.at[0, which]]
            + [plane_in.at[plane, which] for plane in range(3)],
            out[which],
        )
    last.wait()
    small_out[...] = small_last[...] + small_other[...]
    for plane in range(4):
        for which in range(5):
            at = None if which == 4 else which
            for near in range(2):
                to_second(which, plane, near).wait_send()
            to_first(at, plane).wait_send()
            if plane > 0:
                to_plane(at, plane).wait_send()
    for copy in swaps:
        copy.wait()


def reduce_all(whole, small, halves, count):
    rows, width = whole[0].shape[0] // count, whole[0].shape[1]
    low = jnp.bfloat16
    hbm = pl.BlockSpec(memory_space=pl.ANY)
    vmem = pl.BlockSpec(memory_space=pltpu.VMEM)
    tiny = small.shape[1:]

    def wide(*dims):
        return pltpu.VMEM(dims + (rows, width), low)

    def little(*dims):
        return pltpu.VMEM(dims + tiny, jnp.float32)

    def sems(*dims):
        return pltpu.SemaphoreType.DMA(dims)

    return pl.pallas_call(
        functools.partial(reduce_kernel, rows),
        in_specs=[hbm] * 8,
        out_specs=[vmem] * 5 + [hbm] * 3,
        out_shape=[jax.ShapeDtypeStruct((rows, width), jnp.float32)] * 4
        + [jax.ShapeDtypeStruct(tiny, jnp.float32)]
        + [
            jax.ShapeDtypeStruct((dims[0] // cut, dims[1] // (3 - cut)), jnp.float32)
            for dims, cut in ((halves[0].shape, 1), (halves[1].shape, 1), (halves[2].shape, 2))
        ],
        scratch_shapes=[wide(8, 4), wide(8, 4), wide(4, 4), wide(3, 4), wide(4, 4), wide(3, 4)]
        + [little(8), little(8), little(4), little(3), little(4), little(3), little(), little()]
        + [sems(8, 5)] * 3
        + [sems(4, 5)] * 2
        + [sems(3, 5)] * 2
        + [sems(3)] * 2
        + [sems(1)] * 2,
        compiler_params=pltpu.CompilerParams(
            collective_id=2, has_side_effects=True, vmem_limit_bytes=60 * 1024 * 1024
        ),
        name="reduce_all",
    )(*whole, small, *halves)


def split_three(value):
    high = value.astype(jnp.bfloat16)
    rest = value - high.astype(jnp.float32)
    middle = rest.astype(jnp.bfloat16)
    low = (rest - middle.astype(jnp.float32)).astype(jnp.bfloat16)
    return jnp.concatenate([high, middle, low], axis=-1)


def join_three(parts, length):
    parts = parts.astype(jnp.float32)
    return (
        parts[..., :length] + parts[..., length : 2 * length] + parts[..., 2 * length : 3 * length]
    )


def expert_turn(blocks, grads, weights, capacity):
    wg, wu, wd = weights
    me = lax.axis_index("expert")
    experts = blocks[0].shape[0] - SEQ
    gate = jnp.concatenate(
        [
            join_three(lax.dynamic_slice(block, (SEQ + me, 0), (1, 3 * SEQ)), SEQ)
            for block in blocks
        ],
        axis=0,
    )
    used = gate > 0.0
    ordered = (jnp.arange(SEQ)[:, None] < jnp.arange(SEQ)[None, :]).astype(jnp.bfloat16)
    slot = jnp.dot(used.astype(jnp.bfloat16), ordered, preferred_element_type=jnp.float32)
    slot = slot.astype(jnp.int32)
    hot = (jnp.arange(capacity)[None, :, None] == slot[:, None, :]) & used[:, None, :]
    pick = hot.astype(jnp.bfloat16)
    slot_gate = jnp.sum(jnp.where(hot, gate[:, None, :], 0.0), axis=2).reshape(-1, 1)
    rows = jnp.concatenate(
        [
            jnp.dot(pick[i], block[:SEQ], preferred_element_type=jnp.float32).astype(jnp.bfloat16)
            for i, block in enumerate(blocks)
        ],
        axis=0,
    )
    grad_rows = jnp.concatenate(
        [
            jnp.dot(pick[i], block, preferred_element_type=jnp.float32).astype(jnp.bfloat16)
            for i, block in enumerate(grads)
        ],
        axis=0,
    )
    gate_lin = jnp.dot(rows, wg, preferred_element_type=jnp.float32)
    up_lin = jnp.dot(rows, wu, preferred_element_type=jnp.float32)
    grad_full = contract_cols(grad_rows, wd)
    sigmoid_gate = jax.nn.sigmoid(gate_lin)
    activated = gate_lin * sigmoid_gate
    hidden = activated * up_lin
    hidden_low = (hidden * slot_gate).astype(jnp.bfloat16)
    slot_grad = jnp.sum(hidden * grad_full, axis=1).reshape(len(blocks), capacity, 1)
    grad_hidden = grad_full * slot_gate
    silu_slope = sigmoid_gate * (1.0 + gate_lin * (1.0 - sigmoid_gate))
    grad_gate = (grad_hidden * up_lin * silu_slope).astype(jnp.bfloat16)
    grad_up = (grad_hidden * activated).astype(jnp.bfloat16)
    value = jnp.dot(hidden_low, wd, preferred_element_type=jnp.float32).astype(jnp.bfloat16)
    grad_in = (contract_cols(grad_gate, wg) + contract_cols(grad_up, wu)).astype(jnp.bfloat16)
    token_grad = split_three(jnp.sum(jnp.where(hot, slot_grad, 0.0), axis=1))
    outs, backs = [], []
    for i in range(len(blocks)):
        span = slice(i * capacity, (i + 1) * capacity)
        outs.append(contract_rows(pick[i], value[span]).astype(jnp.bfloat16))
        back = contract_rows(pick[i], grad_in[span]).astype(jnp.bfloat16)
        extra = jnp.where(
            (jnp.arange(experts) == me)[:, None],
            jnp.pad(token_grad[i : i + 1], ((0, 0), (0, D - 3 * SEQ))),
            0,
        )
        backs.append(jnp.concatenate([back, extra], axis=0))
    return outs, backs, (rows, grad_rows, hidden_low, grad_gate, grad_up)


def moe_kernel(
    capacity,
    experts,
    own,
    *refs,
):
    weights, grads, refs = refs[:6], refs[6], refs[7:]
    parts, refs = refs[:8], refs[8:]
    (
    blocks,
    far_sums,
    near_sums,
    plane_sums,
    rows_out,
    grows_out,
    hidden_out,
    gate_out,
    up_out,
    result,
    wg_v,
    wu_v,
    wd_v,
    block_v,
    grad_v,
    rows_v,
    grows_v,
    hidden_v,
    gate_v,
    up_v,
    pick_v,
    pick_t,
    ordered,
    stage,
    part_v,
    taken,
    weight_sem,
    load_sem,
    save_sem,
    send_sem,
    recv_sem,
    back_send,
    back_recv,
    piece_send,
    piece_recv,
    ) = refs
    me = lax.axis_index("expert")
    core = lax.axis_index("tensor")
    top, mid, low = me // 4, (me // 2) % 2, me % 2
    flip_low = me + 1 - 2 * low
    flip_mid = me + 2 - 4 * mid
    first = flip_low + core * (flip_mid - flip_low)
    second = flip_mid + core * (flip_low - flip_mid)
    plane_one = me + 4 - 8 * (top % 2)
    plane_two = me + 8 - 16 * (top // 2)
    plane_three = me + 12 - 8 * top
    far_plane = plane_three + core * (plane_two - plane_three)
    mesh = pl.DeviceIdType.MESH

    barrier = pltpu.get_barrier_semaphore()
    for device in (first, second, plane_one, plane_two, plane_three):
        pl.semaphore_signal(barrier, inc=1, device_id=(device, core), device_id_type=mesh)
    pl.semaphore_wait(barrier, 5)

    def pass_on(source, slot, device):
        return pltpu.make_async_remote_copy(
            src_ref=source,
            dst_ref=blocks.at[slot],
            send_sem=send_sem.at[slot],
            recv_sem=recv_sem.at[slot],
            device_id=(device, core),
            device_id_type=mesh,
        )

    def give(source, target, index, device):
        return pltpu.make_async_remote_copy(
            src_ref=source,
            dst_ref=target,
            send_sem=back_send.at[index],
            recv_sem=back_recv.at[index],
            device_id=(device, core),
            device_id_type=mesh,
        )

    half = wg_v.shape[1] // 2
    targets = []
    for span in (slice(0, half), slice(half, 2 * half)):
        targets += [wg_v.at[:, span], wu_v.at[:, span], wd_v.at[span]]
    loads = [
        pltpu.make_async_copy(source, target, weight_sem.at[index])
        for index, (source, target) in enumerate(zip(weights, targets))
    ]

    @pl.when(core == 0)
    def _():
        pass_on(own, 1, first).start()
        pass_on(own, 2, second).start()

    @pl.when(core == 1)
    def _():
        pass_on(own, 0, plane_one).start()

    pass_on(own, 4, far_plane).start()
    for copy in loads:
        copy.start()

    length = SEQ
    ordered[...] = jnp.where(
        lax.broadcasted_iota(jnp.int32, (length, length), 0)
        < lax.broadcasted_iota(jnp.int32, (length, length), 1),
        1.0,
        0.0,
    ).astype(jnp.bfloat16)
    width = block_v.shape[1]
    hidden = hidden_v.shape[1]
    both = (((1,), (1,)), ((), ()))

    def dot(left, right):
        return jnp.dot(left, right, preferred_element_type=jnp.float32)

    def dot_t(left, right):
        return lax.dot_general(left, right, both, preferred_element_type=jnp.float32)

    def add_block(slot, sources, start=0, size=length + experts):
        part = pl.ds(start, size)
        copies = [
            pltpu.make_async_copy(source.at[part], taken.at[index, part], load_sem.at[2 + index])
            for index, source in enumerate(sources)
        ]
        for copy in copies:
            copy.start()
        for copy in copies:
            copy.wait()

        def rows_of(step, carry):
            span = pl.ds(pl.multiple_of(start + step * 16, 16), 16)
            total = stage[slot, span, :].astype(jnp.float32)
            for index in range(len(sources)):
                total = total + taken[index, span, :].astype(jnp.float32)
            stage[slot, span, :] = total.astype(jnp.bfloat16)
            return carry

        lax.fori_loop(0, size // 16, rows_of, 0)

    pieces = 3
    size = (length + experts) // pieces

    def give_piece(source, target, kind, piece, device):
        part = pl.ds(piece * size, size)
        return pltpu.make_async_remote_copy(
            src_ref=source.at[part],
            dst_ref=target.at[part],
            send_sem=piece_send.at[kind, piece],
            recv_sem=piece_recv.at[kind, piece],
            device_id=(device, core),
            device_id_type=mesh,
        )

    def far_piece(which, piece):
        return give_piece(stage.at[6 + which], far_sums.at[2 + which], which, piece, second)

    def near_piece(piece):
        return give_piece(stage.at[5], near_sums.at[1], 2, piece, first)

    def plane_piece(piece):
        return give_piece(stage.at[4], plane_sums.at[1], 3, piece, far_plane)

    def first_sum(turn):
        give(far_sums.at[2 * turn + 1], far_sums.at[2 * turn + 1], 2 * turn + 1, second).wait_recv()
        add_block(4 * turn + 1, [far_sums.at[2 * turn + 1]])
        give(stage.at[4 * turn + 1], near_sums.at[turn], 4 + turn, first).start()

    def plane_sum(turn):
        give(far_sums.at[2 * turn], far_sums.at[2 * turn], 2 * turn, second).wait_recv()
        give(near_sums.at[turn], near_sums.at[turn], 4 + turn, first).wait_recv()
        add_block(4 * turn, [far_sums.at[2 * turn], near_sums.at[turn]])

    def block_step(k, carry):
        turn_at = k % 4
        relayed = jnp.logical_or(k != 0, core != 0)

        @pl.when(relayed)
        def _():
            pass_on(blocks.at[k], k, first).wait_recv()
            pltpu.make_async_copy(blocks.at[k], block_v, load_sem.at[0]).start()

        @pl.when(jnp.logical_not(relayed))
        def _():
            pltpu.make_async_copy(own, block_v, load_sem.at[0]).start()

        @pl.when(jnp.logical_and(relayed, turn_at == 0))
        def _():
            pass_on(blocks.at[k], k + 1, first).start()

        @pl.when(jnp.logical_and(relayed, turn_at < 2))
        def _():
            pass_on(blocks.at[k], k + 2, second).start()

        pltpu.make_async_copy(grads.at[k], grad_v, load_sem.at[1]).start()

        @pl.when(k == 0)
        def _():
            for copy in loads:
                copy.wait()

        pltpu.make_async_copy(blocks.at[k], block_v, load_sem.at[0]).wait()

        here = lax.broadcasted_iota(jnp.int32, (experts, 3 * length), 0) == me
        row = jnp.sum(
            jnp.where(here, block_v[length:, : 3 * length].astype(jnp.float32), 0.0),
            axis=0,
            keepdims=True,
        )
        gate = row[:, :length] + row[:, length : 2 * length] + row[:, 2 * length :]
        used = jnp.where(gate > 0.0, 1.0, 0.0)
        slot = dot(jnp.broadcast_to(used, (16, length)).astype(jnp.bfloat16), ordered[...])[:1]
        slot = jnp.where(gate > 0.0, slot, -1.0)
        number = lax.broadcasted_iota(jnp.int32, (capacity, length), 0).astype(jnp.float32)
        pick = jnp.where(number == slot, 1.0, 0.0)
        slot_gate = jnp.sum(pick * gate, axis=1, keepdims=True)
        pick_v[...] = pick.astype(jnp.bfloat16)
        pick_t[...] = pick.T.astype(jnp.bfloat16)
        for at in range(0, width, 512):
            span = slice(at, at + 512)
            rows_v[:, span] = dot(pick_v[...], block_v[:length, span]).astype(jnp.bfloat16)
        pltpu.make_async_copy(grads.at[k], grad_v, load_sem.at[1]).wait()
        for at in range(0, width, 512):
            span = slice(at, at + 512)
            grows_v[:, span] = dot(pick_v[...], grad_v[:, span]).astype(jnp.bfloat16)
        slot_grad = jnp.zeros((capacity, 1), jnp.float32)
        for at in range(0, hidden, 256):
            span = slice(at, at + 256)
            gate_lin = dot(rows_v[...], wg_v[:, span])
            up_lin = dot(rows_v[...], wu_v[:, span])
            grad_full = dot_t(grows_v[...], wd_v[span, :])
            sigmoid_gate = 1.0 / (1.0 + jnp.exp(-gate_lin))
            activated = gate_lin * sigmoid_gate
            value = activated * up_lin
            hidden_v[:, span] = (value * slot_gate).astype(jnp.bfloat16)
            slot_grad = slot_grad + jnp.sum(value * grad_full, axis=1, keepdims=True)
            grad_hidden = grad_full * slot_gate
            slope = sigmoid_gate * (1.0 + gate_lin * (1.0 - sigmoid_gate))
            gate_v[:, span] = (grad_hidden * up_lin * slope).astype(jnp.bfloat16)
            up_v[:, span] = (grad_hidden * activated).astype(jnp.bfloat16)
        at = pl.multiple_of(k * capacity, capacity)
        saves = [
            pltpu.make_async_copy(source, target.at[pl.ds(at, capacity)], save_sem.at[index])
            for index, (source, target) in enumerate(
                (
                    (rows_v, rows_out),
                    (grows_v, grows_out),
                    (hidden_v, hidden_out),
                    (gate_v, gate_out),
                    (up_v, up_out),
                )
            )
        ]
        for copy in saves:
            copy.start()

        @pl.when(k > 0)
        def _():
            pltpu.make_async_copy(part_v, parts[0], save_sem.at[5]).wait()

        for at in range(0, width, 512):
            span = slice(at, at + 512)
            value = dot(hidden_v[...], wd_v[:, span]).astype(jnp.bfloat16)
            part_v[:, span] = dot(pick_t[...], value).astype(jnp.bfloat16)
            back = dot_t(gate_v[...], wg_v[span, :]) + dot_t(up_v[...], wu_v[span, :])
            stage[k, :length, span] = dot(pick_t[...], back.astype(jnp.bfloat16)).astype(
                jnp.bfloat16
            )
        total = jnp.sum(pick_v[...].astype(jnp.float32) * slot_grad, axis=0, keepdims=True)
        here = lax.broadcasted_iota(jnp.int32, (experts, length), 0) == me
        for index in range(3):
            high = total.astype(jnp.bfloat16).astype(jnp.float32)
            stage[k, length:, index * length : (index + 1) * length] = jnp.where(
                here, high, 0.0
            ).astype(jnp.bfloat16)
            total = total - high
        stage[k, length:, 3 * length :] = jnp.zeros((experts, width - 3 * length), jnp.bfloat16)
        for index in range(8):

            @pl.when(k == index)
            def _():
                pltpu.make_async_copy(part_v, parts[index], save_sem.at[5]).start()

        @pl.when(jnp.logical_and(turn_at >= 2, k < 4))
        def _():
            index = turn_at - 2
            give(stage.at[k], far_sums.at[index], index, second).start()

        for which in range(2):

            @pl.when(k == 6 + which)
            def _():
                for piece in range(pieces):
                    far_piece(which, piece).start()

        @pl.when(k == 5)
        def _():
            first_sum(0)

        @pl.when(k == 6)
        def _():
            plane_sum(0)

            @pl.when(core == 1)
            def _():
                give(stage.at[0], plane_sums.at[0], 6, plane_one).start()

        for copy in saves:
            copy.wait()
        return carry

    lax.fori_loop(0, 8, block_step, 0)
    for piece in range(pieces):
        far_piece(1, piece).wait_recv()
        add_block(5, [far_sums.at[3]], piece * size, size)
        near_piece(piece).start()
    for piece in range(pieces):
        far_piece(0, piece).wait_recv()
        near_piece(piece).wait_recv()
        add_block(4, [far_sums.at[2], near_sums.at[1]], piece * size, size)
        plane_piece(piece).start()

    @pl.when(core == 1)
    def _():
        give(stage.at[0], plane_sums.at[0], 6, plane_one).wait()
        pltpu.make_async_copy(plane_sums.at[0], stage.at[0], load_sem.at[0]).start()
        pltpu.make_async_copy(plane_sums.at[0], stage.at[0], load_sem.at[0]).wait()

    for piece in range(pieces):
        plane_piece(piece).wait_recv()
        add_block(0, [plane_sums.at[1]], piece * size, size)
    final = pltpu.make_async_copy(stage.at[0], result, load_sem.at[0])
    final.start()
    pltpu.make_async_copy(part_v, parts[7], save_sem.at[5]).wait()
    for k in range(8):
        if k > 0:
            pass_on(blocks.at[k], k, first).wait_send()
    @pl.when(core == 1)
    def _():
        pass_on(blocks.at[0], 0, first).wait_send()

    for index in (0, 1, 4):
        give(result, result, index, first).wait_send()
    for piece in range(pieces):
        for which in range(2):
            far_piece(which, piece).wait_send()
        near_piece(piece).wait_send()
        plane_piece(piece).wait_send()
    final.wait()


def moe_layer(own, grads, weights, capacity):
    rows, width = own.shape
    hidden = 2 * weights[0].shape[1]
    experts = rows - SEQ
    low = jnp.bfloat16
    hbm = pl.BlockSpec(memory_space=pl.ANY)

    def shape(*dims):
        return jax.ShapeDtypeStruct(dims, low)

    return pl.pallas_call(
        functools.partial(moe_kernel, capacity, experts),
        in_specs=[hbm] * 8,
        out_specs=[hbm] * 18,
        out_shape=[shape(SEQ, width)] * 8
        + [
            shape(8, rows, width),
            shape(4, rows, width),
            shape(2, rows, width),
            shape(2, rows, width),
            shape(8 * capacity, width),
            shape(8 * capacity, width),
            shape(8 * capacity, hidden),
            shape(8 * capacity, hidden),
            shape(8 * capacity, hidden),
            shape(rows, width),
        ],
        scratch_shapes=[
            pltpu.VMEM((width, hidden), low),
            pltpu.VMEM((width, hidden), low),
            pltpu.VMEM((hidden, width), low),
            pltpu.VMEM((rows, width), low),
            pltpu.VMEM((SEQ, width), low),
            pltpu.VMEM((capacity, width), low),
            pltpu.VMEM((capacity, width), low),
            pltpu.VMEM((capacity, hidden), low),
            pltpu.VMEM((capacity, hidden), low),
            pltpu.VMEM((capacity, hidden), low),
            pltpu.VMEM((capacity, SEQ), low),
            pltpu.VMEM((SEQ, capacity), low),
            pltpu.VMEM((SEQ, SEQ), low),
            pltpu.VMEM((8, rows, width), low),
            pltpu.VMEM((SEQ, width), low),
            pltpu.VMEM((2, rows, width), low),
            pltpu.SemaphoreType.DMA((6,)),
            pltpu.SemaphoreType.DMA((4,)),
            pltpu.SemaphoreType.DMA((6,)),
            pltpu.SemaphoreType.DMA((8,)),
            pltpu.SemaphoreType.DMA((8,)),
            pltpu.SemaphoreType.DMA((8,)),
            pltpu.SemaphoreType.DMA((8,)),
            pltpu.SemaphoreType.DMA((4, 3)),
            pltpu.SemaphoreType.DMA((4, 3)),
        ],
        compiler_params=pltpu.CompilerParams(
            collective_id=0, has_side_effects=True, vmem_limit_bytes=67043328
        ),
        name="moe_layer",
    )(own, *weights, grads)


def local(
    tokens,
    lengths,
    routes,
    attn_gain,
    w_query,
    w_key,
    w_value,
    query_gain,
    key_gain,
    w_out,
    ffn_gain,
    w_router,
    w_gate,
    w_up,
    w_down,
    cotangent,
):
    grid = Grid(lax.axis_size("expert"))
    count = grid.count
    experts = w_router.shape[1]
    capacity = SEQ * TOP * 9 // (8 * experts)
    scale = 1.0 / math.sqrt(HD)
    low = jnp.bfloat16
    own_rows, width = w_query.shape
    heads_here = width // HD
    core = lax.axis_index("tensor")

    small = jnp.concatenate(
        [
            w_router.astype(low).T,
            jnp.pad(
                jnp.stack(
                    [
                        attn_gain.astype(low),
                        ffn_gain.astype(low),
                        jnp.pad(query_gain.astype(low), (0, own_rows - HD // count)),
                        jnp.pad(key_gain.astype(low), (0, own_rows - HD // count)),
                    ]
                ),
                ((0, experts - 4), (0, 0)),
            ),
        ],
        axis=1,
    )
    small = jnp.pad(small, ((0, 0), (0, width - 2 * own_rows)))
    mine = [w_query.astype(low), w_key.astype(low), w_value.astype(low), w_out.astype(low), small]
    halves = [w_gate[0].astype(low), w_up[0].astype(low), w_down[0].astype(low)]
    allowed = jnp.arange(SEQ) < lengths[0]
    grad_two_low = jnp.where(allowed[:, None], cotangent, 0)
    if grid.side == 2:
        wq_full, wk_full, wv_full, wo_full, smalls, grad_blocks, *others = gather_all(
            mine, grad_two_low, halves, count
        )
    else:
        whole = jnp.concatenate(mine, axis=0)
        arrived = []
        for top in range(PLANES):
            base = whole if top == 0 else grid.send(whole, (top * grid.plane,) * CORES)
            arrived += spread(grid, base)
        wq_full, wk_full, wv_full, wo_full, smalls = assemble(grid, arrived, own_rows, experts)
    router_t = smalls[:, :, :own_rows].transpose(1, 0, 2).reshape(experts, D)
    gain_one = smalls[:, 0, own_rows : 2 * own_rows].reshape(D).astype(jnp.float32)
    gain_two = smalls[:, 1, own_rows : 2 * own_rows].reshape(D).astype(jnp.float32)
    head_cols = slice(own_rows, own_rows + HD // count)
    gain_query = smalls[:, 2, head_cols].reshape(HD).astype(jnp.float32)
    gain_key = smalls[:, 3, head_cols].reshape(HD).astype(jnp.float32)

    grad_two = grad_two_low.astype(jnp.float32)

    cosine, sine_tab = rope_tables(SEQ, HD)
    resid_zero = tokens.astype(jnp.float32)
    normed_one, inverse_one = norm_stats(resid_zero)
    attn_in = (normed_one * gain_one).astype(low)
    query_lin = jnp.dot(attn_in, wq_full, preferred_element_type=jnp.float32).reshape(
        SEQ, heads_here, HD
    )
    key_lin = jnp.dot(attn_in, wk_full, preferred_element_type=jnp.float32).reshape(
        SEQ, heads_here, HD
    )
    values_b = (
        jnp.dot(attn_in, wv_full, preferred_element_type=jnp.float32)
        .astype(low)
        .reshape(SEQ, heads_here, HD)
    )
    query_hat, query_inv = norm_stats(query_lin)
    key_hat, key_inv = norm_stats(key_lin)
    queries = rotate(query_hat * gain_query, cosine, sine_tab).astype(low)
    keys_rot = rotate(key_hat * gain_key, cosine, sine_tab).astype(low)

    def masked_scores():
        scores = (
            jnp.einsum("qhd,khd->hqk", queries, keys_rot, preferred_element_type=jnp.float32)
            * scale
        )
        return jnp.where(allowed[None, None, :], scores, NEG_BIG)

    masked = masked_scores()
    top_score = jnp.max(masked, axis=-1, keepdims=True)
    expo_vals = jnp.exp(masked - top_score)
    totals = jnp.sum(expo_vals, axis=-1, keepdims=True)
    probs_low = (expo_vals / totals).astype(low)
    log_total = top_score + jnp.log(totals)
    mixed = (
        jnp.einsum("hqk,khd->qhd", probs_low, values_b, preferred_element_type=jnp.float32)
        .reshape(SEQ, heads_here * HD)
        .astype(low)
    )
    attn_part = contract_cols(mixed, wo_full)
    resid_one = resid_zero + (attn_part + swap(attn_part))
    normed_two, inverse_two = norm_stats(resid_one)
    ffn_in = (normed_two * gain_two).astype(low)
    logits = contract_cols(ffn_in, router_t)
    route_hot = routes[:, :, None] == jnp.arange(experts)[None, None, :]
    chosen = jnp.sum(jnp.where(route_hot, logits[:, None, :], 0.0), axis=2)
    gates = jax.nn.softmax(chosen, axis=1)
    gates_wide = jnp.sum(jnp.where(route_hot, gates[:, :, None], 0.0), axis=1)

    gate_rows = jnp.pad(split_three(gates_wide.T), ((0, 0), (0, D - 3 * SEQ)))
    token_block = jnp.concatenate([ffn_in, gate_rows], axis=0)
    if grid.side == 2:
        done = moe_layer(token_block, grad_blocks, halves + others, capacity)
        saved = [tuple(done[12:17])]
        far = [grid.send(done[at], grid.second(1)) for at in (6, 7, 2, 3)]
        back_sum = both_cores(done[17])
    else:
        wg, wu, wd = (
            jnp.concatenate([half, swap(half)], axis=axis) for half, axis in zip(halves, (1, 1, 0))
        )
        grad_turns = gather_tokens(grid, grad_two_low)
        token_turns = gather_tokens(grid, token_block)
        out_turns, back_turns, saved = [], [], []
        for turn in range(2):
            outs, backs, kept = expert_turn(
                token_turns[turn], grad_turns[turn], (wg, wu, wd), capacity
            )
            out_turns.append(outs)
            back_turns.append(backs)
            saved.append(kept)
        back_sum = scatter_tokens(grid, back_turns)

    def over_turns(left, right):
        return sum(contract_rows(kept[left], kept[right]) for kept in saved)

    half = w_gate.shape[2]
    gate_w = over_turns(0, 3)
    up_w = over_turns(0, 4)
    down_w = over_turns(2, 1)
    if grid.side == 2:
        back_sum, gate_w, up_w, down_w = lax.optimization_barrier((back_sum, gate_w, up_w, down_w))

    grad_gates_wide = join_three(back_sum[SEQ:], SEQ).T
    grad_gate_sel = jnp.sum(jnp.where(route_hot, grad_gates_wide[:, None, :], 0.0), axis=2)
    grad_chosen = gates * (grad_gate_sel - jnp.sum(gates * grad_gate_sel, axis=1, keepdims=True))
    grad_logits = jnp.sum(jnp.where(route_hot, grad_chosen[:, :, None], 0.0), axis=1).astype(low)
    grad_router_t = contract_rows(grad_logits, ffn_in)
    grad_ffn_in = back_sum[:SEQ] + jnp.dot(
        grad_logits, router_t, preferred_element_type=jnp.float32
    )
    grad_gain_two = jnp.sum(grad_ffn_in * normed_two, axis=0)
    grad_one = grad_two + norm_back(grad_ffn_in * gain_two, normed_two, inverse_two)
    grad_attn = grad_one.astype(low)

    part_wo = contract_rows(grad_attn, mixed)
    grad_mixed = (
        jnp.dot(grad_attn, wo_full, preferred_element_type=jnp.float32)
        .astype(low)
        .reshape(SEQ, heads_here, HD)
    )
    if grid.side == 2:
        far, grad_mixed = lax.optimization_barrier((far, grad_mixed))
        sums_kept = [
            done[at].astype(jnp.float32) + part.astype(jnp.float32)
            for at, part in zip((4, 5, 0, 1), far)
        ]
        near = [grid.send(sums_kept[at].astype(low), grid.first(1)) for at in (1, 3)]
    masked = masked_scores()
    attn_probs = jnp.exp(masked - log_total)
    probs_again = attn_probs.astype(low)
    grad_probs = jnp.einsum(
        "qhd,khd->hqk", grad_mixed, values_b, preferred_element_type=jnp.float32
    )
    grad_values = jnp.einsum(
        "hqk,qhd->khd", probs_again, grad_mixed, preferred_element_type=jnp.float32
    )
    grad_value_lin = grad_values.astype(low).reshape(SEQ, heads_here * HD)
    part_wv = contract_rows(attn_in, grad_value_lin)
    grad_scores = (
        attn_probs * (grad_probs - jnp.sum(attn_probs * grad_probs, axis=-1, keepdims=True))
    ).astype(low)
    if grid.side == 2:
        near, grad_scores = lax.optimization_barrier((near, grad_scores))
        crossing = [
            grid.send((kept + part.astype(jnp.float32)).astype(low), grid.planes_of(turn))
            for kept, part, turn in zip(sums_kept[::2], near, (1, 0))
        ]
    grad_queries = (
        jnp.einsum("hqk,khd->qhd", grad_scores, keys_rot, preferred_element_type=jnp.float32)
        * scale
    )
    grad_keys = (
        jnp.einsum("hqk,qhd->khd", grad_scores, queries, preferred_element_type=jnp.float32) * scale
    )
    grad_query_scaled = rotate_back(grad_queries, cosine, sine_tab)
    grad_key_scaled = rotate_back(grad_keys, cosine, sine_tab)
    grad_gain_query = jnp.sum(grad_query_scaled * query_hat, axis=(0, 1))
    grad_gain_key = jnp.sum(grad_key_scaled * key_hat, axis=(0, 1))
    grad_query_lin = (
        norm_back(grad_query_scaled * gain_query, query_hat, query_inv)
        .astype(low)
        .reshape(SEQ, heads_here * HD)
    )
    grad_key_lin = (
        norm_back(grad_key_scaled * gain_key, key_hat, key_inv)
        .astype(low)
        .reshape(SEQ, heads_here * HD)
    )
    part_wq = contract_rows(attn_in, grad_query_lin)
    part_wk = contract_rows(attn_in, grad_key_lin)
    grad_attn_part = (
        contract_cols(grad_query_lin, wq_full)
        + contract_cols(grad_key_lin, wk_full)
        + contract_cols(grad_value_lin, wv_full)
    ).astype(low)
    grad_attn_in = grad_attn_part.astype(jnp.float32) + swap(grad_attn_part).astype(jnp.float32)
    grad_gain_one = jnp.sum(grad_attn_in * normed_one, axis=0)
    grad_input = grad_one + norm_back(grad_attn_in * gain_one, normed_one, inverse_one)

    head_part = HD // count
    heads_row = jnp.stack([grad_gain_query, grad_gain_key]).reshape(2, count, head_part)
    heads_row = jnp.pad(heads_row, ((0, 0), (0, 0), (0, own_rows - head_part)))
    parts = jnp.concatenate(
        [
            jnp.concatenate([grad_router_t, grad_gain_one[None], grad_gain_two[None]]).reshape(
                experts + 2, count, own_rows
            ),
            heads_row,
        ],
        axis=0,
    ).transpose(1, 0, 2)
    weight_parts = [part_wq, part_wk, part_wv, part_wo]
    if grid.side == 2:
        weight_parts = [part.astype(low) for part in weight_parts]
        parts = jnp.pad(parts, ((0, 0), (0, 4), (0, 0)))
        grad_wq, grad_wk, grad_wv, grad_wo, sums, *received = reduce_all(
            weight_parts, parts, [gate_w, up_w, down_w], count
        )
        crossing, sums = lax.optimization_barrier((crossing, sums))
        out_sum = both_cores(
            (crossing[0].astype(jnp.float32) + crossing[1].astype(jnp.float32)).astype(low)
        )
    else:
        shape = (PLANES, grid.side, grid.side)
        grad_wq, grad_wk, grad_wv, grad_wo = [
            scatter_rows(grid, part.reshape(shape + (own_rows, width)), axes, low)
            for part, axes in zip(weight_parts, ((1, 2, 0), (2, 1, 0)) * 2)
        ]
        sums = scatter_rows(
            grid, parts.reshape(shape + (experts + 4, own_rows)), (1, 2, 0), jnp.float32
        )
        sums = sums + swap(sums)
        received = [swap(part) for part in (gate_w[:, half:], up_w[:, half:], down_w[half:])]
        out_sum = scatter_tokens(grid, out_turns)
    output = (resid_one + out_sum).astype(low)
    grad_gate_w = (gate_w[:, :half] + received[0])[None]
    grad_up_w = (up_w[:, :half] + received[1])[None]
    grad_down_w = (down_w[:half] + received[2])[None]
    return (
        output,
        grad_input.astype(low),
        0.5 * sums[experts],
        grad_wq,
        grad_wk,
        grad_wv,
        sums[experts + 2, :head_part],
        sums[experts + 3, :head_part],
        grad_wo,
        0.5 * sums[experts + 1],
        0.5 * sums[:experts].T,
        grad_gate_w,
        grad_up_w,
        grad_down_w,
    )


def solution(mesh):
    return jax.shard_map(
        local,
        mesh=mesh,
        in_specs=(
            P("expert", None),
            P("expert"),
            P("expert", None),
            P("expert"),
            P("expert", "tensor"),
            P("expert", "tensor"),
            P("expert", "tensor"),
            P("expert"),
            P("expert"),
            P("expert", "tensor"),
            P("expert"),
            P("expert", None),
            P("expert", None, "tensor"),
            P("expert", None, "tensor"),
            P("expert", "tensor", None),
            P("expert", None),
        ),
        out_specs=(
            P("expert", None),
            P("expert", None),
            P("expert"),
            P("expert", "tensor"),
            P("expert", "tensor"),
            P("expert", "tensor"),
            P("expert"),
            P("expert"),
            P("expert", "tensor"),
            P("expert"),
            P("expert", None),
            P("expert", None, "tensor"),
            P("expert", None, "tensor"),
            P("expert", "tensor", None),
        ),
        check_vma=False,
    )
```

```python
import functools
import math

import jax
import jax.numpy as jnp
from jax import lax
from jax.experimental import pallas as pl
from jax.experimental.pallas import tpu as pltpu
from jax.sharding import PartitionSpec as P

D = 2048
HD = 128
TOP = 8
SEQ = 512


EPSILON = 1e-06
ROPE_BASE = 10000.0
NEG_BIG = -1e30


def rope_tables(seq_len, head_dim):
    half_dim = head_dim // 2
    inverse = ROPE_BASE ** (-(jnp.arange(half_dim).astype(jnp.float32) * 2.0 / head_dim))
    angles = jnp.arange(seq_len).astype(jnp.float32)[:, None] * inverse[None, :]
    return (jnp.cos(angles), jnp.sin(angles))


def rotate(values, cosine, sine_tab):
    half_dim = values.shape[-1] // 2
    lower_half = values[..., :half_dim]
    upper_half = values[..., half_dim:]
    cos_b = cosine[:, None, :]
    sin_b = sine_tab[:, None, :]
    return jnp.concatenate(
        [lower_half * cos_b - upper_half * sin_b, upper_half * cos_b + lower_half * sin_b], axis=-1
    )


def rotate_back(grads_in, cosine, sine_tab):
    half_dim = grads_in.shape[-1] // 2
    lower_half = grads_in[..., :half_dim]
    upper_half = grads_in[..., half_dim:]
    cos_b = cosine[:, None, :]
    sin_b = sine_tab[:, None, :]
    return jnp.concatenate(
        [lower_half * cos_b + upper_half * sin_b, upper_half * cos_b - lower_half * sin_b], axis=-1
    )


def norm_stats(values):
    inverse = lax.rsqrt(jnp.mean(values * values, axis=-1, keepdims=True) + EPSILON)
    return (values * inverse, inverse)


def norm_back(grad_normed, normed, inverse):
    return inverse * (grad_normed - normed * jnp.mean(grad_normed * normed, axis=-1, keepdims=True))


def contract_rows(left_mat, right_mat):
    return lax.dot_general(
        left_mat, right_mat, (((0,), (0,)), ((), ())), preferred_element_type=jnp.float32
    )


def contract_cols(left_mat, right_mat):
    return lax.dot_general(
        left_mat, right_mat, (((1,), (1,)), ((), ())), preferred_element_type=jnp.float32
    )


PLANES = 4
CORES = 2


class Grid:
    def __init__(self, count):
        self.count = count
        self.plane = count // PLANES
        self.side = math.isqrt(self.plane)
        self.near = range(1, self.side)

    def first(self, step):
        return (step, step * self.side)

    def second(self, step):
        return (step * self.side, step)

    def planes_of(self, turn):
        return ((0, 3)[turn] * self.plane, (1, 2)[turn] * self.plane)

    def send(self, value, masks):
        pairs = [
            (device * CORES + core, (device ^ masks[core]) * CORES + core)
            for device in range(self.count)
            for core in range(CORES)
        ]
        return lax.ppermute(value, ("expert", "tensor"), pairs)


def swap(value):
    return lax.ppermute(value, "tensor", [(0, 1), (1, 0)])


def both_cores(part):
    return part.astype(jnp.float32) + swap(part).astype(jnp.float32)


def spread(grid, base):
    row = [base] + [grid.send(base, grid.first(step)) for step in grid.near]
    blocks = list(row)
    for step in grid.near:
        blocks += [grid.send(block, grid.second(step)) for block in row]
    return blocks


def gather_tokens(grid, block):
    return [spread(grid, grid.send(block, grid.planes_of(turn))) for turn in range(2)]


def collect(grid, blocks):
    side = grid.side
    sums = [block.astype(jnp.float32) for block in blocks[:side]]
    for far in grid.near:
        for step in range(side):
            sums[step] = sums[step] + grid.send(
                blocks[far * side + step], grid.second(far)
            ).astype(jnp.float32)
    total = sums[0]
    for step in grid.near:
        total = total + grid.send(sums[step].astype(jnp.bfloat16), grid.first(step)).astype(
            jnp.float32
        )
    return total


def scatter_tokens(grid, turns):
    total = None
    for turn in (1, 0):
        part = grid.send(collect(grid, turns[turn]).astype(jnp.bfloat16), grid.planes_of(turn))
        part = part.astype(jnp.float32)
        total = part if total is None else total + part
    return both_cores(total.astype(jnp.bfloat16))


def scatter_rows(grid, value, axes, wire):
    me = lax.axis_index("expert")
    units = (grid.plane, grid.side, 1)
    sizes = (PLANES, grid.side, grid.side)
    gone = []
    for axis in axes:
        unit, size = units[axis], sizes[axis]
        place = (me // unit) % size
        at = axis - sum(1 for other in gone if other < axis)
        total = lax.dynamic_index_in_dim(value, place, at, keepdims=False).astype(jnp.float32)
        for step in range(1, size):
            part = lax.dynamic_index_in_dim(value, place ^ step, at, keepdims=False).astype(wire)
            total = total + grid.send(part, (unit * step,) * CORES).astype(jnp.float32)
        value = total
        gone.append(axis)
    return value


def assemble(grid, blocks, rows, extra):
    count, width = grid.count, blocks[0].shape[1]
    me = lax.axis_index("expert")
    core = lax.axis_index("tensor")
    place = jnp.arange(count)
    top, mid, low = place // grid.plane, (place // grid.side) % grid.side, place % grid.side
    turned = top * grid.plane + low * grid.side + mid
    owner = me ^ jnp.where(core == 0, place, turned)

    def body(owner_ref, *refs):
        ins, outs, small, sem = refs[:count], refs[count : count + 4], refs[count + 4], refs[-1]
        copies = []
        for index in range(count):
            at = owner_ref[index]
            for which in range(4):
                copies.append(
                    pltpu.make_async_copy(
                        ins[index].at[pl.ds(which * rows, rows)],
                        outs[which].at[pl.ds(pl.multiple_of(at * rows, rows), rows)],
                        sem.at[index, which],
                    )
                )
            copies.append(
                pltpu.make_async_copy(
                    ins[index].at[pl.ds(4 * rows, extra)], small.at[at], sem.at[index, 4]
                )
            )
        for copy in copies:
            copy.start()
        for copy in copies:
            copy.wait()

    full = jax.ShapeDtypeStruct((count * rows, width), jnp.bfloat16)
    small = jax.ShapeDtypeStruct((count, extra, width), jnp.bfloat16)
    return pl.pallas_call(
        body,
        grid_spec=pltpu.PrefetchScalarGridSpec(
            num_scalar_prefetch=1,
            grid=(),
            in_specs=[pl.BlockSpec(memory_space=pl.ANY)] * count,
            out_specs=[pl.BlockSpec(memory_space=pltpu.VMEM)] * 5,
            scratch_shapes=[pltpu.SemaphoreType.DMA((count, 5))],
        ),
        out_shape=[full] * 4 + [small],
        name="assemble",
    )(owner, *blocks)


class Place:
    def __init__(self):
        self.me = me = lax.axis_index("expert")
        self.core = core = lax.axis_index("tensor")
        top, mid, low = me // 4, (me // 2) % 2, me % 2
        flip_low = me + 1 - 2 * low
        flip_mid = me + 2 - 4 * mid
        self.first = flip_low + core * (flip_mid - flip_low)
        self.second = flip_mid + core * (flip_low - flip_mid)
        self.planes = (
            me,
            me + 4 - 8 * (top % 2),
            me + 8 - 16 * (top // 2),
            me + 12 - 8 * top,
        )

    def owner(self, plane, far, near):
        return self.planes[plane] + far * (self.second - self.me) + near * (self.first - self.me)

    def greet(self, sibling):
        barrier = pltpu.get_barrier_semaphore()
        partners = [(device, self.core) for device in (self.first, self.second) + self.planes[1:]]
        if sibling:
            partners.append((self.me, 1 - self.core))
        for partner in partners:
            pl.semaphore_signal(
                barrier, inc=1, device_id=partner, device_id_type=pl.DeviceIdType.MESH
            )
        pl.semaphore_wait(barrier, len(partners))


def remote(source, target, send, recv, device):
    return pltpu.make_async_remote_copy(
        src_ref=source,
        dst_ref=target,
        send_sem=send,
        recv_sem=recv,
        device_id=device,
        device_id_type=pl.DeviceIdType.MESH,
    )


def gather_kernel(rows, *refs):
    mine, grad, halves, refs = refs[:5], refs[5], refs[6:9], refs[9:]
    full, grads, others, refs = refs[:5], refs[5], refs[6:9], refs[9:]
    send_sem, recv_sem, grad_send, grad_recv, half_send, half_recv, own_sem = refs
    place = Place()
    core = place.core
    place.greet(True)

    def part(which, plane, far, near):
        owner = place.owner(plane, far, near)
        if which == 4:
            return full[4].at[owner]
        return full[which].at[pl.ds(pl.multiple_of(owner * rows, rows), rows)]

    def pass_weights(source, plane, slot, device):
        out = []
        for which in range(5):
            here = part(which, *source)
            out.append(
                remote(
                    mine[which] if source == (0, 0, 0) else here,
                    here,
                    send_sem.at[4 * plane + slot, which],
                    recv_sem.at[4 * plane + slot, which],
                    (device, core),
                )
            )
        return out

    def start(copies):
        for copy in copies:
            copy.start()

    def arrived(plane, slot):
        for copy in pass_weights((plane, slot // 2, slot % 2), plane, slot, place.first):
            copy.wait_recv()

    def pass_grad(source, slot, device):
        return remote(
            source, grads.at[slot], grad_send.at[slot], grad_recv.at[slot], (device, core)
        )

    for plane in (1, 2, 3):
        start(pass_weights((0, 0, 0), plane, 0, place.planes[plane]))
    start(pass_weights((0, 0, 0), 0, 1, place.first))
    start(pass_weights((0, 0, 0), 0, 2, place.second))
    far_plane = place.planes[3] + core * (place.planes[2] - place.planes[3])

    @pl.when(core == 1)
    def _():
        pass_grad(grad, 0, place.planes[1]).start()

    pass_grad(grad, 4, far_plane).start()
    swaps = [
        remote(halves[i], others[i], half_send.at[i], half_recv.at[i], (place.me, 1 - core))
        for i in range(3)
    ]
    start(swaps)
    keeps = [
        pltpu.make_async_copy(mine[which], part(which, 0, 0, 0), own_sem.at[which])
        for which in range(5)
    ]
    start(keeps)

    @pl.when(core == 0)
    def _():
        pltpu.make_async_copy(grad, grads.at[0], own_sem.at[5]).start()

    for plane in range(4):
        if plane > 0:
            arrived(plane, 0)
            start(pass_weights((plane, 0, 0), plane, 1, place.first))
            start(pass_weights((plane, 0, 0), plane, 2, place.second))
        arrived(plane, 1)
        start(pass_weights((plane, 0, 1), plane, 3, place.second))

    @pl.when(core == 0)
    def _():
        pass_grad(grad, 1, place.first).start()
        pass_grad(grad, 2, place.second).start()

    @pl.when(core == 1)
    def _():
        pass_grad(grads.at[0], 0, place.first).wait_recv()
        pass_grad(grads.at[0], 1, place.first).start()
        pass_grad(grads.at[0], 2, place.second).start()

    pass_grad(grads.at[1], 1, place.first).wait_recv()
    pass_grad(grads.at[1], 3, place.second).start()
    pass_grad(grads.at[4], 4, place.first).wait_recv()
    pass_grad(grads.at[4], 5, place.first).start()
    pass_grad(grads.at[4], 6, place.second).start()
    pass_grad(grads.at[5], 5, place.first).wait_recv()
    pass_grad(grads.at[5], 7, place.second).start()

    for plane in range(4):
        arrived(plane, 2)
        arrived(plane, 3)
    for slot in (2, 3, 6, 7):
        pass_grad(grads.at[slot], slot, place.first).wait_recv()
    for slot in range(1, 16):
        for copy in pass_weights((slot // 4, 0, 0), slot // 4, slot % 4, place.first):
            copy.wait_send()
    for slot in range(1, 8):
        pass_grad(grads.at[slot], slot, place.first).wait_send()

    @pl.when(core == 1)
    def _():
        pass_grad(grads.at[0], 0, place.first).wait_send()

    @pl.when(core == 0)
    def _():
        pltpu.make_async_copy(grad, grads.at[0], own_sem.at[5]).wait()

    for copy in swaps + keeps:
        copy.wait()


def gather_all(mine, grad, halves, count):
    rows, width = mine[0].shape
    extra = mine[4].shape[0]
    low = jnp.bfloat16
    hbm = pl.BlockSpec(memory_space=pl.ANY)
    full = jax.ShapeDtypeStruct((count * rows, width), low)
    return pl.pallas_call(
        functools.partial(gather_kernel, rows),
        in_specs=[hbm] * 9,
        out_specs=[hbm] * 9,
        out_shape=[full] * 4
        + [
            jax.ShapeDtypeStruct((count, extra, width), low),
            jax.ShapeDtypeStruct((8,) + grad.shape, low),
        ]
        + [jax.ShapeDtypeStruct(half.shape, low) for half in halves],
        scratch_shapes=[
            pltpu.SemaphoreType.DMA((16, 5)),
            pltpu.SemaphoreType.DMA((16, 5)),
            pltpu.SemaphoreType.DMA((8,)),
            pltpu.SemaphoreType.DMA((8,)),
            pltpu.SemaphoreType.DMA((3,)),
            pltpu.SemaphoreType.DMA((3,)),
            pltpu.SemaphoreType.DMA((6,)),
        ],
        compiler_params=pltpu.CompilerParams(collective_id=1, has_side_effects=True),
        name="gather_all",
    )(*mine, grad, *halves)


def reduce_kernel(rows, *refs):
    whole, small, halves, refs = refs[:4], refs[4], refs[5:8], refs[8:]
    out, small_out, others, refs = refs[:4], refs[4], refs[5:8], refs[8:]
    (
        own,
        far_in,
        near_in,
        plane_in,
        near_stage,
        plane_stage,
        small_own,
        small_far,
        small_near,
        small_plane,
        small_near_stage,
        small_plane_stage,
        small_last,
        small_other,
        load_sem,
        far_send,
        far_recv,
        near_send,
        near_recv,
        plane_send,
        plane_recv,
        half_send,
        half_recv,
        last_send,
        last_recv,
    ) = refs
    place = Place()
    core = place.core
    sibling = (place.me, 1 - core)
    place.greet(True)
    second, first = (place.second, core), (place.first, core)

    def source(which, plane, far, near):
        owner = place.owner(plane, far, near)
        if which == 4:
            return small.at[owner]
        return whole[which].at[pl.ds(pl.multiple_of(owner * rows, rows), rows)]

    def load(which, plane, near):
        target = small_own.at[2 * plane + near] if which == 4 else own.at[2 * plane + near, which]
        return pltpu.make_async_copy(
            source(which, plane, 0, near), target, load_sem.at[2 * plane + near, which]
        )

    def to_second(which, plane, near):
        target = small_far.at[2 * plane + near]
        if which != 4:
            target = far_in.at[2 * plane + near, which]
        return remote(
            source(which, plane, 1, near),
            target,
            far_send.at[2 * plane + near, which],
            far_recv.at[2 * plane + near, which],
            second,
        )

    def to_first(which, plane):
        here, there = small_near_stage.at[plane], small_near.at[plane]
        if which is not None:
            here, there = near_stage.at[plane, which], near_in.at[plane, which]
        at = 4 if which is None else which
        return remote(here, there, near_send.at[plane, at], near_recv.at[plane, at], first)

    def to_plane(which, plane):
        here, there = small_plane_stage.at[plane - 1], small_plane.at[plane - 1]
        if which is not None:
            here, there = plane_stage.at[plane - 1, which], plane_in.at[plane - 1, which]
        at = 4 if which is None else which
        return remote(
            here,
            there,
            plane_send.at[plane - 1, at],
            plane_recv.at[plane - 1, at],
            (place.planes[plane], core),
        )

    for plane in (3, 2, 1, 0):
        for near in (1, 0):
            for which in range(5):
                to_second(which, plane, near).start()
    for plane in (3, 2, 1, 0):
        for near in (1, 0):
            for which in range(5):
                load(which, plane, near).start()
    middle = others[0].shape[1]
    theirs = [
        halves[0].at[:, pl.ds(middle, middle)],
        halves[1].at[:, pl.ds(middle, middle)],
        halves[2].at[pl.ds(middle, middle)],
    ]
    swaps = [
        remote(theirs[i], others[i], half_send.at[i], half_recv.at[i], sibling) for i in range(3)
    ]
    for copy in swaps:
        copy.start()

    def added(parts, target):
        total = parts[0].astype(jnp.float32)
        for value in parts[1:]:
            total = total + value.astype(jnp.float32)
        return total.astype(target.dtype)

    def over_rows(parts, target):
        def body(step, carry):
            span = pl.ds(pl.multiple_of(step * 16, 16), 16)
            target[span, :] = added([part[span, :] for part in parts], target)
            return carry

        lax.fori_loop(0, rows // 16, body, 0)

    def near_sums(plane):
        for which in range(4):
            load(which, plane, 1).wait()
            to_second(which, plane, 1).wait_recv()
            over_rows(
                [own.at[2 * plane + 1, which], far_in.at[2 * plane + 1, which]],
                near_stage.at[plane, which],
            )
            to_first(which, plane).start()
        load(4, plane, 1).wait()
        to_second(4, plane, 1).wait_recv()
        small_near_stage[plane] = small_own[2 * plane + 1] + small_far[2 * plane + 1]
        to_first(None, plane).start()

    def plane_sums(plane):
        for which in range(4):
            load(which, plane, 0).wait()
            to_second(which, plane, 0).wait_recv()
            to_first(which, plane).wait_recv()
            over_rows(
                [
                    own.at[2 * plane, which],
                    far_in.at[2 * plane, which],
                    near_in.at[plane, which],
                ],
                plane_stage.at[plane - 1, which],
            )
            to_plane(which, plane).start()
        load(4, plane, 0).wait()
        to_second(4, plane, 0).wait_recv()
        to_first(None, plane).wait_recv()
        small_plane_stage[plane - 1] = (
            small_own[2 * plane] + small_far[2 * plane] + small_near[plane]
        )
        to_plane(None, plane).start()

    near_sums(3)
    near_sums(2)
    plane_sums(3)
    near_sums(1)
    plane_sums(2)
    near_sums(0)
    plane_sums(1)
    load(4, 0, 0).wait()
    to_second(4, 0, 0).wait_recv()
    to_first(None, 0).wait_recv()
    for plane in (1, 2, 3):
        to_plane(None, plane).wait_recv()
    small_last[...] = (
        small_own[0]
        + small_far[0]
        + small_near[0]
        + small_plane[0]
        + small_plane[1]
        + small_plane[2]
    )
    last = remote(small_last, small_other, last_send.at[0], last_recv.at[0], sibling)
    last.start()
    for which in range(4):
        load(which, 0, 0).wait()
        to_second(which, 0, 0).wait_recv()
        to_first(which, 0).wait_recv()
        for plane in (1, 2, 3):
            to_plane(which, plane).wait_recv()
        over_rows(
            [own.at[0, which], far_in.at[0, which], near_in.at[0, which]]
            + [plane_in.at[plane, which] for plane in range(3)],
            out[which],
        )
    last.wait()
    small_out[...] = small_last[...] + small_other[...]
    for plane in range(4):
        for which in range(5):
            at = None if which == 4 else which
            for near in range(2):
                to_second(which, plane, near).wait_send()
            to_first(at, plane).wait_send()
            if plane > 0:
                to_plane(at, plane).wait_send()
    for copy in swaps:
        copy.wait()


def reduce_all(whole, small, halves, count):
    rows, width = whole[0].shape[0] // count, whole[0].shape[1]
    low = jnp.bfloat16
    hbm = pl.BlockSpec(memory_space=pl.ANY)
    vmem = pl.BlockSpec(memory_space=pltpu.VMEM)
    tiny = small.shape[1:]

    def wide(*dims):
        return pltpu.VMEM(dims + (rows, width), low)

    def little(*dims):
        return pltpu.VMEM(dims + tiny, jnp.float32)

    def sems(*dims):
        return pltpu.SemaphoreType.DMA(dims)

    return pl.pallas_call(
        functools.partial(reduce_kernel, rows),
        in_specs=[hbm] * 8,
        out_specs=[vmem] * 5 + [hbm] * 3,
        out_shape=[jax.ShapeDtypeStruct((rows, width), jnp.float32)] * 4
        + [jax.ShapeDtypeStruct(tiny, jnp.float32)]
        + [
            jax.ShapeDtypeStruct((dims[0] // cut, dims[1] // (3 - cut)), jnp.float32)
            for dims, cut in ((halves[0].shape, 1), (halves[1].shape, 1), (halves[2].shape, 2))
        ],
        scratch_shapes=[wide(8, 4), wide(8, 4), wide(4, 4), wide(3, 4), wide(4, 4), wide(3, 4)]
        + [little(8), little(8), little(4), little(3), little(4), little(3), little(), little()]
        + [sems(8, 5)] * 3
        + [sems(4, 5)] * 2
        + [sems(3, 5)] * 2
        + [sems(3)] * 2
        + [sems(1)] * 2,
        compiler_params=pltpu.CompilerParams(
            collective_id=2, has_side_effects=True, vmem_limit_bytes=60 * 1024 * 1024
        ),
        name="reduce_all",
    )(*whole, small, *halves)


def split_three(value):
    high = value.astype(jnp.bfloat16)
    rest = value - high.astype(jnp.float32)
    middle = rest.astype(jnp.bfloat16)
    low = (rest - middle.astype(jnp.float32)).astype(jnp.bfloat16)
    return jnp.concatenate([high, middle, low], axis=-1)


def join_three(parts, length):
    parts = parts.astype(jnp.float32)
    return (
        parts[..., :length] + parts[..., length : 2 * length] + parts[..., 2 * length : 3 * length]
    )


def expert_turn(blocks, grads, weights, capacity):
    wg, wu, wd = weights
    me = lax.axis_index("expert")
    experts = blocks[0].shape[0] - SEQ
    gate = jnp.concatenate(
        [
            join_three(lax.dynamic_slice(block, (SEQ + me, 0), (1, 3 * SEQ)), SEQ)
            for block in blocks
        ],
        axis=0,
    )
    used = gate > 0.0
    ordered = (jnp.arange(SEQ)[:, None] < jnp.arange(SEQ)[None, :]).astype(jnp.bfloat16)
    slot = jnp.dot(used.astype(jnp.bfloat16), ordered, preferred_element_type=jnp.float32)
    slot = slot.astype(jnp.int32)
    hot = (jnp.arange(capacity)[None, :, None] == slot[:, None, :]) & used[:, None, :]
    pick = hot.astype(jnp.bfloat16)
    slot_gate = jnp.sum(jnp.where(hot, gate[:, None, :], 0.0), axis=2).reshape(-1, 1)
    rows = jnp.concatenate(
        [
            jnp.dot(pick[i], block[:SEQ], preferred_element_type=jnp.float32).astype(jnp.bfloat16)
            for i, block in enumerate(blocks)
        ],
        axis=0,
    )
    grad_rows = jnp.concatenate(
        [
            jnp.dot(pick[i], block, preferred_element_type=jnp.float32).astype(jnp.bfloat16)
            for i, block in enumerate(grads)
        ],
        axis=0,
    )
    gate_lin = jnp.dot(rows, wg, preferred_element_type=jnp.float32)
    up_lin = jnp.dot(rows, wu, preferred_element_type=jnp.float32)
    grad_full = contract_cols(grad_rows, wd)
    sigmoid_gate = jax.nn.sigmoid(gate_lin)
    activated = gate_lin * sigmoid_gate
    hidden = activated * up_lin
    hidden_low = (hidden * slot_gate).astype(jnp.bfloat16)
    slot_grad = jnp.sum(hidden * grad_full, axis=1).reshape(len(blocks), capacity, 1)
    grad_hidden = grad_full * slot_gate
    silu_slope = sigmoid_gate * (1.0 + gate_lin * (1.0 - sigmoid_gate))
    grad_gate = (grad_hidden * up_lin * silu_slope).astype(jnp.bfloat16)
    grad_up = (grad_hidden * activated).astype(jnp.bfloat16)
    value = jnp.dot(hidden_low, wd, preferred_element_type=jnp.float32).astype(jnp.bfloat16)
    grad_in = (contract_cols(grad_gate, wg) + contract_cols(grad_up, wu)).astype(jnp.bfloat16)
    token_grad = split_three(jnp.sum(jnp.where(hot, slot_grad, 0.0), axis=1))
    outs, backs = [], []
    for i in range(len(blocks)):
        span = slice(i * capacity, (i + 1) * capacity)
        outs.append(contract_rows(pick[i], value[span]).astype(jnp.bfloat16))
        back = contract_rows(pick[i], grad_in[span]).astype(jnp.bfloat16)
        extra = jnp.where(
            (jnp.arange(experts) == me)[:, None],
            jnp.pad(token_grad[i : i + 1], ((0, 0), (0, D - 3 * SEQ))),
            0,
        )
        backs.append(jnp.concatenate([back, extra], axis=0))
    return outs, backs, (rows, grad_rows, hidden_low, grad_gate, grad_up)


def moe_kernel(
    capacity,
    experts,
    own,
    *refs,
):
    weights, grads, refs = refs[:6], refs[6], refs[7:]
    parts, outs, refs = refs[:8], refs[8:12], refs[12:]
    (
    blocks,
    far_sums,
    near_sums,
    plane_sums,
    rows_out,
    grows_out,
    hidden_out,
    gate_out,
    up_out,
    result,
    wg_v,
    wu_v,
    wd_v,
    block_v,
    grad_v,
    rows_v,
    grows_v,
    hidden_v,
    gate_v,
    up_v,
    pick_v,
    pick_t,
    ordered,
    stage,
    part_v,
    taken,
    weight_sem,
    load_sem,
    save_sem,
    send_sem,
    recv_sem,
    back_send,
    back_recv,
    piece_send,
    piece_recv,
    out_send,
    out_recv,
    ) = refs
    me = lax.axis_index("expert")
    core = lax.axis_index("tensor")
    top, mid, low = me // 4, (me // 2) % 2, me % 2
    flip_low = me + 1 - 2 * low
    flip_mid = me + 2 - 4 * mid
    first = flip_low + core * (flip_mid - flip_low)
    second = flip_mid + core * (flip_low - flip_mid)
    plane_one = me + 4 - 8 * (top % 2)
    plane_two = me + 8 - 16 * (top // 2)
    plane_three = me + 12 - 8 * top
    far_plane = plane_three + core * (plane_two - plane_three)
    mesh = pl.DeviceIdType.MESH

    barrier = pltpu.get_barrier_semaphore()
    for device in (first, second, plane_one, plane_two, plane_three):
        pl.semaphore_signal(barrier, inc=1, device_id=(device, core), device_id_type=mesh)
    pl.semaphore_wait(barrier, 5)

    def pass_on(source, slot, device):
        return pltpu.make_async_remote_copy(
            src_ref=source,
            dst_ref=blocks.at[slot],
            send_sem=send_sem.at[slot],
            recv_sem=recv_sem.at[slot],
            device_id=(device, core),
            device_id_type=mesh,
        )

    def give(source, target, index, device):
        return pltpu.make_async_remote_copy(
            src_ref=source,
            dst_ref=target,
            send_sem=back_send.at[index],
            recv_sem=back_recv.at[index],
            device_id=(device, core),
            device_id_type=mesh,
        )

    half = wg_v.shape[1] // 2
    targets = []
    for span in (slice(0, half), slice(half, 2 * half)):
        targets += [wg_v.at[:, span], wu_v.at[:, span], wd_v.at[span]]
    loads = [
        pltpu.make_async_copy(source, target, weight_sem.at[index])
        for index, (source, target) in enumerate(zip(weights, targets))
    ]

    @pl.when(core == 0)
    def _():
        pass_on(own, 1, first).start()
        pass_on(own, 2, second).start()

    @pl.when(core == 1)
    def _():
        pass_on(own, 0, plane_one).start()

    pass_on(own, 4, far_plane).start()
    for copy in loads:
        copy.start()

    length = SEQ
    ordered[...] = jnp.where(
        lax.broadcasted_iota(jnp.int32, (length, length), 0)
        < lax.broadcasted_iota(jnp.int32, (length, length), 1),
        1.0,
        0.0,
    ).astype(jnp.bfloat16)
    width = block_v.shape[1]
    hidden = hidden_v.shape[1]
    both = (((1,), (1,)), ((), ()))

    def dot(left, right):
        return jnp.dot(left, right, preferred_element_type=jnp.float32)

    def dot_t(left, right):
        return lax.dot_general(left, right, both, preferred_element_type=jnp.float32)

    def add_block(slot, sources, start=0, size=length + experts):
        part = pl.ds(start, size)
        copies = [
            pltpu.make_async_copy(source.at[part], taken.at[index, part], load_sem.at[2 + index])
            for index, source in enumerate(sources)
        ]
        for copy in copies:
            copy.start()
        for copy in copies:
            copy.wait()

        def rows_of(step, carry):
            span = pl.ds(pl.multiple_of(start + step * 16, 16), 16)
            total = stage[slot, span, :].astype(jnp.float32)
            for index in range(len(sources)):
                total = total + taken[index, span, :].astype(jnp.float32)
            stage[slot, span, :] = total.astype(jnp.bfloat16)
            return carry

        lax.fori_loop(0, size // 16, rows_of, 0)

    pieces = 3
    size = (length + experts) // pieces

    def give_piece(source, target, kind, piece, device):
        part = pl.ds(piece * size, size)
        return pltpu.make_async_remote_copy(
            src_ref=source.at[part],
            dst_ref=target.at[part],
            send_sem=piece_send.at[kind, piece],
            recv_sem=piece_recv.at[kind, piece],
            device_id=(device, core),
            device_id_type=mesh,
        )

    def far_piece(which, piece):
        return give_piece(stage.at[6 + which], far_sums.at[2 + which], which, piece, second)

    def near_piece(piece):
        return give_piece(stage.at[5], near_sums.at[1], 2, piece, first)

    def plane_piece(piece):
        return give_piece(stage.at[4], plane_sums.at[1], 3, piece, far_plane)

    def send_out(index):
        return pltpu.make_async_remote_copy(
            src_ref=parts[(2, 3, 6, 7)[index]],
            dst_ref=outs[index],
            send_sem=out_send.at[index],
            recv_sem=out_recv.at[index],
            device_id=(second, core),
            device_id_type=mesh,
        )

    def first_sum(turn):
        give(far_sums.at[2 * turn + 1], far_sums.at[2 * turn + 1], 2 * turn + 1, second).wait_recv()
        add_block(4 * turn + 1, [far_sums.at[2 * turn + 1]])
        give(stage.at[4 * turn + 1], near_sums.at[turn], 4 + turn, first).start()

    def plane_sum(turn):
        give(far_sums.at[2 * turn], far_sums.at[2 * turn], 2 * turn, second).wait_recv()
        give(near_sums.at[turn], near_sums.at[turn], 4 + turn, first).wait_recv()
        add_block(4 * turn, [far_sums.at[2 * turn], near_sums.at[turn]])

    def block_step(k, carry):
        turn_at = k % 4
        relayed = jnp.logical_or(k != 0, core != 0)

        @pl.when(relayed)
        def _():
            pass_on(blocks.at[k], k, first).wait_recv()
            pltpu.make_async_copy(blocks.at[k], block_v, load_sem.at[0]).start()

        @pl.when(jnp.logical_not(relayed))
        def _():
            pltpu.make_async_copy(own, block_v, load_sem.at[0]).start()

        @pl.when(jnp.logical_and(relayed, turn_at == 0))
        def _():
            pass_on(blocks.at[k], k + 1, first).start()

        @pl.when(jnp.logical_and(relayed, turn_at < 2))
        def _():
            pass_on(blocks.at[k], k + 2, second).start()

        pltpu.make_async_copy(grads.at[k], grad_v, load_sem.at[1]).start()

        @pl.when(k == 0)
        def _():
            for copy in loads:
                copy.wait()

        pltpu.make_async_copy(blocks.at[k], block_v, load_sem.at[0]).wait()

        here = lax.broadcasted_iota(jnp.int32, (experts, 3 * length), 0) == me
        row = jnp.sum(
            jnp.where(here, block_v[length:, : 3 * length].astype(jnp.float32), 0.0),
            axis=0,
            keepdims=True,
        )
        gate = row[:, :length] + row[:, length : 2 * length] + row[:, 2 * length :]
        used = jnp.where(gate > 0.0, 1.0, 0.0)
        slot = dot(jnp.broadcast_to(used, (16, length)).astype(jnp.bfloat16), ordered[...])[:1]
        slot = jnp.where(gate > 0.0, slot, -1.0)
        number = lax.broadcasted_iota(jnp.int32, (capacity, length), 0).astype(jnp.float32)
        pick = jnp.where(number == slot, 1.0, 0.0)
        slot_gate = jnp.sum(pick * gate, axis=1, keepdims=True)
        pick_v[...] = pick.astype(jnp.bfloat16)
        pick_t[...] = pick.T.astype(jnp.bfloat16)
        for at in range(0, width, 512):
            span = slice(at, at + 512)
            rows_v[:, span] = dot(pick_v[...], block_v[:length, span]).astype(jnp.bfloat16)
        pltpu.make_async_copy(grads.at[k], grad_v, load_sem.at[1]).wait()
        for at in range(0, width, 512):
            span = slice(at, at + 512)
            grows_v[:, span] = dot(pick_v[...], grad_v[:, span]).astype(jnp.bfloat16)
        slot_grad = jnp.zeros((capacity, 1), jnp.float32)
        for at in range(0, hidden, 256):
            span = slice(at, at + 256)
            gate_lin = dot(rows_v[...], wg_v[:, span])
            up_lin = dot(rows_v[...], wu_v[:, span])
            grad_full = dot_t(grows_v[...], wd_v[span, :])
            sigmoid_gate = 1.0 / (1.0 + jnp.exp(-gate_lin))
            activated = gate_lin * sigmoid_gate
            value = activated * up_lin
            hidden_v[:, span] = (value * slot_gate).astype(jnp.bfloat16)
            slot_grad = slot_grad + jnp.sum(value * grad_full, axis=1, keepdims=True)
            grad_hidden = grad_full * slot_gate
            slope = sigmoid_gate * (1.0 + gate_lin * (1.0 - sigmoid_gate))
            gate_v[:, span] = (grad_hidden * up_lin * slope).astype(jnp.bfloat16)
            up_v[:, span] = (grad_hidden * activated).astype(jnp.bfloat16)
        at = pl.multiple_of(k * capacity, capacity)
        saves = [
            pltpu.make_async_copy(source, target.at[pl.ds(at, capacity)], save_sem.at[index])
            for index, (source, target) in enumerate(
                (
                    (rows_v, rows_out),
                    (grows_v, grows_out),
                    (hidden_v, hidden_out),
                    (gate_v, gate_out),
                    (up_v, up_out),
                )
            )
        ]
        for copy in saves:
            copy.start()

        for index in range(8):

            @pl.when(k == index + 1)
            def _():
                pltpu.make_async_copy(part_v, parts[index], save_sem.at[5]).wait()

        for index in range(2):

            @pl.when(k == 3 + index)
            def _():
                send_out(index).start()

        for at in range(0, width, 512):
            span = slice(at, at + 512)
            value = dot(hidden_v[...], wd_v[:, span]).astype(jnp.bfloat16)
            part_v[:, span] = dot(pick_t[...], value).astype(jnp.bfloat16)
            back = dot_t(gate_v[...], wg_v[span, :]) + dot_t(up_v[...], wu_v[span, :])
            stage[k, :length, span] = dot(pick_t[...], back.astype(jnp.bfloat16)).astype(
                jnp.bfloat16
            )
        total = jnp.sum(pick_v[...].astype(jnp.float32) * slot_grad, axis=0, keepdims=True)
        here = lax.broadcasted_iota(jnp.int32, (experts, length), 0) == me
        for index in range(3):
            high = total.astype(jnp.bfloat16).astype(jnp.float32)
            stage[k, length:, index * length : (index + 1) * length] = jnp.where(
                here, high, 0.0
            ).astype(jnp.bfloat16)
            total = total - high
        stage[k, length:, 3 * length :] = jnp.zeros((experts, width - 3 * length), jnp.bfloat16)
        for index in range(8):

            @pl.when(k == index)
            def _():
                pltpu.make_async_copy(part_v, parts[index], save_sem.at[5]).start()

        @pl.when(jnp.logical_and(turn_at >= 2, k < 4))
        def _():
            index = turn_at - 2
            give(stage.at[k], far_sums.at[index], index, second).start()

        for which in range(2):

            @pl.when(k == 6 + which)
            def _():
                for piece in range(pieces):
                    far_piece(which, piece).start()

        @pl.when(k == 5)
        def _():
            first_sum(0)

        @pl.when(k == 6)
        def _():
            plane_sum(0)

            @pl.when(core == 1)
            def _():
                give(stage.at[0], plane_sums.at[0], 6, plane_one).start()

        for copy in saves:
            copy.wait()
        return carry

    lax.fori_loop(0, 8, block_step, 0)
    pltpu.make_async_copy(part_v, parts[7], save_sem.at[5]).wait()
    send_out(2).start()
    send_out(3).start()
    for piece in range(pieces):
        far_piece(1, piece).wait_recv()
        add_block(5, [far_sums.at[3]], piece * size, size)
        near_piece(piece).start()
    for piece in range(pieces):
        far_piece(0, piece).wait_recv()
        near_piece(piece).wait_recv()
        add_block(4, [far_sums.at[2], near_sums.at[1]], piece * size, size)
        plane_piece(piece).start()

    @pl.when(core == 1)
    def _():
        give(stage.at[0], plane_sums.at[0], 6, plane_one).wait()
        pltpu.make_async_copy(plane_sums.at[0], stage.at[0], load_sem.at[0]).start()
        pltpu.make_async_copy(plane_sums.at[0], stage.at[0], load_sem.at[0]).wait()

    for piece in range(pieces):
        plane_piece(piece).wait_recv()
        add_block(0, [plane_sums.at[1]], piece * size, size)
    final = pltpu.make_async_copy(stage.at[0], result, load_sem.at[0])
    final.start()
    for index in range(4):
        send_out(index).wait()
    for k in range(8):
        if k > 0:
            pass_on(blocks.at[k], k, first).wait_send()
    @pl.when(core == 1)
    def _():
        pass_on(blocks.at[0], 0, first).wait_send()

    for index in (0, 1, 4):
        give(result, result, index, first).wait_send()
    for piece in range(pieces):
        for which in range(2):
            far_piece(which, piece).wait_send()
        near_piece(piece).wait_send()
        plane_piece(piece).wait_send()
    final.wait()


def moe_layer(own, grads, weights, capacity):
    rows, width = own.shape
    hidden = 2 * weights[0].shape[1]
    experts = rows - SEQ
    low = jnp.bfloat16
    hbm = pl.BlockSpec(memory_space=pl.ANY)

    def shape(*dims):
        return jax.ShapeDtypeStruct(dims, low)

    return pl.pallas_call(
        functools.partial(moe_kernel, capacity, experts),
        in_specs=[hbm] * 8,
        out_specs=[hbm] * 22,
        out_shape=[shape(SEQ, width)] * 12
        + [
            shape(8, rows, width),
            shape(4, rows, width),
            shape(2, rows, width),
            shape(2, rows, width),
            shape(8 * capacity, width),
            shape(8 * capacity, width),
            shape(8 * capacity, hidden),
            shape(8 * capacity, hidden),
            shape(8 * capacity, hidden),
            shape(rows, width),
        ],
        scratch_shapes=[
            pltpu.VMEM((width, hidden), low),
            pltpu.VMEM((width, hidden), low),
            pltpu.VMEM((hidden, width), low),
            pltpu.VMEM((rows, width), low),
            pltpu.VMEM((SEQ, width), low),
            pltpu.VMEM((capacity, width), low),
            pltpu.VMEM((capacity, width), low),
            pltpu.VMEM((capacity, hidden), low),
            pltpu.VMEM((capacity, hidden), low),
            pltpu.VMEM((capacity, hidden), low),
            pltpu.VMEM((capacity, SEQ), low),
            pltpu.VMEM((SEQ, capacity), low),
            pltpu.VMEM((SEQ, SEQ), low),
            pltpu.VMEM((8, rows, width), low),
            pltpu.VMEM((SEQ, width), low),
            pltpu.VMEM((2, rows, width), low),
            pltpu.SemaphoreType.DMA((6,)),
            pltpu.SemaphoreType.DMA((4,)),
            pltpu.SemaphoreType.DMA((6,)),
            pltpu.SemaphoreType.DMA((8,)),
            pltpu.SemaphoreType.DMA((8,)),
            pltpu.SemaphoreType.DMA((8,)),
            pltpu.SemaphoreType.DMA((8,)),
            pltpu.SemaphoreType.DMA((4, 3)),
            pltpu.SemaphoreType.DMA((4, 3)),
            pltpu.SemaphoreType.DMA((4,)),
            pltpu.SemaphoreType.DMA((4,)),
        ],
        compiler_params=pltpu.CompilerParams(
            collective_id=0, has_side_effects=True, vmem_limit_bytes=67043328
        ),
        name="moe_layer",
    )(own, *weights, grads)


def local(
    tokens,
    lengths,
    routes,
    attn_gain,
    w_query,
    w_key,
    w_value,
    query_gain,
    key_gain,
    w_out,
    ffn_gain,
    w_router,
    w_gate,
    w_up,
    w_down,
    cotangent,
):
    grid = Grid(lax.axis_size("expert"))
    count = grid.count
    experts = w_router.shape[1]
    capacity = SEQ * TOP * 9 // (8 * experts)
    scale = 1.0 / math.sqrt(HD)
    low = jnp.bfloat16
    own_rows, width = w_query.shape
    heads_here = width // HD
    core = lax.axis_index("tensor")

    small = jnp.concatenate(
        [
            w_router.astype(low).T,
            jnp.pad(
                jnp.stack(
                    [
                        attn_gain.astype(low),
                        ffn_gain.astype(low),
                        jnp.pad(query_gain.astype(low), (0, own_rows - HD // count)),
                        jnp.pad(key_gain.astype(low), (0, own_rows - HD // count)),
                    ]
                ),
                ((0, experts - 4), (0, 0)),
            ),
        ],
        axis=1,
    )
    small = jnp.pad(small, ((0, 0), (0, width - 2 * own_rows)))
    mine = [w_query.astype(low), w_key.astype(low), w_value.astype(low), w_out.astype(low), small]
    halves = [w_gate[0].astype(low), w_up[0].astype(low), w_down[0].astype(low)]
    allowed = jnp.arange(SEQ) < lengths[0]
    grad_two_low = jnp.where(allowed[:, None], cotangent, 0)
    if grid.side == 2:
        wq_full, wk_full, wv_full, wo_full, smalls, grad_blocks, *others = gather_all(
            mine, grad_two_low, halves, count
        )
    else:
        whole = jnp.concatenate(mine, axis=0)
        arrived = []
        for top in range(PLANES):
            base = whole if top == 0 else grid.send(whole, (top * grid.plane,) * CORES)
            arrived += spread(grid, base)
        wq_full, wk_full, wv_full, wo_full, smalls = assemble(grid, arrived, own_rows, experts)
    router_t = smalls[:, :, :own_rows].transpose(1, 0, 2).reshape(experts, D)
    gain_one = smalls[:, 0, own_rows : 2 * own_rows].reshape(D).astype(jnp.float32)
    gain_two = smalls[:, 1, own_rows : 2 * own_rows].reshape(D).astype(jnp.float32)
    head_cols = slice(own_rows, own_rows + HD // count)
    gain_query = smalls[:, 2, head_cols].reshape(HD).astype(jnp.float32)
    gain_key = smalls[:, 3, head_cols].reshape(HD).astype(jnp.float32)

    grad_two = grad_two_low.astype(jnp.float32)

    cosine, sine_tab = rope_tables(SEQ, HD)
    resid_zero = tokens.astype(jnp.float32)
    normed_one, inverse_one = norm_stats(resid_zero)
    attn_in = (normed_one * gain_one).astype(low)
    query_lin = jnp.dot(attn_in, wq_full, preferred_element_type=jnp.float32).reshape(
        SEQ, heads_here, HD
    )
    key_lin = jnp.dot(attn_in, wk_full, preferred_element_type=jnp.float32).reshape(
        SEQ, heads_here, HD
    )
    values_b = (
        jnp.dot(attn_in, wv_full, preferred_element_type=jnp.float32)
        .astype(low)
        .reshape(SEQ, heads_here, HD)
    )
    query_hat, query_inv = norm_stats(query_lin)
    key_hat, key_inv = norm_stats(key_lin)
    queries = rotate(query_hat * gain_query, cosine, sine_tab).astype(low)
    keys_rot = rotate(key_hat * gain_key, cosine, sine_tab).astype(low)

    def masked_scores():
        scores = (
            jnp.einsum("qhd,khd->hqk", queries, keys_rot, preferred_element_type=jnp.float32)
            * scale
        )
        return jnp.where(allowed[None, None, :], scores, NEG_BIG)

    masked = masked_scores()
    top_score = jnp.max(masked, axis=-1, keepdims=True)
    expo_vals = jnp.exp(masked - top_score)
    totals = jnp.sum(expo_vals, axis=-1, keepdims=True)
    probs_low = (expo_vals / totals).astype(low)
    log_total = top_score + jnp.log(totals)
    mixed = (
        jnp.einsum("hqk,khd->qhd", probs_low, values_b, preferred_element_type=jnp.float32)
        .reshape(SEQ, heads_here * HD)
        .astype(low)
    )
    attn_part = contract_cols(mixed, wo_full)
    resid_one = resid_zero + (attn_part + swap(attn_part))
    normed_two, inverse_two = norm_stats(resid_one)
    ffn_in = (normed_two * gain_two).astype(low)
    logits = contract_cols(ffn_in, router_t)
    route_hot = routes[:, :, None] == jnp.arange(experts)[None, None, :]
    chosen = jnp.sum(jnp.where(route_hot, logits[:, None, :], 0.0), axis=2)
    gates = jax.nn.softmax(chosen, axis=1)
    gates_wide = jnp.sum(jnp.where(route_hot, gates[:, :, None], 0.0), axis=1)

    gate_rows = jnp.pad(split_three(gates_wide.T), ((0, 0), (0, D - 3 * SEQ)))
    token_block = jnp.concatenate([ffn_in, gate_rows], axis=0)
    if grid.side == 2:
        done = moe_layer(token_block, grad_blocks, halves + others, capacity)
        saved = [tuple(done[16:21])]
        sums_kept = [
            done[at].astype(jnp.float32) + done[part].astype(jnp.float32)
            for at, part in zip((4, 5, 0, 1), (10, 11, 8, 9))
        ]
        near = [grid.send(sums_kept[at].astype(low), grid.first(1)) for at in (1, 3)]
        back_sum = both_cores(done[21])
    else:
        wg, wu, wd = (
            jnp.concatenate([half, swap(half)], axis=axis) for half, axis in zip(halves, (1, 1, 0))
        )
        grad_turns = gather_tokens(grid, grad_two_low)
        token_turns = gather_tokens(grid, token_block)
        out_turns, back_turns, saved = [], [], []
        for turn in range(2):
            outs, backs, kept = expert_turn(
                token_turns[turn], grad_turns[turn], (wg, wu, wd), capacity
            )
            out_turns.append(outs)
            back_turns.append(backs)
            saved.append(kept)
        back_sum = scatter_tokens(grid, back_turns)

    def over_turns(left, right):
        return sum(contract_rows(kept[left], kept[right]) for kept in saved)

    half = w_gate.shape[2]
    gate_w = over_turns(0, 3)
    up_w = over_turns(0, 4)
    down_w = over_turns(2, 1)
    if grid.side == 2:
        back_sum, gate_w, up_w, down_w = lax.optimization_barrier((back_sum, gate_w, up_w, down_w))

    grad_gates_wide = join_three(back_sum[SEQ:], SEQ).T
    grad_gate_sel = jnp.sum(jnp.where(route_hot, grad_gates_wide[:, None, :], 0.0), axis=2)
    grad_chosen = gates * (grad_gate_sel - jnp.sum(gates * grad_gate_sel, axis=1, keepdims=True))
    grad_logits = jnp.sum(jnp.where(route_hot, grad_chosen[:, :, None], 0.0), axis=1).astype(low)
    grad_router_t = contract_rows(grad_logits, ffn_in)
    grad_ffn_in = back_sum[:SEQ] + jnp.dot(
        grad_logits, router_t, preferred_element_type=jnp.float32
    )
    grad_gain_two = jnp.sum(grad_ffn_in * normed_two, axis=0)
    grad_one = grad_two + norm_back(grad_ffn_in * gain_two, normed_two, inverse_two)
    grad_attn = grad_one.astype(low)

    part_wo = contract_rows(grad_attn, mixed)
    grad_mixed = (
        jnp.dot(grad_attn, wo_full, preferred_element_type=jnp.float32)
        .astype(low)
        .reshape(SEQ, heads_here, HD)
    )
    if grid.side == 2:
        near, grad_mixed = lax.optimization_barrier((near, grad_mixed))
        crossing = [
            grid.send((kept + part.astype(jnp.float32)).astype(low), grid.planes_of(turn))
            for kept, part, turn in zip(sums_kept[::2], near, (1, 0))
        ]
    masked = masked_scores()
    attn_probs = jnp.exp(masked - log_total)
    probs_again = attn_probs.astype(low)
    grad_probs = jnp.einsum(
        "qhd,khd->hqk", grad_mixed, values_b, preferred_element_type=jnp.float32
    )
    grad_values = jnp.einsum(
        "hqk,qhd->khd", probs_again, grad_mixed, preferred_element_type=jnp.float32
    )
    grad_value_lin = grad_values.astype(low).reshape(SEQ, heads_here * HD)
    part_wv = contract_rows(attn_in, grad_value_lin)
    grad_scores = (
        attn_probs * (grad_probs - jnp.sum(attn_probs * grad_probs, axis=-1, keepdims=True))
    ).astype(low)
    grad_queries = (
        jnp.einsum("hqk,khd->qhd", grad_scores, keys_rot, preferred_element_type=jnp.float32)
        * scale
    )
    grad_keys = (
        jnp.einsum("hqk,qhd->khd", grad_scores, queries, preferred_element_type=jnp.float32) * scale
    )
    grad_query_scaled = rotate_back(grad_queries, cosine, sine_tab)
    grad_key_scaled = rotate_back(grad_keys, cosine, sine_tab)
    grad_gain_query = jnp.sum(grad_query_scaled * query_hat, axis=(0, 1))
    grad_gain_key = jnp.sum(grad_key_scaled * key_hat, axis=(0, 1))
    grad_query_lin = (
        norm_back(grad_query_scaled * gain_query, query_hat, query_inv)
        .astype(low)
        .reshape(SEQ, heads_here * HD)
    )
    grad_key_lin = (
        norm_back(grad_key_scaled * gain_key, key_hat, key_inv)
        .astype(low)
        .reshape(SEQ, heads_here * HD)
    )
    part_wq = contract_rows(attn_in, grad_query_lin)
    part_wk = contract_rows(attn_in, grad_key_lin)
    grad_attn_part = (
        contract_cols(grad_query_lin, wq_full)
        + contract_cols(grad_key_lin, wk_full)
        + contract_cols(grad_value_lin, wv_full)
    ).astype(low)
    grad_attn_in = grad_attn_part.astype(jnp.float32) + swap(grad_attn_part).astype(jnp.float32)
    grad_gain_one = jnp.sum(grad_attn_in * normed_one, axis=0)
    grad_input = grad_one + norm_back(grad_attn_in * gain_one, normed_one, inverse_one)

    head_part = HD // count
    heads_row = jnp.stack([grad_gain_query, grad_gain_key]).reshape(2, count, head_part)
    heads_row = jnp.pad(heads_row, ((0, 0), (0, 0), (0, own_rows - head_part)))
    parts = jnp.concatenate(
        [
            jnp.concatenate([grad_router_t, grad_gain_one[None], grad_gain_two[None]]).reshape(
                experts + 2, count, own_rows
            ),
            heads_row,
        ],
        axis=0,
    ).transpose(1, 0, 2)
    weight_parts = [part_wq, part_wk, part_wv, part_wo]
    if grid.side == 2:
        weight_parts = [part.astype(low) for part in weight_parts]
        parts = jnp.pad(parts, ((0, 0), (0, 4), (0, 0)))
        grad_wq, grad_wk, grad_wv, grad_wo, sums, *received = reduce_all(
            weight_parts, parts, [gate_w, up_w, down_w], count
        )
        crossing, sums = lax.optimization_barrier((crossing, sums))
        out_sum = both_cores(
            (crossing[0].astype(jnp.float32) + crossing[1].astype(jnp.float32)).astype(low)
        )
    else:
        shape = (PLANES, grid.side, grid.side)
        grad_wq, grad_wk, grad_wv, grad_wo = [
            scatter_rows(grid, part.reshape(shape + (own_rows, width)), axes, low)
            for part, axes in zip(weight_parts, ((1, 2, 0), (2, 1, 0)) * 2)
        ]
        sums = scatter_rows(
            grid, parts.reshape(shape + (experts + 4, own_rows)), (1, 2, 0), jnp.float32
        )
        sums = sums + swap(sums)
        received = [swap(part) for part in (gate_w[:, half:], up_w[:, half:], down_w[half:])]
        out_sum = scatter_tokens(grid, out_turns)
    output = (resid_one + out_sum).astype(low)
    grad_gate_w = (gate_w[:, :half] + received[0])[None]
    grad_up_w = (up_w[:, :half] + received[1])[None]
    grad_down_w = (down_w[:half] + received[2])[None]
    return (
        output,
        grad_input.astype(low),
        0.5 * sums[experts],
        grad_wq,
        grad_wk,
        grad_wv,
        sums[experts + 2, :head_part],
        sums[experts + 3, :head_part],
        grad_wo,
        0.5 * sums[experts + 1],
        0.5 * sums[:experts].T,
        grad_gate_w,
        grad_up_w,
        grad_down_w,
    )


def solution(mesh):
    return jax.shard_map(
        local,
        mesh=mesh,
        in_specs=(
            P("expert", None),
            P("expert"),
            P("expert", None),
            P("expert"),
            P("expert", "tensor"),
            P("expert", "tensor"),
            P("expert", "tensor"),
            P("expert"),
            P("expert"),
            P("expert", "tensor"),
            P("expert"),
            P("expert", None),
            P("expert", None, "tensor"),
            P("expert", None, "tensor"),
            P("expert", "tensor", None),
            P("expert", None),
        ),
        out_specs=(
            P("expert", None),
            P("expert", None),
            P("expert"),
            P("expert", "tensor"),
            P("expert", "tensor"),
            P("expert", "tensor"),
            P("expert"),
            P("expert"),
            P("expert", "tensor"),
            P("expert"),
            P("expert", None),
            P("expert", None, "tensor"),
            P("expert", None, "tensor"),
            P("expert", "tensor", None),
        ),
        check_vma=False,
    )
```

```python
import functools
import math

import jax
import jax.numpy as jnp
from jax import lax
from jax.experimental import pallas as pl
from jax.experimental.pallas import tpu as pltpu
from jax.sharding import PartitionSpec as P

D = 2048
HD = 128
TOP = 8
SEQ = 512


EPSILON = 1e-06
ROPE_BASE = 10000.0
NEG_BIG = -1e30


def rope_tables(seq_len, head_dim):
    half_dim = head_dim // 2
    inverse = ROPE_BASE ** (-(jnp.arange(half_dim).astype(jnp.float32) * 2.0 / head_dim))
    angles = jnp.arange(seq_len).astype(jnp.float32)[:, None] * inverse[None, :]
    return (jnp.cos(angles), jnp.sin(angles))


def rotate(values, cosine, sine_tab):
    half_dim = values.shape[-1] // 2
    lower_half = values[..., :half_dim]
    upper_half = values[..., half_dim:]
    cos_b = cosine[:, None, :]
    sin_b = sine_tab[:, None, :]
    return jnp.concatenate(
        [lower_half * cos_b - upper_half * sin_b, upper_half * cos_b + lower_half * sin_b], axis=-1
    )


def rotate_back(grads_in, cosine, sine_tab):
    half_dim = grads_in.shape[-1] // 2
    lower_half = grads_in[..., :half_dim]
    upper_half = grads_in[..., half_dim:]
    cos_b = cosine[:, None, :]
    sin_b = sine_tab[:, None, :]
    return jnp.concatenate(
        [lower_half * cos_b + upper_half * sin_b, upper_half * cos_b - lower_half * sin_b], axis=-1
    )


def norm_stats(values):
    inverse = lax.rsqrt(jnp.mean(values * values, axis=-1, keepdims=True) + EPSILON)
    return (values * inverse, inverse)


def norm_back(grad_normed, normed, inverse):
    return inverse * (grad_normed - normed * jnp.mean(grad_normed * normed, axis=-1, keepdims=True))


def contract_rows(left_mat, right_mat):
    return lax.dot_general(
        left_mat, right_mat, (((0,), (0,)), ((), ())), preferred_element_type=jnp.float32
    )


def contract_cols(left_mat, right_mat):
    return lax.dot_general(
        left_mat, right_mat, (((1,), (1,)), ((), ())), preferred_element_type=jnp.float32
    )


PLANES = 4
CORES = 2


class Grid:
    def __init__(self, count):
        self.count = count
        self.plane = count // PLANES
        self.side = math.isqrt(self.plane)
        self.near = range(1, self.side)

    def first(self, step):
        return (step, step * self.side)

    def second(self, step):
        return (step * self.side, step)

    def planes_of(self, turn):
        return ((0, 3)[turn] * self.plane, (1, 2)[turn] * self.plane)

    def send(self, value, masks):
        pairs = [
            (device * CORES + core, (device ^ masks[core]) * CORES + core)
            for device in range(self.count)
            for core in range(CORES)
        ]
        return lax.ppermute(value, ("expert", "tensor"), pairs)


def swap(value):
    return lax.ppermute(value, "tensor", [(0, 1), (1, 0)])


def both_cores(part):
    return part.astype(jnp.float32) + swap(part).astype(jnp.float32)


def spread(grid, base):
    row = [base] + [grid.send(base, grid.first(step)) for step in grid.near]
    blocks = list(row)
    for step in grid.near:
        blocks += [grid.send(block, grid.second(step)) for block in row]
    return blocks


def gather_tokens(grid, block):
    return [spread(grid, grid.send(block, grid.planes_of(turn))) for turn in range(2)]


def collect(grid, blocks):
    side = grid.side
    sums = [block.astype(jnp.float32) for block in blocks[:side]]
    for far in grid.near:
        for step in range(side):
            sums[step] = sums[step] + grid.send(
                blocks[far * side + step], grid.second(far)
            ).astype(jnp.float32)
    total = sums[0]
    for step in grid.near:
        total = total + grid.send(sums[step].astype(jnp.bfloat16), grid.first(step)).astype(
            jnp.float32
        )
    return total


def scatter_tokens(grid, turns):
    total = None
    for turn in (1, 0):
        part = grid.send(collect(grid, turns[turn]).astype(jnp.bfloat16), grid.planes_of(turn))
        part = part.astype(jnp.float32)
        total = part if total is None else total + part
    return both_cores(total.astype(jnp.bfloat16))


def scatter_rows(grid, value, axes, wire):
    me = lax.axis_index("expert")
    units = (grid.plane, grid.side, 1)
    sizes = (PLANES, grid.side, grid.side)
    gone = []
    for axis in axes:
        unit, size = units[axis], sizes[axis]
        place = (me // unit) % size
        at = axis - sum(1 for other in gone if other < axis)
        total = lax.dynamic_index_in_dim(value, place, at, keepdims=False).astype(jnp.float32)
        for step in range(1, size):
            part = lax.dynamic_index_in_dim(value, place ^ step, at, keepdims=False).astype(wire)
            total = total + grid.send(part, (unit * step,) * CORES).astype(jnp.float32)
        value = total
        gone.append(axis)
    return value


def assemble(grid, blocks, rows, extra):
    count, width = grid.count, blocks[0].shape[1]
    me = lax.axis_index("expert")
    core = lax.axis_index("tensor")
    place = jnp.arange(count)
    top, mid, low = place // grid.plane, (place // grid.side) % grid.side, place % grid.side
    turned = top * grid.plane + low * grid.side + mid
    owner = me ^ jnp.where(core == 0, place, turned)

    def body(owner_ref, *refs):
        ins, outs, small, sem = refs[:count], refs[count : count + 4], refs[count + 4], refs[-1]
        copies = []
        for index in range(count):
            at = owner_ref[index]
            for which in range(4):
                copies.append(
                    pltpu.make_async_copy(
                        ins[index].at[pl.ds(which * rows, rows)],
                        outs[which].at[pl.ds(pl.multiple_of(at * rows, rows), rows)],
                        sem.at[index, which],
                    )
                )
            copies.append(
                pltpu.make_async_copy(
                    ins[index].at[pl.ds(4 * rows, extra)], small.at[at], sem.at[index, 4]
                )
            )
        for copy in copies:
            copy.start()
        for copy in copies:
            copy.wait()

    full = jax.ShapeDtypeStruct((count * rows, width), jnp.bfloat16)
    small = jax.ShapeDtypeStruct((count, extra, width), jnp.bfloat16)
    return pl.pallas_call(
        body,
        grid_spec=pltpu.PrefetchScalarGridSpec(
            num_scalar_prefetch=1,
            grid=(),
            in_specs=[pl.BlockSpec(memory_space=pl.ANY)] * count,
            out_specs=[pl.BlockSpec(memory_space=pltpu.VMEM)] * 5,
            scratch_shapes=[pltpu.SemaphoreType.DMA((count, 5))],
        ),
        out_shape=[full] * 4 + [small],
        name="assemble",
    )(owner, *blocks)


class Place:
    def __init__(self):
        self.me = me = lax.axis_index("expert")
        self.core = core = lax.axis_index("tensor")
        top, mid, low = me // 4, (me // 2) % 2, me % 2
        flip_low = me + 1 - 2 * low
        flip_mid = me + 2 - 4 * mid
        self.first = flip_low + core * (flip_mid - flip_low)
        self.second = flip_mid + core * (flip_low - flip_mid)
        self.planes = (
            me,
            me + 4 - 8 * (top % 2),
            me + 8 - 16 * (top // 2),
            me + 12 - 8 * top,
        )

    def owner(self, plane, far, near):
        return self.planes[plane] + far * (self.second - self.me) + near * (self.first - self.me)

    def greet(self, sibling):
        barrier = pltpu.get_barrier_semaphore()
        partners = [(device, self.core) for device in (self.first, self.second) + self.planes[1:]]
        if sibling:
            partners.append((self.me, 1 - self.core))
        for partner in partners:
            pl.semaphore_signal(
                barrier, inc=1, device_id=partner, device_id_type=pl.DeviceIdType.MESH
            )
        pl.semaphore_wait(barrier, len(partners))


def remote(source, target, send, recv, device):
    return pltpu.make_async_remote_copy(
        src_ref=source,
        dst_ref=target,
        send_sem=send,
        recv_sem=recv,
        device_id=device,
        device_id_type=pl.DeviceIdType.MESH,
    )


def gather_kernel(rows, *refs):
    mine, grad, halves, refs = refs[:5], refs[5], refs[6:9], refs[9:]
    full, grads, others, refs = refs[:5], refs[5], refs[6:9], refs[9:]
    send_sem, recv_sem, grad_send, grad_recv, half_send, half_recv, own_sem = refs
    place = Place()
    core = place.core
    place.greet(True)

    def part(which, plane, far, near):
        owner = place.owner(plane, far, near)
        if which == 4:
            return full[4].at[owner]
        return full[which].at[pl.ds(pl.multiple_of(owner * rows, rows), rows)]

    def pass_weights(source, plane, slot, device):
        out = []
        for which in range(5):
            here = part(which, *source)
            out.append(
                remote(
                    mine[which] if source == (0, 0, 0) else here,
                    here,
                    send_sem.at[4 * plane + slot, which],
                    recv_sem.at[4 * plane + slot, which],
                    (device, core),
                )
            )
        return out

    def start(copies):
        for copy in copies:
            copy.start()

    def arrived(plane, slot):
        for copy in pass_weights((plane, slot // 2, slot % 2), plane, slot, place.first):
            copy.wait_recv()

    def pass_grad(source, slot, device):
        return remote(
            source, grads.at[slot], grad_send.at[slot], grad_recv.at[slot], (device, core)
        )

    for plane in (1, 2, 3):
        start(pass_weights((0, 0, 0), plane, 0, place.planes[plane]))
    start(pass_weights((0, 0, 0), 0, 1, place.first))
    start(pass_weights((0, 0, 0), 0, 2, place.second))
    far_plane = place.planes[3] + core * (place.planes[2] - place.planes[3])

    @pl.when(core == 1)
    def _():
        pass_grad(grad, 0, place.planes[1]).start()

    pass_grad(grad, 4, far_plane).start()
    swaps = [
        remote(halves[i], others[i], half_send.at[i], half_recv.at[i], (place.me, 1 - core))
        for i in range(3)
    ]
    start(swaps)
    keeps = [
        pltpu.make_async_copy(mine[which], part(which, 0, 0, 0), own_sem.at[which])
        for which in range(5)
    ]
    start(keeps)

    @pl.when(core == 0)
    def _():
        pltpu.make_async_copy(grad, grads.at[0], own_sem.at[5]).start()

    for plane in range(4):
        if plane > 0:
            arrived(plane, 0)
            start(pass_weights((plane, 0, 0), plane, 1, place.first))
            start(pass_weights((plane, 0, 0), plane, 2, place.second))
        arrived(plane, 1)
        start(pass_weights((plane, 0, 1), plane, 3, place.second))

    @pl.when(core == 0)
    def _():
        pass_grad(grad, 1, place.first).start()
        pass_grad(grad, 2, place.second).start()

    @pl.when(core == 1)
    def _():
        pass_grad(grads.at[0], 0, place.first).wait_recv()
        pass_grad(grads.at[0], 1, place.first).start()
        pass_grad(grads.at[0], 2, place.second).start()

    pass_grad(grads.at[1], 1, place.first).wait_recv()
    pass_grad(grads.at[1], 3, place.second).start()
    pass_grad(grads.at[4], 4, place.first).wait_recv()
    pass_grad(grads.at[4], 5, place.first).start()
    pass_grad(grads.at[4], 6, place.second).start()
    pass_grad(grads.at[5], 5, place.first).wait_recv()
    pass_grad(grads.at[5], 7, place.second).start()

    for plane in range(4):
        arrived(plane, 2)
        arrived(plane, 3)
    for slot in (2, 3, 6, 7):
        pass_grad(grads.at[slot], slot, place.first).wait_recv()
    for slot in range(1, 16):
        for copy in pass_weights((slot // 4, 0, 0), slot // 4, slot % 4, place.first):
            copy.wait_send()
    for slot in range(1, 8):
        pass_grad(grads.at[slot], slot, place.first).wait_send()

    @pl.when(core == 1)
    def _():
        pass_grad(grads.at[0], 0, place.first).wait_send()

    @pl.when(core == 0)
    def _():
        pltpu.make_async_copy(grad, grads.at[0], own_sem.at[5]).wait()

    for copy in swaps + keeps:
        copy.wait()


def gather_all(mine, grad, halves, count):
    rows, width = mine[0].shape
    extra = mine[4].shape[0]
    low = jnp.bfloat16
    hbm = pl.BlockSpec(memory_space=pl.ANY)
    full = jax.ShapeDtypeStruct((count * rows, width), low)
    return pl.pallas_call(
        functools.partial(gather_kernel, rows),
        in_specs=[hbm] * 9,
        out_specs=[hbm] * 9,
        out_shape=[full] * 4
        + [
            jax.ShapeDtypeStruct((count, extra, width), low),
            jax.ShapeDtypeStruct((8,) + grad.shape, low),
        ]
        + [jax.ShapeDtypeStruct(half.shape, low) for half in halves],
        scratch_shapes=[
            pltpu.SemaphoreType.DMA((16, 5)),
            pltpu.SemaphoreType.DMA((16, 5)),
            pltpu.SemaphoreType.DMA((8,)),
            pltpu.SemaphoreType.DMA((8,)),
            pltpu.SemaphoreType.DMA((3,)),
            pltpu.SemaphoreType.DMA((3,)),
            pltpu.SemaphoreType.DMA((6,)),
        ],
        compiler_params=pltpu.CompilerParams(collective_id=1, has_side_effects=True),
        name="gather_all",
    )(*mine, grad, *halves)


def reduce_kernel(rows, *refs):
    whole, small, halves, refs = refs[:4], refs[4], refs[5:8], refs[8:]
    out, small_out, others, refs = refs[:4], refs[4], refs[5:8], refs[8:]
    (
        own,
        far_in,
        near_in,
        plane_in,
        near_stage,
        plane_stage,
        small_own,
        small_far,
        small_near,
        small_plane,
        small_near_stage,
        small_plane_stage,
        small_last,
        small_other,
        load_sem,
        far_send,
        far_recv,
        near_send,
        near_recv,
        plane_send,
        plane_recv,
        half_send,
        half_recv,
        last_send,
        last_recv,
    ) = refs
    place = Place()
    core = place.core
    sibling = (place.me, 1 - core)
    place.greet(True)
    second, first = (place.second, core), (place.first, core)

    def source(which, plane, far, near):
        owner = place.owner(plane, far, near)
        if which == 4:
            return small.at[owner]
        return whole[which].at[pl.ds(pl.multiple_of(owner * rows, rows), rows)]

    def load(which, plane, near):
        target = small_own.at[2 * plane + near] if which == 4 else own.at[2 * plane + near, which]
        return pltpu.make_async_copy(
            source(which, plane, 0, near), target, load_sem.at[2 * plane + near, which]
        )

    def to_second(which, plane, near):
        target = small_far.at[2 * plane + near]
        if which != 4:
            target = far_in.at[2 * plane + near, which]
        return remote(
            source(which, plane, 1, near),
            target,
            far_send.at[2 * plane + near, which],
            far_recv.at[2 * plane + near, which],
            second,
        )

    def to_first(which, plane):
        here, there = small_near_stage.at[plane], small_near.at[plane]
        if which is not None:
            here, there = near_stage.at[plane, which], near_in.at[plane, which]
        at = 4 if which is None else which
        return remote(here, there, near_send.at[plane, at], near_recv.at[plane, at], first)

    def to_plane(which, plane):
        here, there = small_plane_stage.at[plane - 1], small_plane.at[plane - 1]
        if which is not None:
            here, there = plane_stage.at[plane - 1, which], plane_in.at[plane - 1, which]
        at = 4 if which is None else which
        return remote(
            here,
            there,
            plane_send.at[plane - 1, at],
            plane_recv.at[plane - 1, at],
            (place.planes[plane], core),
        )

    for plane in (3, 2, 1, 0):
        for near in (1, 0):
            for which in range(5):
                to_second(which, plane, near).start()
    for plane in (3, 2, 1, 0):
        for near in (1, 0):
            for which in range(5):
                load(which, plane, near).start()
    middle = others[0].shape[1]
    theirs = [
        halves[0].at[:, pl.ds(middle, middle)],
        halves[1].at[:, pl.ds(middle, middle)],
        halves[2].at[pl.ds(middle, middle)],
    ]
    swaps = [
        remote(theirs[i], others[i], half_send.at[i], half_recv.at[i], sibling) for i in range(3)
    ]
    for copy in swaps:
        copy.start()

    def added(parts, target):
        total = parts[0].astype(jnp.float32)
        for value in parts[1:]:
            total = total + value.astype(jnp.float32)
        return total.astype(target.dtype)

    def over_rows(parts, target):
        def body(step, carry):
            span = pl.ds(pl.multiple_of(step * 16, 16), 16)
            target[span, :] = added([part[span, :] for part in parts], target)
            return carry

        lax.fori_loop(0, rows // 16, body, 0)

    def near_sums(plane):
        for which in range(4):
            load(which, plane, 1).wait()
            to_second(which, plane, 1).wait_recv()
            over_rows(
                [own.at[2 * plane + 1, which], far_in.at[2 * plane + 1, which]],
                near_stage.at[plane, which],
            )
            to_first(which, plane).start()
        load(4, plane, 1).wait()
        to_second(4, plane, 1).wait_recv()
        small_near_stage[plane] = small_own[2 * plane + 1] + small_far[2 * plane + 1]
        to_first(None, plane).start()

    def plane_sums(plane):
        for which in range(4):
            load(which, plane, 0).wait()
            to_second(which, plane, 0).wait_recv()
            to_first(which, plane).wait_recv()
            over_rows(
                [
                    own.at[2 * plane, which],
                    far_in.at[2 * plane, which],
                    near_in.at[plane, which],
                ],
                plane_stage.at[plane - 1, which],
            )
            to_plane(which, plane).start()
        load(4, plane, 0).wait()
        to_second(4, plane, 0).wait_recv()
        to_first(None, plane).wait_recv()
        small_plane_stage[plane - 1] = (
            small_own[2 * plane] + small_far[2 * plane] + small_near[plane]
        )
        to_plane(None, plane).start()

    near_sums(3)
    near_sums(2)
    plane_sums(3)
    near_sums(1)
    plane_sums(2)
    near_sums(0)
    plane_sums(1)
    load(4, 0, 0).wait()
    to_second(4, 0, 0).wait_recv()
    to_first(None, 0).wait_recv()
    for plane in (1, 2, 3):
        to_plane(None, plane).wait_recv()
    small_last[...] = (
        small_own[0]
        + small_far[0]
        + small_near[0]
        + small_plane[0]
        + small_plane[1]
        + small_plane[2]
    )
    last = remote(small_last, small_other, last_send.at[0], last_recv.at[0], sibling)
    last.start()
    for which in range(4):
        load(which, 0, 0).wait()
        to_second(which, 0, 0).wait_recv()
        to_first(which, 0).wait_recv()
        for plane in (1, 2, 3):
            to_plane(which, plane).wait_recv()
        over_rows(
            [own.at[0, which], far_in.at[0, which], near_in.at[0, which]]
            + [plane_in.at[plane, which] for plane in range(3)],
            out[which],
        )
    last.wait()
    small_out[...] = small_last[...] + small_other[...]
    for plane in range(4):
        for which in range(5):
            at = None if which == 4 else which
            for near in range(2):
                to_second(which, plane, near).wait_send()
            to_first(at, plane).wait_send()
            if plane > 0:
                to_plane(at, plane).wait_send()
    for copy in swaps:
        copy.wait()


def reduce_all(whole, small, halves, count):
    rows, width = whole[0].shape[0] // count, whole[0].shape[1]
    low = jnp.bfloat16
    hbm = pl.BlockSpec(memory_space=pl.ANY)
    vmem = pl.BlockSpec(memory_space=pltpu.VMEM)
    tiny = small.shape[1:]

    def wide(*dims):
        return pltpu.VMEM(dims + (rows, width), low)

    def little(*dims):
        return pltpu.VMEM(dims + tiny, jnp.float32)

    def sems(*dims):
        return pltpu.SemaphoreType.DMA(dims)

    return pl.pallas_call(
        functools.partial(reduce_kernel, rows),
        in_specs=[hbm] * 8,
        out_specs=[vmem] * 5 + [hbm] * 3,
        out_shape=[jax.ShapeDtypeStruct((rows, width), jnp.float32)] * 4
        + [jax.ShapeDtypeStruct(tiny, jnp.float32)]
        + [
            jax.ShapeDtypeStruct((dims[0] // cut, dims[1] // (3 - cut)), jnp.float32)
            for dims, cut in ((halves[0].shape, 1), (halves[1].shape, 1), (halves[2].shape, 2))
        ],
        scratch_shapes=[wide(8, 4), wide(8, 4), wide(4, 4), wide(3, 4), wide(4, 4), wide(3, 4)]
        + [little(8), little(8), little(4), little(3), little(4), little(3), little(), little()]
        + [sems(8, 5)] * 3
        + [sems(4, 5)] * 2
        + [sems(3, 5)] * 2
        + [sems(3)] * 2
        + [sems(1)] * 2,
        compiler_params=pltpu.CompilerParams(
            collective_id=2, has_side_effects=True, vmem_limit_bytes=60 * 1024 * 1024
        ),
        name="reduce_all",
    )(*whole, small, *halves)


def split_three(value):
    high = value.astype(jnp.bfloat16)
    rest = value - high.astype(jnp.float32)
    middle = rest.astype(jnp.bfloat16)
    low = (rest - middle.astype(jnp.float32)).astype(jnp.bfloat16)
    return jnp.concatenate([high, middle, low], axis=-1)


def join_three(parts, length):
    parts = parts.astype(jnp.float32)
    return (
        parts[..., :length] + parts[..., length : 2 * length] + parts[..., 2 * length : 3 * length]
    )


def expert_turn(blocks, grads, weights, capacity):
    wg, wu, wd = weights
    me = lax.axis_index("expert")
    experts = blocks[0].shape[0] - SEQ
    gate = jnp.concatenate(
        [
            join_three(lax.dynamic_slice(block, (SEQ + me, 0), (1, 3 * SEQ)), SEQ)
            for block in blocks
        ],
        axis=0,
    )
    used = gate > 0.0
    ordered = (jnp.arange(SEQ)[:, None] < jnp.arange(SEQ)[None, :]).astype(jnp.bfloat16)
    slot = jnp.dot(used.astype(jnp.bfloat16), ordered, preferred_element_type=jnp.float32)
    slot = slot.astype(jnp.int32)
    hot = (jnp.arange(capacity)[None, :, None] == slot[:, None, :]) & used[:, None, :]
    pick = hot.astype(jnp.bfloat16)
    slot_gate = jnp.sum(jnp.where(hot, gate[:, None, :], 0.0), axis=2).reshape(-1, 1)
    rows = jnp.concatenate(
        [
            jnp.dot(pick[i], block[:SEQ], preferred_element_type=jnp.float32).astype(jnp.bfloat16)
            for i, block in enumerate(blocks)
        ],
        axis=0,
    )
    grad_rows = jnp.concatenate(
        [
            jnp.dot(pick[i], block, preferred_element_type=jnp.float32).astype(jnp.bfloat16)
            for i, block in enumerate(grads)
        ],
        axis=0,
    )
    gate_lin = jnp.dot(rows, wg, preferred_element_type=jnp.float32)
    up_lin = jnp.dot(rows, wu, preferred_element_type=jnp.float32)
    grad_full = contract_cols(grad_rows, wd)
    sigmoid_gate = jax.nn.sigmoid(gate_lin)
    activated = gate_lin * sigmoid_gate
    hidden = activated * up_lin
    hidden_low = (hidden * slot_gate).astype(jnp.bfloat16)
    slot_grad = jnp.sum(hidden * grad_full, axis=1).reshape(len(blocks), capacity, 1)
    grad_hidden = grad_full * slot_gate
    silu_slope = sigmoid_gate * (1.0 + gate_lin * (1.0 - sigmoid_gate))
    grad_gate = (grad_hidden * up_lin * silu_slope).astype(jnp.bfloat16)
    grad_up = (grad_hidden * activated).astype(jnp.bfloat16)
    value = jnp.dot(hidden_low, wd, preferred_element_type=jnp.float32).astype(jnp.bfloat16)
    grad_in = (contract_cols(grad_gate, wg) + contract_cols(grad_up, wu)).astype(jnp.bfloat16)
    token_grad = split_three(jnp.sum(jnp.where(hot, slot_grad, 0.0), axis=1))
    outs, backs = [], []
    for i in range(len(blocks)):
        span = slice(i * capacity, (i + 1) * capacity)
        outs.append(contract_rows(pick[i], value[span]).astype(jnp.bfloat16))
        back = contract_rows(pick[i], grad_in[span]).astype(jnp.bfloat16)
        extra = jnp.where(
            (jnp.arange(experts) == me)[:, None],
            jnp.pad(token_grad[i : i + 1], ((0, 0), (0, D - 3 * SEQ))),
            0,
        )
        backs.append(jnp.concatenate([back, extra], axis=0))
    return outs, backs, (rows, grad_rows, hidden_low, grad_gate, grad_up)


def moe_kernel(
    capacity,
    experts,
    own,
    *refs,
):
    weights, grads, refs = refs[:6], refs[6], refs[7:]
    parts, outs, refs = refs[:8], refs[8:12], refs[12:]
    (
    blocks,
    far_sums,
    near_sums,
    plane_sums,
    rows_out,
    grows_out,
    hidden_out,
    gate_out,
    up_out,
    result,
    wg_v,
    wu_v,
    wd_v,
    block_v,
    grad_v,
    rows_v,
    grows_v,
    hidden_v,
    gate_v,
    up_v,
    pick_v,
    pick_t,
    ordered,
    stage,
    part_v,
    taken,
    weight_sem,
    load_sem,
    save_sem,
    send_sem,
    recv_sem,
    back_send,
    back_recv,
    piece_send,
    piece_recv,
    out_send,
    out_recv,
    ) = refs
    me = lax.axis_index("expert")
    core = lax.axis_index("tensor")
    top, mid, low = me // 4, (me // 2) % 2, me % 2
    flip_low = me + 1 - 2 * low
    flip_mid = me + 2 - 4 * mid
    first = flip_low + core * (flip_mid - flip_low)
    second = flip_mid + core * (flip_low - flip_mid)
    plane_one = me + 4 - 8 * (top % 2)
    plane_two = me + 8 - 16 * (top // 2)
    plane_three = me + 12 - 8 * top
    far_plane = plane_three + core * (plane_two - plane_three)
    mesh = pl.DeviceIdType.MESH

    barrier = pltpu.get_barrier_semaphore()
    for device in (first, second, plane_one, plane_two, plane_three):
        pl.semaphore_signal(barrier, inc=1, device_id=(device, core), device_id_type=mesh)
    pl.semaphore_wait(barrier, 5)

    def pass_on(source, slot, device):
        return pltpu.make_async_remote_copy(
            src_ref=source,
            dst_ref=blocks.at[slot],
            send_sem=send_sem.at[slot],
            recv_sem=recv_sem.at[slot],
            device_id=(device, core),
            device_id_type=mesh,
        )

    def give(source, target, index, device):
        return pltpu.make_async_remote_copy(
            src_ref=source,
            dst_ref=target,
            send_sem=back_send.at[index],
            recv_sem=back_recv.at[index],
            device_id=(device, core),
            device_id_type=mesh,
        )

    half = wg_v.shape[1] // 2
    targets = []
    for span in (slice(0, half), slice(half, 2 * half)):
        targets += [wg_v.at[:, span], wu_v.at[:, span], wd_v.at[span]]
    loads = [
        pltpu.make_async_copy(source, target, weight_sem.at[index])
        for index, (source, target) in enumerate(zip(weights, targets))
    ]

    @pl.when(core == 0)
    def _():
        pass_on(own, 1, first).start()
        pass_on(own, 2, second).start()

    @pl.when(core == 1)
    def _():
        pass_on(own, 0, plane_one).start()

    pass_on(own, 4, far_plane).start()
    for copy in loads:
        copy.start()

    length = SEQ
    ordered[...] = jnp.where(
        lax.broadcasted_iota(jnp.int32, (length, length), 0)
        < lax.broadcasted_iota(jnp.int32, (length, length), 1),
        1.0,
        0.0,
    ).astype(jnp.bfloat16)
    width = block_v.shape[1]
    hidden = hidden_v.shape[1]
    both = (((1,), (1,)), ((), ()))

    def dot(left, right):
        return jnp.dot(left, right, preferred_element_type=jnp.float32)

    def dot_t(left, right):
        return lax.dot_general(left, right, both, preferred_element_type=jnp.float32)

    def add_block(slot, sources, start=0, size=length + experts):
        part = pl.ds(start, size)
        copies = [
            pltpu.make_async_copy(source.at[part], taken.at[index, part], load_sem.at[2 + index])
            for index, source in enumerate(sources)
        ]
        for copy in copies:
            copy.start()
        for copy in copies:
            copy.wait()

        def rows_of(step, carry):
            span = pl.ds(pl.multiple_of(start + step * 16, 16), 16)
            total = stage[slot, span, :].astype(jnp.float32)
            for index in range(len(sources)):
                total = total + taken[index, span, :].astype(jnp.float32)
            stage[slot, span, :] = total.astype(jnp.bfloat16)
            return carry

        lax.fori_loop(0, size // 16, rows_of, 0)

    pieces = 3
    size = (length + experts) // pieces

    def give_piece(source, target, kind, piece, device):
        part = pl.ds(piece * size, size)
        return pltpu.make_async_remote_copy(
            src_ref=source.at[part],
            dst_ref=target.at[part],
            send_sem=piece_send.at[kind, piece],
            recv_sem=piece_recv.at[kind, piece],
            device_id=(device, core),
            device_id_type=mesh,
        )

    def far_piece(which, piece):
        return give_piece(stage.at[6 + which], far_sums.at[2 + which], which, piece, second)

    def near_piece(piece):
        return give_piece(stage.at[5], near_sums.at[1], 2, piece, first)

    def plane_piece(piece):
        return give_piece(stage.at[4], plane_sums.at[1], 3, piece, far_plane)

    def send_out(index):
        return pltpu.make_async_remote_copy(
            src_ref=parts[(2, 3, 6, 7)[index]],
            dst_ref=outs[index],
            send_sem=out_send.at[index],
            recv_sem=out_recv.at[index],
            device_id=(second, core),
            device_id_type=mesh,
        )

    def first_sum(turn):
        give(far_sums.at[2 * turn + 1], far_sums.at[2 * turn + 1], 2 * turn + 1, second).wait_recv()
        add_block(4 * turn + 1, [far_sums.at[2 * turn + 1]])
        give(stage.at[4 * turn + 1], near_sums.at[turn], 4 + turn, first).start()

    def plane_sum(turn):
        give(far_sums.at[2 * turn], far_sums.at[2 * turn], 2 * turn, second).wait_recv()
        give(near_sums.at[turn], near_sums.at[turn], 4 + turn, first).wait_recv()
        add_block(4 * turn, [far_sums.at[2 * turn], near_sums.at[turn]])

    def block_step(k, carry):
        turn_at = k % 4
        relayed = jnp.logical_or(k != 0, core != 0)

        @pl.when(relayed)
        def _():
            pass_on(blocks.at[k], k, first).wait_recv()
            pltpu.make_async_copy(blocks.at[k], block_v, load_sem.at[0]).start()

        @pl.when(jnp.logical_not(relayed))
        def _():
            pltpu.make_async_copy(own, block_v, load_sem.at[0]).start()

        @pl.when(jnp.logical_and(relayed, turn_at == 0))
        def _():
            pass_on(blocks.at[k], k + 1, first).start()

        @pl.when(jnp.logical_and(relayed, turn_at < 2))
        def _():
            pass_on(blocks.at[k], k + 2, second).start()

        pltpu.make_async_copy(grads.at[k], grad_v, load_sem.at[1]).start()

        @pl.when(k == 0)
        def _():
            for copy in loads:
                copy.wait()

        pltpu.make_async_copy(blocks.at[k], block_v, load_sem.at[0]).wait()

        here = lax.broadcasted_iota(jnp.int32, (experts, 3 * length), 0) == me
        row = jnp.sum(
            jnp.where(here, block_v[length:, : 3 * length].astype(jnp.float32), 0.0),
            axis=0,
            keepdims=True,
        )
        gate = row[:, :length] + row[:, length : 2 * length] + row[:, 2 * length :]
        used = jnp.where(gate > 0.0, 1.0, 0.0)
        slot = dot(jnp.broadcast_to(used, (16, length)).astype(jnp.bfloat16), ordered[...])[:1]
        slot = jnp.where(gate > 0.0, slot, -1.0)
        number = lax.broadcasted_iota(jnp.int32, (capacity, length), 0).astype(jnp.float32)
        pick = jnp.where(number == slot, 1.0, 0.0)
        slot_gate = jnp.sum(pick * gate, axis=1, keepdims=True)
        pick_v[...] = pick.astype(jnp.bfloat16)
        pick_t[...] = pick.T.astype(jnp.bfloat16)
        for at in range(0, width, 512):
            span = slice(at, at + 512)
            rows_v[:, span] = dot(pick_v[...], block_v[:length, span]).astype(jnp.bfloat16)
        pltpu.make_async_copy(grads.at[k], grad_v, load_sem.at[1]).wait()
        for at in range(0, width, 512):
            span = slice(at, at + 512)
            grows_v[:, span] = dot(pick_v[...], grad_v[:, span]).astype(jnp.bfloat16)
        slot_grad = jnp.zeros((capacity, 1), jnp.float32)
        for at in range(0, hidden, 256):
            span = slice(at, at + 256)
            gate_lin = dot(rows_v[...], wg_v[:, span])
            up_lin = dot(rows_v[...], wu_v[:, span])
            grad_full = dot_t(grows_v[...], wd_v[span, :])
            sigmoid_gate = 1.0 / (1.0 + jnp.exp(-gate_lin))
            activated = gate_lin * sigmoid_gate
            value = activated * up_lin
            hidden_v[:, span] = (value * slot_gate).astype(jnp.bfloat16)
            slot_grad = slot_grad + jnp.sum(value * grad_full, axis=1, keepdims=True)
            grad_hidden = grad_full * slot_gate
            slope = sigmoid_gate * (1.0 + gate_lin * (1.0 - sigmoid_gate))
            gate_v[:, span] = (grad_hidden * up_lin * slope).astype(jnp.bfloat16)
            up_v[:, span] = (grad_hidden * activated).astype(jnp.bfloat16)
        at = pl.multiple_of(k * capacity, capacity)
        saves = [
            pltpu.make_async_copy(source, target.at[pl.ds(at, capacity)], save_sem.at[index])
            for index, (source, target) in enumerate(
                (
                    (rows_v, rows_out),
                    (grows_v, grows_out),
                    (hidden_v, hidden_out),
                    (gate_v, gate_out),
                    (up_v, up_out),
                )
            )
        ]
        for copy in saves:
            copy.start()

        for index in range(8):

            @pl.when(k == index + 1)
            def _():
                pltpu.make_async_copy(part_v, parts[index], save_sem.at[5]).wait()

        for index in range(2):

            @pl.when(k == 3 + index)
            def _():
                send_out(index).start()

        for at in range(0, width, 512):
            span = slice(at, at + 512)
            value = dot(hidden_v[...], wd_v[:, span]).astype(jnp.bfloat16)
            part_v[:, span] = dot(pick_t[...], value).astype(jnp.bfloat16)
            back = dot_t(gate_v[...], wg_v[span, :]) + dot_t(up_v[...], wu_v[span, :])
            stage[k, :length, span] = dot(pick_t[...], back.astype(jnp.bfloat16)).astype(
                jnp.bfloat16
            )
        total = jnp.sum(pick_v[...].astype(jnp.float32) * slot_grad, axis=0, keepdims=True)
        here = lax.broadcasted_iota(jnp.int32, (experts, length), 0) == me
        for index in range(3):
            high = total.astype(jnp.bfloat16).astype(jnp.float32)
            stage[k, length:, index * length : (index + 1) * length] = jnp.where(
                here, high, 0.0
            ).astype(jnp.bfloat16)
            total = total - high
        stage[k, length:, 3 * length :] = jnp.zeros((experts, width - 3 * length), jnp.bfloat16)
        for index in range(8):

            @pl.when(k == index)
            def _():
                pltpu.make_async_copy(part_v, parts[index], save_sem.at[5]).start()

        @pl.when(jnp.logical_and(turn_at >= 2, k < 4))
        def _():
            index = turn_at - 2
            give(stage.at[k], far_sums.at[index], index, second).start()

        for which in range(2):

            @pl.when(k == 6 + which)
            def _():
                for piece in range(pieces):
                    far_piece(which, piece).start()

        @pl.when(k == 5)
        def _():
            first_sum(0)

        @pl.when(k == 6)
        def _():
            plane_sum(0)

            @pl.when(core == 1)
            def _():
                give(stage.at[0], plane_sums.at[0], 6, plane_one).start()

        for copy in saves:
            copy.wait()
        return carry

    lax.fori_loop(0, 8, block_step, 0)
    pltpu.make_async_copy(part_v, parts[7], save_sem.at[5]).wait()
    send_out(2).start()
    send_out(3).start()
    for piece in range(pieces):
        far_piece(1, piece).wait_recv()
        add_block(5, [far_sums.at[3]], piece * size, size)
        near_piece(piece).start()
    for piece in range(pieces):
        far_piece(0, piece).wait_recv()
        near_piece(piece).wait_recv()
        add_block(4, [far_sums.at[2], near_sums.at[1]], piece * size, size)
        plane_piece(piece).start()

    @pl.when(core == 1)
    def _():
        give(stage.at[0], plane_sums.at[0], 6, plane_one).wait()
        pltpu.make_async_copy(plane_sums.at[0], stage.at[0], load_sem.at[0]).start()
        pltpu.make_async_copy(plane_sums.at[0], stage.at[0], load_sem.at[0]).wait()

    for piece in range(pieces):
        plane_piece(piece).wait_recv()
        add_block(0, [plane_sums.at[1]], piece * size, size)
    final = pltpu.make_async_copy(stage.at[0], result, load_sem.at[0])
    final.start()
    for index in range(4):
        send_out(index).wait()
    for k in range(8):
        if k > 0:
            pass_on(blocks.at[k], k, first).wait_send()
    @pl.when(core == 1)
    def _():
        pass_on(blocks.at[0], 0, first).wait_send()

    for index in (0, 1, 4):
        give(result, result, index, first).wait_send()
    for piece in range(pieces):
        for which in range(2):
            far_piece(which, piece).wait_send()
        near_piece(piece).wait_send()
        plane_piece(piece).wait_send()
    final.wait()


def moe_layer(own, grads, weights, capacity):
    rows, width = own.shape
    hidden = 2 * weights[0].shape[1]
    experts = rows - SEQ
    low = jnp.bfloat16
    hbm = pl.BlockSpec(memory_space=pl.ANY)

    def shape(*dims):
        return jax.ShapeDtypeStruct(dims, low)

    return pl.pallas_call(
        functools.partial(moe_kernel, capacity, experts),
        in_specs=[hbm] * 8,
        out_specs=[hbm] * 22,
        out_shape=[shape(SEQ, width)] * 12
        + [
            shape(8, rows, width),
            shape(4, rows, width),
            shape(2, rows, width),
            shape(2, rows, width),
            shape(8 * capacity, width),
            shape(8 * capacity, width),
            shape(8 * capacity, hidden),
            shape(8 * capacity, hidden),
            shape(8 * capacity, hidden),
            shape(rows, width),
        ],
        scratch_shapes=[
            pltpu.VMEM((width, hidden), low),
            pltpu.VMEM((width, hidden), low),
            pltpu.VMEM((hidden, width), low),
            pltpu.VMEM((rows, width), low),
            pltpu.VMEM((SEQ, width), low),
            pltpu.VMEM((capacity, width), low),
            pltpu.VMEM((capacity, width), low),
            pltpu.VMEM((capacity, hidden), low),
            pltpu.VMEM((capacity, hidden), low),
            pltpu.VMEM((capacity, hidden), low),
            pltpu.VMEM((capacity, SEQ), low),
            pltpu.VMEM((SEQ, capacity), low),
            pltpu.VMEM((SEQ, SEQ), low),
            pltpu.VMEM((8, rows, width), low),
            pltpu.VMEM((SEQ, width), low),
            pltpu.VMEM((2, rows, width), low),
            pltpu.SemaphoreType.DMA((6,)),
            pltpu.SemaphoreType.DMA((4,)),
            pltpu.SemaphoreType.DMA((6,)),
            pltpu.SemaphoreType.DMA((8,)),
            pltpu.SemaphoreType.DMA((8,)),
            pltpu.SemaphoreType.DMA((8,)),
            pltpu.SemaphoreType.DMA((8,)),
            pltpu.SemaphoreType.DMA((4, 3)),
            pltpu.SemaphoreType.DMA((4, 3)),
            pltpu.SemaphoreType.DMA((4,)),
            pltpu.SemaphoreType.DMA((4,)),
        ],
        compiler_params=pltpu.CompilerParams(
            collective_id=0, has_side_effects=True, vmem_limit_bytes=67043328
        ),
        name="moe_layer",
    )(own, *weights, grads)


def local(
    tokens,
    lengths,
    routes,
    attn_gain,
    w_query,
    w_key,
    w_value,
    query_gain,
    key_gain,
    w_out,
    ffn_gain,
    w_router,
    w_gate,
    w_up,
    w_down,
    cotangent,
):
    grid = Grid(lax.axis_size("expert"))
    count = grid.count
    experts = w_router.shape[1]
    capacity = SEQ * TOP * 9 // (8 * experts)
    scale = 1.0 / math.sqrt(HD)
    low = jnp.bfloat16
    own_rows, width = w_query.shape
    heads_here = width // HD
    core = lax.axis_index("tensor")

    small = jnp.concatenate(
        [
            w_router.astype(low).T,
            jnp.pad(
                jnp.stack(
                    [
                        attn_gain.astype(low),
                        ffn_gain.astype(low),
                        jnp.pad(query_gain.astype(low), (0, own_rows - HD // count)),
                        jnp.pad(key_gain.astype(low), (0, own_rows - HD // count)),
                    ]
                ),
                ((0, experts - 4), (0, 0)),
            ),
        ],
        axis=1,
    )
    small = jnp.pad(small, ((0, 0), (0, width - 2 * own_rows)))
    mine = [w_query.astype(low), w_key.astype(low), w_value.astype(low), w_out.astype(low), small]
    halves = [w_gate[0].astype(low), w_up[0].astype(low), w_down[0].astype(low)]
    allowed = jnp.arange(SEQ) < lengths[0]
    grad_two_low = jnp.where(allowed[:, None], cotangent, 0)
    if grid.side == 2:
        wq_full, wk_full, wv_full, wo_full, smalls, grad_blocks, *others = gather_all(
            mine, grad_two_low, halves, count
        )
    else:
        whole = jnp.concatenate(mine, axis=0)
        arrived = []
        for top in range(PLANES):
            base = whole if top == 0 else grid.send(whole, (top * grid.plane,) * CORES)
            arrived += spread(grid, base)
        wq_full, wk_full, wv_full, wo_full, smalls = assemble(grid, arrived, own_rows, experts)
    router_t = smalls[:, :, :own_rows].transpose(1, 0, 2).reshape(experts, D)
    gain_one = smalls[:, 0, own_rows : 2 * own_rows].reshape(D).astype(jnp.float32)
    gain_two = smalls[:, 1, own_rows : 2 * own_rows].reshape(D).astype(jnp.float32)
    head_cols = slice(own_rows, own_rows + HD // count)
    gain_query = smalls[:, 2, head_cols].reshape(HD).astype(jnp.float32)
    gain_key = smalls[:, 3, head_cols].reshape(HD).astype(jnp.float32)

    grad_two = grad_two_low.astype(jnp.float32)

    cosine, sine_tab = rope_tables(SEQ, HD)
    resid_zero = tokens.astype(jnp.float32)
    normed_one, inverse_one = norm_stats(resid_zero)
    attn_in = (normed_one * gain_one).astype(low)
    query_lin = jnp.dot(attn_in, wq_full, preferred_element_type=jnp.float32).reshape(
        SEQ, heads_here, HD
    )
    key_lin = jnp.dot(attn_in, wk_full, preferred_element_type=jnp.float32).reshape(
        SEQ, heads_here, HD
    )
    values_b = (
        jnp.dot(attn_in, wv_full, preferred_element_type=jnp.float32)
        .astype(low)
        .reshape(SEQ, heads_here, HD)
    )
    query_hat, query_inv = norm_stats(query_lin)
    key_hat, key_inv = norm_stats(key_lin)
    queries = rotate(query_hat * gain_query, cosine, sine_tab).astype(low)
    keys_rot = rotate(key_hat * gain_key, cosine, sine_tab).astype(low)

    def masked_scores():
        scores = (
            jnp.einsum("qhd,khd->hqk", queries, keys_rot, preferred_element_type=jnp.float32)
            * scale
        )
        return jnp.where(allowed[None, None, :], scores, NEG_BIG)

    masked = masked_scores()
    top_score = jnp.max(masked, axis=-1, keepdims=True)
    expo_vals = jnp.exp(masked - top_score)
    totals = jnp.sum(expo_vals, axis=-1, keepdims=True)
    probs_low = (expo_vals / totals).astype(low)
    log_total = top_score + jnp.log(totals)
    mixed = (
        jnp.einsum("hqk,khd->qhd", probs_low, values_b, preferred_element_type=jnp.float32)
        .reshape(SEQ, heads_here * HD)
        .astype(low)
    )
    attn_part = contract_cols(mixed, wo_full)
    resid_one = resid_zero + (attn_part + swap(attn_part))
    normed_two, inverse_two = norm_stats(resid_one)
    ffn_in = (normed_two * gain_two).astype(low)
    logits = contract_cols(ffn_in, router_t)
    route_hot = routes[:, :, None] == jnp.arange(experts)[None, None, :]
    chosen = jnp.sum(jnp.where(route_hot, logits[:, None, :], 0.0), axis=2)
    gates = jax.nn.softmax(chosen, axis=1)
    gates_wide = jnp.sum(jnp.where(route_hot, gates[:, :, None], 0.0), axis=1)

    gate_rows = jnp.pad(split_three(gates_wide.T), ((0, 0), (0, D - 3 * SEQ)))
    token_block = jnp.concatenate([ffn_in, gate_rows], axis=0)
    if grid.side == 2:
        done = moe_layer(token_block, grad_blocks, halves + others, capacity)
        saved = [tuple(done[16:21])]
        sums_kept = [
            done[at].astype(jnp.float32) + done[part].astype(jnp.float32)
            for at, part in zip((4, 5, 0, 1), (10, 11, 8, 9))
        ]
        near = [grid.send(sums_kept[at].astype(low), grid.first(1)) for at in (1, 3)]
        back_sum = both_cores(done[21])
    else:
        wg, wu, wd = (
            jnp.concatenate([half, swap(half)], axis=axis) for half, axis in zip(halves, (1, 1, 0))
        )
        grad_turns = gather_tokens(grid, grad_two_low)
        token_turns = gather_tokens(grid, token_block)
        out_turns, back_turns, saved = [], [], []
        for turn in range(2):
            outs, backs, kept = expert_turn(
                token_turns[turn], grad_turns[turn], (wg, wu, wd), capacity
            )
            out_turns.append(outs)
            back_turns.append(backs)
            saved.append(kept)
        back_sum = scatter_tokens(grid, back_turns)

    def over_turns(left, right):
        return sum(contract_rows(kept[left], kept[right]) for kept in saved)

    half = w_gate.shape[2]
    gate_w = over_turns(0, 3)
    up_w = over_turns(0, 4)
    down_w = over_turns(2, 1)
    if grid.side == 2:
        back_sum, gate_w, up_w, down_w = lax.optimization_barrier((back_sum, gate_w, up_w, down_w))

    grad_gates_wide = join_three(back_sum[SEQ:], SEQ).T
    grad_gate_sel = jnp.sum(jnp.where(route_hot, grad_gates_wide[:, None, :], 0.0), axis=2)
    grad_chosen = gates * (grad_gate_sel - jnp.sum(gates * grad_gate_sel, axis=1, keepdims=True))
    grad_logits = jnp.sum(jnp.where(route_hot, grad_chosen[:, :, None], 0.0), axis=1).astype(low)
    grad_router_t = contract_rows(grad_logits, ffn_in)
    grad_ffn_in = back_sum[:SEQ] + jnp.dot(
        grad_logits, router_t, preferred_element_type=jnp.float32
    )
    grad_gain_two = jnp.sum(grad_ffn_in * normed_two, axis=0)
    grad_one = grad_two + norm_back(grad_ffn_in * gain_two, normed_two, inverse_two)
    grad_attn = grad_one.astype(low)

    part_wo = contract_rows(grad_attn, mixed)
    grad_mixed = (
        jnp.dot(grad_attn, wo_full, preferred_element_type=jnp.float32)
        .astype(low)
        .reshape(SEQ, heads_here, HD)
    )
    masked = masked_scores()
    attn_probs = jnp.exp(masked - log_total)
    probs_again = attn_probs.astype(low)
    grad_probs = jnp.einsum(
        "qhd,khd->hqk", grad_mixed, values_b, preferred_element_type=jnp.float32
    )
    grad_values = jnp.einsum(
        "hqk,qhd->khd", probs_again, grad_mixed, preferred_element_type=jnp.float32
    )
    grad_value_lin = grad_values.astype(low).reshape(SEQ, heads_here * HD)
    part_wv = contract_rows(attn_in, grad_value_lin)
    grad_scores = (
        attn_probs * (grad_probs - jnp.sum(attn_probs * grad_probs, axis=-1, keepdims=True))
    ).astype(low)
    if grid.side == 2:
        near, grad_scores = lax.optimization_barrier((near, grad_scores))
        crossing = [
            grid.send((kept + part.astype(jnp.float32)).astype(low), grid.planes_of(turn))
            for kept, part, turn in zip(sums_kept[::2], near, (1, 0))
        ]
    grad_queries = (
        jnp.einsum("hqk,khd->qhd", grad_scores, keys_rot, preferred_element_type=jnp.float32)
        * scale
    )
    grad_keys = (
        jnp.einsum("hqk,qhd->khd", grad_scores, queries, preferred_element_type=jnp.float32) * scale
    )
    grad_query_scaled = rotate_back(grad_queries, cosine, sine_tab)
    grad_key_scaled = rotate_back(grad_keys, cosine, sine_tab)
    grad_gain_query = jnp.sum(grad_query_scaled * query_hat, axis=(0, 1))
    grad_gain_key = jnp.sum(grad_key_scaled * key_hat, axis=(0, 1))
    grad_query_lin = (
        norm_back(grad_query_scaled * gain_query, query_hat, query_inv)
        .astype(low)
        .reshape(SEQ, heads_here * HD)
    )
    grad_key_lin = (
        norm_back(grad_key_scaled * gain_key, key_hat, key_inv)
        .astype(low)
        .reshape(SEQ, heads_here * HD)
    )
    part_wq = contract_rows(attn_in, grad_query_lin)
    part_wk = contract_rows(attn_in, grad_key_lin)
    grad_attn_part = (
        contract_cols(grad_query_lin, wq_full)
        + contract_cols(grad_key_lin, wk_full)
        + contract_cols(grad_value_lin, wv_full)
    ).astype(low)
    grad_attn_in = grad_attn_part.astype(jnp.float32) + swap(grad_attn_part).astype(jnp.float32)
    grad_gain_one = jnp.sum(grad_attn_in * normed_one, axis=0)
    grad_input = grad_one + norm_back(grad_attn_in * gain_one, normed_one, inverse_one)

    head_part = HD // count
    heads_row = jnp.stack([grad_gain_query, grad_gain_key]).reshape(2, count, head_part)
    heads_row = jnp.pad(heads_row, ((0, 0), (0, 0), (0, own_rows - head_part)))
    parts = jnp.concatenate(
        [
            jnp.concatenate([grad_router_t, grad_gain_one[None], grad_gain_two[None]]).reshape(
                experts + 2, count, own_rows
            ),
            heads_row,
        ],
        axis=0,
    ).transpose(1, 0, 2)
    weight_parts = [part_wq, part_wk, part_wv, part_wo]
    if grid.side == 2:
        weight_parts = [part.astype(low) for part in weight_parts]
        parts = jnp.pad(parts, ((0, 0), (0, 4), (0, 0)))
        grad_wq, grad_wk, grad_wv, grad_wo, sums, *received = reduce_all(
            weight_parts, parts, [gate_w, up_w, down_w], count
        )
        crossing, sums = lax.optimization_barrier((crossing, sums))
        out_sum = both_cores(
            (crossing[0].astype(jnp.float32) + crossing[1].astype(jnp.float32)).astype(low)
        )
    else:
        shape = (PLANES, grid.side, grid.side)
        grad_wq, grad_wk, grad_wv, grad_wo = [
            scatter_rows(grid, part.reshape(shape + (own_rows, width)), axes, low)
            for part, axes in zip(weight_parts, ((1, 2, 0), (2, 1, 0)) * 2)
        ]
        sums = scatter_rows(
            grid, parts.reshape(shape + (experts + 4, own_rows)), (1, 2, 0), jnp.float32
        )
        sums = sums + swap(sums)
        received = [swap(part) for part in (gate_w[:, half:], up_w[:, half:], down_w[half:])]
        out_sum = scatter_tokens(grid, out_turns)
    output = (resid_one + out_sum).astype(low)
    grad_gate_w = (gate_w[:, :half] + received[0])[None]
    grad_up_w = (up_w[:, :half] + received[1])[None]
    grad_down_w = (down_w[:half] + received[2])[None]
    return (
        output,
        grad_input.astype(low),
        0.5 * sums[experts],
        grad_wq,
        grad_wk,
        grad_wv,
        sums[experts + 2, :head_part],
        sums[experts + 3, :head_part],
        grad_wo,
        0.5 * sums[experts + 1],
        0.5 * sums[:experts].T,
        grad_gate_w,
        grad_up_w,
        grad_down_w,
    )


def solution(mesh):
    return jax.shard_map(
        local,
        mesh=mesh,
        in_specs=(
            P("expert", None),
            P("expert"),
            P("expert", None),
            P("expert"),
            P("expert", "tensor"),
            P("expert", "tensor"),
            P("expert", "tensor"),
            P("expert"),
            P("expert"),
            P("expert", "tensor"),
            P("expert"),
            P("expert", None),
            P("expert", None, "tensor"),
            P("expert", None, "tensor"),
            P("expert", "tensor", None),
            P("expert", None),
        ),
        out_specs=(
            P("expert", None),
            P("expert", None),
            P("expert"),
            P("expert", "tensor"),
            P("expert", "tensor"),
            P("expert", "tensor"),
            P("expert"),
            P("expert"),
            P("expert", "tensor"),
            P("expert"),
            P("expert", None),
            P("expert", None, "tensor"),
            P("expert", None, "tensor"),
            P("expert", "tensor", None),
        ),
        check_vma=False,
    )
```
